32 devices in a mesh: gx: 2 (over core), gy: 4 (over z), gz: 4 (over y, x).
Axes of the slice: x: 2, y: 2, z: 4, core: 2. Of those that a mesh axis runs over, the one named last changes fastest.
Arguments:
- source: float32 [16, 64, 512], P('gx', 'gy', 'gz'), may hold values from -18 to 18
- pressure_old: float32 [16, 64, 512], P('gx', 'gy', 'gz'), may hold values from -6 to 6
- strain_prev: float32 [16, 64, 512], P('gx', 'gy', 'gz'), may hold values from -6 to 6
- motion_old: float32 [3, 16, 64, 512], P(None, 'gx', 'gy', 'gz'), may hold values from -6 to 6
- body_force: float32 [3, 16, 64, 512], P(None, 'gx', 'gy', 'gz'), may hold values from -6 to 6
- zone_ids: int32 [16, 64, 512], P('gx', 'gy', 'gz'), may hold values from 0 to 7
- drained: int32 [16, 64, 512], P('gx', 'gy', 'gz'), may hold values 0 or 1
- perm_table: float32 [8], replicated, may hold values from 0.1 to 3
- lame_table: float32 [8], replicated, may hold values from 0.5 to 4
- shear_table: float32 [8], replicated, may hold values from 0.3 to 2
Outputs:
- pressure: float32 [16, 64, 512], P('gx', 'gy', 'gz')
- motion: float32 [3, 16, 64, 512], P(None, 'gx', 'gy', 'gz')
- strain: float32 [16, 64, 512], P('gx', 'gy', 'gz')
The draws below stay inside these ranges and needn't reach their ends.
All inputs are finite; a program needn't handle non-finite values. No bound on the sum of `drained` on one device may be relied on, other than what follows from the above.
Results may differ from the reference program's by a relative error of at most 0.0001.
Values sent between devices are 32-bit elements; how exact they have to be, the bound alone decides.
No kernel may reach another device: no remote copies, remote signals or barrier semaphores. Data moves between devices by JAX's collectives and lax.ppermute only.
A program may use at most 64 MiB of HBM per device.

```python
import math
import jax
import jax.numpy as jnp

ITERS = 2
ZONES = 8
NX = 16
NY = 64
NZ = 512


def draw_source(key, part):
    rising = jnp.arange(NX, dtype=jnp.float32) / max(NX - 1, 1)
    base = jnp.clip(jax.random.normal(key, (NX, NY, NZ), jnp.float32), -6.0, 6.0)
    return base * (1.0 + 2.0 * rising)[:, None, None]


def place_ends(values, key, least, high):
    index_at = [jax.random.randint(jax.random.fold_in(key, axis), (), 0, length) for axis, length in enumerate(values.shape)]
    widest = values.shape.index(max(values.shape))
    neighbour = index_at[:widest] + [(index_at[widest] + 1) % values.shape[widest]] + index_at[widest + 1:]
    return values.at[tuple(index_at)].set(least).at[tuple(neighbour)].set(high)


def levels(rng, dims, pieces, low, high):
    factor_of, own = 1.0, jax.random.fold_in(rng, 6)
    for dim, blocks in pieces:
        draws = jnp.exp(jax.random.uniform(jax.random.fold_in(own, dim), (blocks,), jnp.float32, low / len(pieces), high / len(pieces)))
        factor_of = factor_of * jnp.repeat(draws, dims[dim] // blocks).reshape([-1 if axis == dim else 1 for axis in range(len(dims))])
    return factor_of


def scatter_about(own_key, extent, width, reach, shards=(), kind=jnp.bfloat16):
    level = levels(own_key, extent, shards, -0.22, 0.18) if shards else 1.0
    array = jax.random.normal(own_key, extent, jnp.float32) * width * level
    return jnp.minimum(jnp.maximum(array, -reach), reach).astype(kind)


def setup_inputs(seed: int = 0) -> dict:
    key_list = jax.random.split(jax.random.key(seed), 11)
    return {
        "source": draw_source(jax.random.fold_in(key_list[10], 71), 0),
        "pressure_old": scatter_about(key_list[1], (NX, NY, NZ), 1.0, 6.0, ((0, 2), (1, 4), (2, 4)), jnp.float32),
        "strain_prev": scatter_about(key_list[2], (NX, NY, NZ), 0.5, 6.0, ((0, 2), (1, 4), (2, 4)), jnp.float32),
        "motion_old": scatter_about(key_list[3], (3, NX, NY, NZ), 0.5, 6.0, ((1, 2), (2, 4), (3, 4)), jnp.float32),
        "body_force": scatter_about(key_list[4], (3, NX, NY, NZ), 1.0, 6.0, ((1, 2), (2, 4), (3, 4)), jnp.float32),
        "zone_ids": place_ends(jax.random.randint(key_list[5], (NX, NY, NZ), 0, ZONES), jax.random.fold_in(key_list[5], 1), 0, ZONES - 1).astype(jnp.int32),
        "drained": place_ends((jax.random.randint(key_list[6], (NX, NY, NZ), 0, 4) < 1).astype(jnp.int32), jax.random.fold_in(key_list[6], 1), 0, 1),
        "perm_table": jnp.clip(jnp.exp(jax.random.uniform(key_list[7], (ZONES,), jnp.float32, math.log(0.1), math.log(3.0))), 0.1, 3.0),
        "lame_table": jnp.clip(jnp.exp(jax.random.uniform(key_list[8], (ZONES,), jnp.float32, math.log(0.5), math.log(4.0))), 0.5, 4.0),
        "shear_table": jnp.clip(jnp.exp(jax.random.uniform(key_list[9], (ZONES,), jnp.float32, math.log(0.3), math.log(2.0))), 0.3, 2.0),
    }


storage = 0.2
biot_coef = 0.8
time_step = 1.0
leakage = 2.0
support = 1.0

def lookup(zone_ids, lookup_table):
    result = jnp.zeros(zone_ids.shape, jnp.float32)
    for zone_index in range(ZONES):
        result = result + jnp.where(zone_ids == zone_index, lookup_table[zone_index], 0.0)
    return result

def interior(padded):
    return padded[..., 1:-1, 1:-1, 1:-1]

def neighbours(padded):
    return [padded[..., 2:, 1:-1, 1:-1], padded[..., :-2, 1:-1, 1:-1], padded[..., 1:-1, 2:, 1:-1], padded[..., 1:-1, :-2, 1:-1], padded[..., 1:-1, 1:-1, 2:], padded[..., 1:-1, 1:-1, :-2]]

def harmonic(own_value, beside):
    return 2.0 * own_value * beside / (own_value + beside)

def central_div(motion_pad):
    return 0.5 * (motion_pad[0, 2:, 1:-1, 1:-1] - motion_pad[0, :-2, 1:-1, 1:-1] + (motion_pad[1, 1:-1, 2:, 1:-1] - motion_pad[1, 1:-1, :-2, 1:-1]) + (motion_pad[2, 1:-1, 1:-1, 2:] - motion_pad[2, 1:-1, 1:-1, :-2]))

def central_grad(press_pad):
    sided = neighbours(press_pad)
    return jnp.stack([0.5 * (sided[0] - sided[1]), 0.5 * (sided[2] - sided[3]), 0.5 * (sided[4] - sided[5])])

def conjugate(start_pad, rhs, diag, apply_padded, faces):
    iterate = interior(start_pad)
    residual = rhs - apply_padded(start_pad)
    precond = residual / diag
    image = apply_padded(faces(precond))
    gamma_now = jnp.sum(residual * precond)
    curvature = jnp.sum(precond * image)
    step_len = gamma_now / curvature
    direction = precond
    along = image
    for iteration in range(ITERS):
        iterate = iterate + step_len * direction
        residual = residual - step_len * along
        if iteration + 1 < ITERS:
            precond = residual / diag
            image = apply_padded(faces(precond))
            gamma_new = jnp.sum(residual * precond)
            curvature = jnp.sum(precond * image)
            momentum = gamma_new / gamma_now
            step_len = gamma_new / (curvature - momentum * gamma_new / step_len)
            direction = precond + momentum * direction
            along = image + momentum * along
            gamma_now = gamma_new
    return iterate

def pad_scalar(values):
    return jnp.pad(values, 1)

def pad_vector(values):
    return jnp.pad(values, ((0, 0), (1, 1), (1, 1), (1, 1)))

def reference(source, pressure_old, strain_prev, motion_old, body_force, zone_ids, drained, perm_table, lame_table, shear_table):
    permeability = lookup(zone_ids, perm_table)
    lame_first = lookup(zone_ids, lame_table)
    shear_mod = lookup(zone_ids, shear_table)
    fixed_term = biot_coef * biot_coef / (lame_first + 2.0 * shear_mod / 3.0)
    perm_pad = pad_scalar(permeability)
    heft_pad = pad_scalar(lame_first + shear_mod)
    shear_pad = pad_scalar(shear_mod)
    press_pad = pad_scalar(pressure_old)
    motion_pad = pad_vector(motion_old)
    transmit = [harmonic(permeability, beside) for beside in neighbours(perm_pad)]
    reaction = storage + fixed_term + leakage * drained.astype(jnp.float32)
    pdiag = reaction + time_step * sum(transmit)

    def apply_pressure(padded):
        center = interior(padded)
        flux = sum((factor * (center - beside) for factor, beside in zip(transmit, neighbours(padded))))
        return reaction * center + time_step * flux
    prhs = source + (storage + fixed_term) * pressure_old - biot_coef * (central_div(motion_pad) - strain_prev)
    pressure = conjugate(press_pad, prhs, pdiag, apply_pressure, pad_scalar)
    heft = interior(heft_pad)
    shear_faces = [harmonic(shear_mod, beside) for beside in neighbours(shear_pad)]
    heft_sides = neighbours(heft_pad)
    base_diag = support + sum(shear_faces) + heft
    ediag = jnp.stack([base_diag + heft_sides[1], base_diag + heft_sides[3], base_diag + heft_sides[5]])

    def apply_motion(padded):
        center = interior(padded)
        spread = sum((factor * (center - beside) for factor, beside in zip(shear_faces, neighbours(padded))))
        diverg = padded[0, 1:, :-1, :-1] - padded[0, :-1, :-1, :-1] + (padded[1, :-1, 1:, :-1] - padded[1, :-1, :-1, :-1]) + (padded[2, :-1, :-1, 1:] - padded[2, :-1, :-1, :-1])
        scaled = heft_pad[:-1, :-1, :-1] * diverg
        own_part = scaled[1:, 1:, 1:]
        push = jnp.stack([scaled[:-1, 1:, 1:] - own_part, scaled[1:, :-1, 1:] - own_part, scaled[1:, 1:, :-1] - own_part])
        return support * center + spread + push
    erhs = body_force - biot_coef * central_grad(pad_scalar(pressure))
    motion = conjugate(motion_pad, erhs, ediag, apply_motion, pad_vector)
    strain = central_div(pad_vector(motion))
    return (pressure, motion, strain)
```

```python
import jax
import jax.numpy as jnp
from jax import lax
from jax.experimental import pallas as pl
from jax.experimental.pallas import tpu as pltpu
from jax.sharding import PartitionSpec as P

ZONES = 8

storage = 0.2
biot_coef = 0.8
leakage = 2.0
support = 1.0

AXES = ("gx", "gy", "gz")
LANES = 128
TILE = 8

ZONE, PRESS, MOTION, SOURCE, DRAIN, BODY = 0, 1, 2, 5, 6, 7
WIDTHS = (5, 5, 5, 5, 5, 4, 4, 2, 2, 2)
NF = len(WIDTHS)
W = max(WIDTHS)
OFFSETS = tuple(sum(WIDTHS[:f]) for f in range(NF))
SLOT = 8
PAIRS = tuple((j, k) for j in range(3) for k in range(j, 3))
SUMS = 4 + 4 * len(PAIRS)


def up_to(value, multiple):
    return -(-value // multiple) * multiple


MSG_ROWS = up_to(sum(WIDTHS), TILE)


def lane_iota(shape):
    return lax.broadcasted_iota(jnp.int32, shape, len(shape) - 1)


def pack_rows(source, pressure, strain, motion, body, zones, drained, fields, upward, downward):
    nx, ny, _ = source.shape
    for x in range(nx):
        values = [
            zones[x].astype(jnp.float32) + 1.0,
            pressure[x],
            motion[0, x],
            motion[1, x],
            motion[2, x],
            source[x] + biot_coef * strain[x],
            drained[x].astype(jnp.float32),
            body[0, x],
            body[1, x],
            body[2, x],
        ]
        for f, value in enumerate(values):
            fields[f, x] = value
            width, offset = WIDTHS[f], OFFSETS[f]
            upward[x, offset : offset + width, :] = value[ny - width :, :]
            downward[x, offset : offset + width, :] = value[:width, :]
        rest = MSG_ROWS - sum(WIDTHS)
        if rest:
            empty = jnp.zeros((rest, source.shape[2]), jnp.float32)
            upward[x, MSG_ROWS - rest :, :] = empty
            downward[x, MSG_ROWS - rest :, :] = empty


def pack_lanes(last_y, fields, low, high, tall, rightward, leftward):
    _, nx, ny, nz = fields.shape
    rows = tall.shape[2]
    parts = LANES // (SLOT * nx)
    height = rows // parts
    at_y = lax.axis_index("gy")
    keep_low = jnp.where(at_y > 0, 1.0, 0.0)
    keep_high = jnp.where(at_y < last_y, 1.0, 0.0)
    for f in range(NF):
        width, offset = WIDTHS[f], OFFSETS[f]

        def fill(x, _, f=f, width=width, offset=offset):
            tall[f, x, :ny, :] = fields[f, x]
            tall[f, x, ny:, :] = jnp.zeros((rows - ny, nz), jnp.float32)
            tall[f, x, ny : ny + width, :] = high[x, offset : offset + width, :] * keep_high
            tall[f, x, rows - width :, :] = low[x, offset : offset + width, :] * keep_low
            return 0

        lax.fori_loop(0, nx, fill, 0)
        lane = lane_iota((height, LANES))
        to_right = jnp.zeros((height, LANES), jnp.float32)
        to_left = jnp.zeros((height, LANES), jnp.float32)
        for x in range(nx):
            for part in range(parts):
                piece = tall[f, x, part * height : (part + 1) * height, :]
                start = part * SLOT * nx + SLOT * x
                mine = (lane >= start) & (lane < start + width)
                ending = piece[:, nz - LANES :]
                to_right = jnp.where(
                    mine, pltpu.roll(ending, (start + width) % LANES, 1), to_right
                )
                to_left = jnp.where(mine, pltpu.roll(piece[:, :LANES], start, 1), to_left)
        rightward[f] = to_right
        leftward[f] = to_left


def harmonic(a, b):
    return 2.0 * a * b / jnp.maximum(a + b, 1e-30)


def main_kernel(
    peers,
    tables,
    tall,
    below,
    above,
    left,
    right,
    left_below,
    right_below,
    left_above,
    right_above,
    basis,
    partial,
    ext,
    perm,
    heft,
    shear,
    fixed,
    tx,
    ty,
    tz,
    mx,
    my,
    mz,
    react,
    pdiag,
    pinv,
    z0,
    p0,
    ediag,
    einv,
    push,
    zs,
    ps,
    acc,
):
    _, nx, rows, nz = tall.shape
    ny = basis.shape[2]
    lanes = ext.shape[3]
    parts = LANES // (SLOT * nx)
    height = rows // parts
    at = [lax.axis_index(a) for a in AXES]
    has_below = (at[0] > 0).astype(jnp.int32)
    has_above = (at[0] < peers[0] - 1).astype(jnp.int32)
    keep_left = jnp.where(at[2] > 0, 1.0, 0.0)
    keep_right = jnp.where(at[2] < peers[2] - 1, 1.0, 0.0)

    def first(halo):
        return W - halo * has_below

    def end(halo):
        return W + nx + halo * has_above

    def yp(v):
        return pltpu.roll(v, v.shape[0] - 1, 0)

    def ym(v):
        return pltpu.roll(v, 1, 0)

    def zp(v):
        return pltpu.roll(v, v.shape[1] - 1, 1)

    def zm(v):
        return pltpu.roll(v, 1, 1)

    def layers(start, stop, body):
        def step(l, carry):
            body(l)
            return carry

        lax.fori_loop(start, stop, step, 0)

    empty = jnp.zeros((rows, lanes), jnp.float32)
    for l in (W - 1, W + nx):
        for ref in (perm, heft, shear, z0, p0):
            ref[l] = empty
        for f in range(NF):
            ext[f, l] = empty
        for i in range(9):
            zs[i, l] = empty
            ps[i, l] = empty

    def assemble(l, x, source, low, high):
        lane = lane_iota((height, LANES))
        for f in range(NF):
            width = WIDTHS[f]
            ext[f, l, :, :nz] = source[f, x]
            for part in range(parts):
                start = part * SLOT * nx + SLOT * x
                after = pltpu.roll(high[f], LANES - start, 1) * keep_right
                before = pltpu.roll(low[f], LANES - width - start, 1) * keep_left
                side = jnp.where(
                    lane < width, after, jnp.where(lane >= LANES - width, before, 0.0)
                )
                ext[f, l, part * height : (part + 1) * height, nz:] = side
        zone = ext[ZONE, l]
        picked = [jnp.zeros((rows, lanes), jnp.float32)] * 3
        for index in range(ZONES):
            here = zone == float(index + 1)
            picked = [
                jnp.where(here, tables[t, index], value) for t, value in enumerate(picked)
            ]
        perm[l] = picked[0]
        heft[l] = picked[1] + picked[2]
        shear[l] = picked[2]
        fixed[l] = jnp.where(
            zone > 0.0,
            biot_coef * biot_coef / jnp.maximum(picked[1] + 2.0 * picked[2] / 3.0, 1e-30),
            0.0,
        )

    layers(
        first(W), W, lambda l: assemble(l, l + nx - W, below, left_below, right_below)
    )
    layers(W, W + nx, lambda l: assemble(l, l - W, tall, left, right))
    layers(
        W + nx, end(W), lambda l: assemble(l, l - W - nx, above, left_above, right_above)
    )

    def press_faces(l):
        own = perm[l]
        tx[l] = harmonic(own, perm[l + 1])
        ty[l] = harmonic(own, yp(own))
        tz[l] = harmonic(own, zp(own))

    layers(first(4) - 1, end(4), press_faces)

    def press_flux(read, l):
        own = read(l)
        along_y = ty[l] * (own - yp(own))
        along_z = tz[l] * (own - zp(own))
        return (
            tx[l] * (own - read(l + 1))
            + tx[l - 1] * (own - read(l - 1))
            + (along_y - ym(along_y))
            + (along_z - zm(along_z))
        )

    def central(read, l):
        a, b = read(1, l), read(2, l)
        return 0.5 * (
            read(0, l + 1) - read(0, l - 1) + (yp(a) - ym(a)) + (zp(b) - zm(b))
        )

    def old_press(l):
        return ext[PRESS, l]

    def old_motion(c, l):
        return ext[MOTION + c, l]

    def press_start(l):
        along_y, along_z = ty[l], tz[l]
        leak = leakage * ext[DRAIN, l]
        reaction = storage + fixed[l] + leak
        diag = (
            reaction
            + tx[l]
            + tx[l - 1]
            + (along_y + ym(along_y))
            + (along_z + zm(along_z))
        )
        inverse = jnp.where(ext[ZONE, l] > 0.0, 1.0 / diag, 0.0)
        residual = (
            ext[SOURCE, l]
            - biot_coef * central(old_motion, l)
            - leak * ext[PRESS, l]
            - press_flux(old_press, l)
        )
        react[l] = reaction
        pdiag[l] = diag
        pinv[l] = inverse
        z0[l] = residual * inverse

    layers(first(4), end(4), press_start)

    def press_next(l):
        own = z0[l]
        p0[l] = (react[l] * own + press_flux(lambda i: z0[i], l)) * pinv[l]

    layers(first(3), end(3), press_next)

    def motion_faces(l):
        own = shear[l]
        mx[l] = harmonic(own, shear[l + 1])
        my[l] = harmonic(own, yp(own))
        mz[l] = harmonic(own, zp(own))

    layers(first(2) - 1, end(2), motion_faces)

    def scaled_div(read, l):
        a, b, c = read(0, l), read(1, l), read(2, l)
        return heft[l] * ((read(0, l + 1) - a) + (yp(b) - b) + (zp(c) - c))

    def elastic(read, l, pushed, pushed_before):
        back = (pushed_before, ym(pushed), zm(pushed))
        out = []
        for c in range(3):
            own = read(c, l)
            along_y = my[l] * (own - yp(own))
            along_z = mz[l] * (own - zp(own))
            out.append(
                support * own
                + (
                    mx[l] * (own - read(c, l + 1))
                    + mx[l - 1] * (own - read(c, l - 1))
                    + (along_y - ym(along_y))
                    + (along_z - zm(along_z))
                )
                + (back[c] - pushed)
            )
        return out

    def gradient(read, l):
        own = read(l)
        return (
            0.5 * (read(l + 1) - read(l - 1)),
            0.5 * (yp(own) - ym(own)),
            0.5 * (zp(own) - zm(own)),
        )

    def motion_start(l):
        weight = heft[l]
        along_y, along_z = my[l], mz[l]
        base = (
            support
            + mx[l]
            + mx[l - 1]
            + (along_y + ym(along_y))
            + (along_z + zm(along_z))
            + weight
        )
        inside = ext[ZONE, l] > 0.0
        for c, beside in enumerate((heft[l - 1], ym(weight), zm(weight))):
            diag = base + beside
            ediag[c, l] = diag
            einv[c, l] = jnp.where(inside, 1.0 / diag, 0.0)
        pushed = scaled_div(old_motion, l)
        push[0, l] = pushed
        image = elastic(old_motion, l, pushed, push[0, l - 1])
        grads = [
            gradient(old_press, l),
            gradient(lambda i: z0[i], l),
            gradient(lambda i: p0[i], l),
        ]
        for c in range(3):
            inverse = einv[c, l]
            zs[c, l] = (ext[BODY + c, l] - biot_coef * grads[0][c] - image[c]) * inverse
            zs[3 + c, l] = -biot_coef * grads[1][c] * inverse
            zs[6 + c, l] = -biot_coef * grads[2][c] * inverse

    push[0, first(2) - 1] = scaled_div(old_motion, first(2) - 1)
    layers(first(2), end(2), motion_start)

    for j in range(3):

        def basis_field(c, l, j=j):
            return zs[3 * j + c, l]

        def motion_next(l, j=j, read=basis_field):
            pushed = scaled_div(read, l)
            push[j, l] = pushed
            image = elastic(read, l, pushed, push[j, l - 1])
            for c in range(3):
                ps[3 * j + c, l] = image[c] * einv[c, l]

        push[j, first(1) - 1] = scaled_div(basis_field, first(1) - 1)
        layers(first(1), end(1), motion_next)

    acc[...] = jnp.zeros(acc.shape, jnp.float32)

    def own_part(v):
        return v[:ny, :nz]

    def finish(l):
        x = l - W

        def add(index, value):
            total = value[:TILE]
            for start in range(TILE, ny, TILE):
                total = total + value[start : start + TILE]
            folded = total[:, :LANES]
            for start in range(LANES, nz, LANES):
                folded = folded + total[:, start : start + LANES]
            acc[index] = acc[index] + folded

        field, image = z0[l], p0[l]
        a, b = own_part(field), own_part(image)
        basis[0, x] = a
        basis[1, x] = b
        diag = own_part(pdiag[l])
        add(0, diag * a * a)
        add(1, diag * a * b)
        add(2, diag * b * b)
        dx = own_part(p0[l + 1]) - b
        dy = own_part(yp(image)) - b
        dz = own_part(zp(image)) - b
        add(
            3,
            own_part(react[l]) * b * b
            + own_part(tx[l]) * dx * dx
            + own_part(ty[l]) * dy * dy
            + own_part(tz[l]) * dz * dz,
        )
        basis[20, x] = own_part(central(old_motion, l))
        za, pa, steps, divs = [], [], [], []
        for j in range(3):
            za.append([own_part(zs[3 * j + c, l]) for c in range(3)])
            pa.append([own_part(ps[3 * j + c, l]) for c in range(3)])
            for c in range(3):
                basis[2 + 3 * j + c, x] = za[j][c]
                basis[11 + 3 * j + c, x] = pa[j][c]
            basis[21 + j, x] = own_part(central(lambda c, i, j=j: zs[3 * j + c, i], l))
            basis[24 + j, x] = own_part(central(lambda c, i, j=j: ps[3 * j + c, i], l))
            moved = []
            for c in range(3):
                own = ps[3 * j + c, l]
                moved.append(
                    (
                        own_part(ps[3 * j + c, l + 1]) - pa[j][c],
                        own_part(yp(own)) - pa[j][c],
                        own_part(zp(own)) - pa[j][c],
                    )
                )
            steps.append(moved)
            divs.append(moved[0][0] + moved[1][1] + moved[2][2])
        diags = [own_part(ediag[c, l]) for c in range(3)]
        faces = [own_part(ref[l]) for ref in (mx, my, mz)]
        weight = own_part(heft[l])
        for i, (j, k) in enumerate(PAIRS):
            add(4 + i, sum(diags[c] * za[j][c] * za[k][c] for c in range(3)))
            add(10 + i, sum(diags[c] * za[j][c] * pa[k][c] for c in range(3)))
            add(16 + i, sum(diags[c] * pa[j][c] * pa[k][c] for c in range(3)))
            energy = support * sum(pa[j][c] * pa[k][c] for c in range(3))
            for d in range(3):
                energy = energy + faces[d] * sum(
                    steps[j][c][d] * steps[k][c][d] for c in range(3)
                )
            add(22 + i, energy + weight * divs[j] * divs[k])

    layers(W, W + nx, finish)

    sums = jnp.concatenate(
        [jnp.sum(acc[i], axis=0, keepdims=True) for i in range(acc.shape[0])], axis=0
    )
    totals = jnp.sum(sums, axis=1, keepdims=True)
    row = lax.broadcasted_iota(jnp.int32, sums.shape, 0)
    spread = jnp.where(row == lane_iota(sums.shape), totals, 0.0)
    line = jnp.sum(spread, axis=0, keepdims=True)
    partial[...] = jnp.broadcast_to(line, partial.shape)


def step_sizes(gamma, delta, cross, energy):
    first = gamma / delta
    gamma_new = gamma - 2.0 * first * delta + first * first * cross
    curved = delta - 2.0 * first * cross + first * first * energy
    ratio = gamma_new / gamma
    second = gamma_new / (curved - ratio * gamma_new / first)
    return first + second * (1.0 + ratio), -first * second


def combine(sums, basis, pressure_old, motion_old, pressure, motion, strain):
    line = jnp.sum(sums[...], axis=0, keepdims=True)
    lane = lane_iota(line.shape)

    def value(index):
        return jnp.sum(jnp.where(lane == index, line, 0.0), axis=1, keepdims=True)

    c1, c2 = step_sizes(*[value(i) for i in range(4)])
    weights = (jnp.ones_like(c1), c1, c2)

    def form(start):
        total = 0.0
        for i, (j, k) in enumerate(PAIRS):
            scale = 1.0 if j == k else 2.0
            total = total + scale * weights[j] * weights[k] * value(start + i)
        return total

    d1, d2 = step_sizes(form(4), form(10), form(16), form(22))
    on_z = [d1 * w for w in weights]
    on_p = [d2 * w for w in weights]
    for x in range(pressure.shape[0]):
        pressure[x] = pressure_old[x] + c1 * basis[0, x] + c2 * basis[1, x]
        for c in range(3):
            total = motion_old[c, x]
            for j in range(3):
                total = total + on_z[j] * basis[2 + 3 * j + c, x]
                total = total + on_p[j] * basis[11 + 3 * j + c, x]
            motion[c, x] = total
        total = basis[20, x]
        for j in range(3):
            total = total + on_z[j] * basis[21 + j, x]
            total = total + on_p[j] * basis[24 + j, x]
        strain[x] = total


def f32(*shape):
    return jax.ShapeDtypeStruct(shape, jnp.float32)


def call(kernel, outs, *args, smem=(), scratch=(), limit=None):
    specs = [
        pl.BlockSpec(memory_space=pltpu.SMEM if i in smem else pltpu.VMEM)
        for i in range(len(args))
    ]
    return pl.pallas_call(
        kernel,
        out_shape=outs,
        in_specs=specs,
        scratch_shapes=scratch,
        compiler_params=pltpu.CompilerParams(vmem_limit_bytes=limit),
    )(*args)


def ring(value, axis, step):
    peers = lax.axis_size(axis)
    return lax.ppermute(value, axis, [(i, (i + step) % peers) for i in range(peers)])


def x_neighbours(value):
    peers = lax.axis_size("gx")
    above = ring(value, "gx", -1)
    below = above if peers == 2 else ring(value, "gx", 1)
    return below, above


def shards(
    source,
    pressure_old,
    strain_prev,
    motion_old,
    body_force,
    zone_ids,
    drained,
    perm_table,
    lame_table,
    shear_table,
):
    nx, ny, nz = source.shape
    peers = [lax.axis_size(a) for a in AXES]
    count = peers[0] * peers[1] * peers[2]
    rows = up_to(ny + 2 * W, 2 * TILE)
    parts = LANES // (SLOT * nx)
    height = rows // parts
    fields, upward, downward = call(
        pack_rows,
        [f32(NF, nx, ny, nz), f32(nx, MSG_ROWS, nz), f32(nx, MSG_ROWS, nz)],
        source,
        pressure_old,
        strain_prev,
        motion_old,
        body_force,
        zone_ids,
        drained,
    )
    low = ring(upward, "gy", 1)
    high = ring(downward, "gy", -1)

    def lanes_kernel(*refs):
        pack_lanes(peers[1] - 1, *refs)

    tall, rightward, leftward = call(
        lanes_kernel,
        [f32(NF, nx, rows, nz), f32(NF, height, LANES), f32(NF, height, LANES)],
        fields,
        low,
        high,
    )
    below, above = x_neighbours(tall)
    left = ring(rightward, "gz", 1)
    right = ring(leftward, "gz", -1)
    left_below, left_above = x_neighbours(left)
    right_below, right_above = x_neighbours(right)
    tables = jnp.stack([perm_table, lame_table, shear_table])

    depth, lanes = nx + 2 * W, nz + LANES

    def layer(*lead):
        return pltpu.VMEM((*lead, depth, rows, lanes), jnp.float32)

    def kernel(*refs):
        main_kernel(peers, *refs)

    basis, partial = call(
        kernel,
        [f32(27, nx, ny, nz), f32(count, LANES)],
        tables,
        tall,
        below,
        above,
        left,
        right,
        left_below,
        right_below,
        left_above,
        right_above,
        smem=(0,),
        scratch=[layer(NF)]
        + [layer() for _ in range(15)]
        + [layer(3), layer(3), layer(3), layer(9), layer(9)]
        + [pltpu.VMEM((up_to(SUMS, TILE), TILE, LANES), jnp.float32)],
        limit=50 * 2**20,
    )
    sums = lax.all_to_all(partial, AXES, 0, 0, tiled=True)
    return tuple(
        call(
            combine,
            [f32(nx, ny, nz), f32(3, nx, ny, nz), f32(nx, ny, nz)],
            sums,
            basis,
            pressure_old,
            motion_old,
        )
    )


def solution(mesh):
    placed = (
        P("gx", "gy", "gz"),
        P("gx", "gy", "gz"),
        P("gx", "gy", "gz"),
        P(None, "gx", "gy", "gz"),
        P(None, "gx", "gy", "gz"),
        P("gx", "gy", "gz"),
        P("gx", "gy", "gz"),
        P(),
        P(),
        P(),
    )
    return jax.shard_map(
        shards,
        mesh=mesh,
        in_specs=placed,
        out_specs=(P("gx", "gy", "gz"), P(None, "gx", "gy", "gz"), P("gx", "gy", "gz")),
        check_vma=False,
    )
```

```python
import jax
import jax.numpy as jnp
from jax import lax
from jax.experimental import pallas as pl
from jax.experimental.pallas import tpu as pltpu
from jax.sharding import PartitionSpec as P

ZONES = 8

storage = 0.2
biot_coef = 0.8
leakage = 2.0
support = 1.0

AXES = ("gx", "gy", "gz")
LANES = 128
TILE = 8
MIB = 2**20

ZONE, PRESS, MOTION, SOURCE, DRAIN, BODY = 0, 1, 2, 5, 6, 7
WIDTHS = (5, 5, 5, 5, 5, 4, 4, 2, 2, 2)
NF = len(WIDTHS)
WIDE = 5
W = max(WIDTHS)
OFFSETS = tuple(sum(WIDTHS[:f]) for f in range(NF))
PAIRS = tuple((j, k) for j in range(3) for k in range(j, 3))
SUMS = 4 + 4 * len(PAIRS)
BASIS = 27
SEG = 16
ENDS = 2 * SEG
UNROLL = 4
PACK_LIMIT = 62


def up_to(value, multiple):
    return -(-value // multiple) * multiple


MSG_ROWS = up_to(sum(WIDTHS), TILE)


def iota(shape, dim):
    return lax.broadcasted_iota(jnp.int32, shape, dim)


def pack_rows(*refs):
    sources, (fields, first, second), rest = refs[:7], refs[7:10], refs[10:]
    held, arrived = rest[:7], rest[7]
    copies = [
        pltpu.make_async_copy(source, copy, arrived.at[i])
        for i, (source, copy) in enumerate(zip(sources, held))
    ]
    for copy in copies:
        copy.start()
    for copy in copies:
        copy.wait()
    source, pressure, strain, motion, body, zones, drained = held
    nx, ny, nz = source.shape
    spare = MSG_ROWS - sum(WIDTHS)
    for x in range(nx):
        values = [
            zones[x].astype(jnp.float32) + 1.0,
            pressure[x],
            motion[0, x],
            motion[1, x],
            motion[2, x],
            source[x] + biot_coef * strain[x],
            drained[x].astype(jnp.float32),
            body[0, x],
            body[1, x],
            body[2, x],
        ]
        for f, value in enumerate(values):
            fields[f, x] = value
        if spare:
            empty = jnp.zeros((spare, nz), jnp.float32)
            first[x, MSG_ROWS - spare :, :] = empty
            second[x, MSG_ROWS - spare :, :] = empty

    def messages(upward, downward):
        for x in range(nx):
            for f in range(NF):
                width, offset = WIDTHS[f], OFFSETS[f]
                upward[x, offset : offset + width, :] = fields[f, x, ny - width :, :]
                downward[x, offset : offset + width, :] = fields[f, x, :width, :]

    even = lax.axis_index("gy") % 2 == 0
    pl.when(even)(lambda: messages(first, second))
    pl.when(jnp.logical_not(even))(lambda: messages(second, first))


class Rows:
    def __init__(self, first, second, peers):
        self.refs = first, second
        self.even = lax.axis_index("gy") % 2 == 0
        self.keep = keeps("gy", peers[1])

    def read(self, f, x):
        width, offset = WIDTHS[f], OFFSETS[f]
        a, b = [ref[x, offset : offset + width, :] for ref in self.refs]
        low, high = jnp.where(self.even, b, a), jnp.where(self.even, a, b)
        return low * self.keep[0], high * self.keep[1]


def keeps(axis, peers):
    at = lax.axis_index(axis)
    return jnp.where(at > 0, 1.0, 0.0), jnp.where(at < peers - 1, 1.0, 0.0)


def pack_ends(peers, fields, first, second, ends, rightward, leftward, stage):
    _, nx, ny, nz = fields.shape
    tall = ny + 2 * TILE
    pack = LANES // tall
    rows = Rows(first, second, peers)
    gap = jnp.zeros((TILE, nz), jnp.float32)
    inner = SEG - W
    spare = MSG_ROWS - sum(WIDTHS)
    for g in range(nx // pack):
        if spare:
            empty = jnp.zeros((spare, LANES), jnp.float32)
            rightward[g, MSG_ROWS - spare :, :] = empty
            leftward[g, MSG_ROWS - spare :, :] = empty
        for f in range(NF):
            width, offset = WIDTHS[f], OFFSETS[f]
            slot = g * NF + f
            for i in range(pack):
                x = g * pack + i
                top = i * tall
                stage[slot, top : top + TILE, :] = gap
                stage[slot, top + TILE + ny : top + tall, :] = gap
                stage[slot, top + TILE : top + TILE + ny, :] = fields[f, x]
                low, high = rows.read(f, x)
                stage[slot, top + TILE - width : top + TILE, :] = low
                stage[slot, top + TILE + ny : top + TILE + ny + width, :] = high
            begin = stage[slot, :, :LANES].T
            finish = begin if nz == LANES else stage[slot, :, nz - LANES :].T
            rightward[g, offset : offset + width, :] = finish[LANES - width :]
            leftward[g, offset : offset + width, :] = begin[:width]
            ends[f, g, :TILE, :] = jnp.zeros((TILE, LANES), jnp.float32)
            ends[f, g, ENDS - TILE :, :] = jnp.zeros((TILE, LANES), jnp.float32)
            ends[f, g, W:SEG, :] = begin[:inner]
            ends[f, g, SEG : ENDS - W, :] = finish[LANES - inner :]


def harmonic(a, b):
    return 2.0 * a * b / jnp.maximum(a + b, 1e-30)


def lookup(zone, tables):
    picked = [jnp.zeros(zone.shape, jnp.float32) for _ in tables]
    for index in range(ZONES):
        here = zone == float(index + 1)
        picked = [
            jnp.where(here, table[row, index], value)
            for (table, row), value in zip(tables, picked)
        ]
    return picked


def fixed_term(zone, lame, shear):
    scale = jnp.maximum(lame + 2.0 * shear / 3.0, 1e-30)
    return jnp.where(zone > 0.0, biot_coef * biot_coef / scale, 0.0)


KEPT = ("motion", "z0", "p0", "zs", "ps")
ARRAYS = (
    ("zone", 0),
    ("press", 0),
    ("motion", 3),
    ("load", 0),
    ("drain", 0),
    ("body", 3),
    ("perm", 0),
    ("heft", 0),
    ("shear", 0),
    ("fixed", 0),
    ("tx", 0),
    ("ty", 0),
    ("tz", 0),
    ("mx", 0),
    ("my", 0),
    ("mz", 0),
    ("react", 0),
    ("pdiag", 0),
    ("pinv", 0),
    ("z0", 0),
    ("p0", 0),
    ("ediag", 3),
    ("einv", 3),
    ("push", 3),
    ("zs", 9),
    ("ps", 9),
)


class Domain:
    def __init__(self, arrays):
        self.__dict__.update(arrays)

    def press_faces(self, l):
        own = self.perm[l]
        self.tx[l] = harmonic(own, self.nxt(self.perm, l))
        self.ty[l] = harmonic(own, self.yp(own))
        self.tz[l] = harmonic(own, self.zp(own))

    def motion_faces(self, l):
        own = self.shear[l]
        self.mx[l] = harmonic(own, self.nxt(self.shear, l))
        self.my[l] = harmonic(own, self.yp(own))
        self.mz[l] = harmonic(own, self.zp(own))

    def steps(self, ref, l):
        own = ref[l]
        return self.nxt(ref, l) - own, self.yp(own) - own, self.zp(own) - own

    def back_y(self, value):
        return self.ym(value) - value

    def back_z(self, value):
        return self.zm(value) - value

    def press_flux(self, ref, l, along_y=True):
        dx, dy, dz = self.steps(ref, l)
        total = self.back_x(self.tx, dx, ref, l) + self.back_z(self.tz[l] * dz)
        return total + self.back_y(self.ty[l] * dy) if along_y else total

    def y_terms(self, l):
        face = self.ty[l]
        own, middle = self.press[l], self.motion[1, l]
        return (
            face + self.ym(face),
            self.back_y(face * (self.yp(own) - own))
            + (0.5 * biot_coef) * (self.yp(middle) - self.ym(middle)),
        )

    def press_start(self, l):
        face_sum, y_part = self.y_terms(l)
        face = self.tz[l]
        leak = leakage * self.drain[l]
        reaction = storage + self.fixed[l] + leak
        diag = (
            reaction
            + self.tx[l]
            + self.prv(self.tx, l)
            + face_sum
            + (face + self.zm(face))
        )
        inverse = jnp.where(self.zone[l] > 0.0, 1.0 / diag, 0.0)
        along_x, along_z = self.motion.at[0], self.motion[2, l]
        change = (self.nxt(along_x, l) - self.prv(along_x, l)) + (
            self.zp(along_z) - self.zm(along_z)
        )
        residual = (
            self.load[l]
            - (0.5 * biot_coef) * change
            - leak * self.press[l]
            - self.press_flux(self.press, l, False)
            - y_part
        )
        self.react[l] = reaction
        self.pdiag[l] = diag
        self.pinv[l] = inverse
        self.z0[l] = residual * inverse

    def press_next(self, l):
        image = self.react[l] * self.z0[l] + self.press_flux(self.z0, l)
        self.p0[l] = image * self.pinv[l]

    @staticmethod
    def parts(ref, j):
        return [ref.at[3 * j + c] for c in range(3)]

    def elastic(self, refs, l, j):
        steps = [self.steps(ref, l) for ref in refs]
        pushed = self.heft[l] * (steps[0][0] + steps[1][1] + steps[2][2])
        self.keep_push(j, l, pushed)
        out = []
        for c in range(3):
            dx, dy, dz = steps[c]
            step_y, step_z = self.my[l] * dy, self.mz[l] * dz
            if c == 1:
                step_y = step_y + pushed
            if c == 2:
                step_z = step_z + pushed
            push = (j, pushed) if c == 0 else None
            out.append(
                support * refs[c][l]
                + self.back_x(self.mx, dx, refs[c], l, push)
                + self.back_y(step_y)
                + self.back_z(step_z)
            )
        return out

    def gradient(self, ref, l):
        own = ref[l]
        return (
            0.5 * (self.nxt(ref, l) - self.prv(ref, l)),
            0.5 * (self.yp(own) - self.ym(own)),
            0.5 * (self.zp(own) - self.zm(own)),
        )

    def motion_start(self, l):
        weight = self.heft[l]
        along_y, along_z = self.my[l], self.mz[l]
        base = (
            support
            + self.mx[l]
            + self.prv(self.mx, l)
            + (along_y + self.ym(along_y))
            + (along_z + self.zm(along_z))
            + weight
        )
        inside = self.zone[l] > 0.0
        beside = (self.prv(self.heft, l), self.ym(weight), self.zm(weight))
        image = self.elastic(self.parts(self.motion, 0), l, 0)
        grads = [self.gradient(ref, l) for ref in (self.press, self.z0, self.p0)]
        for c in range(3):
            diag = base + beside[c]
            inverse = jnp.where(inside, 1.0 / diag, 0.0)
            self.ediag[c, l] = diag
            self.einv[c, l] = inverse
            start = self.body[c, l] - biot_coef * grads[0][c] - image[c]
            self.zs[c, l] = start * inverse
            scale = -biot_coef * inverse
            self.zs[3 + c, l] = grads[1][c] * scale
            self.zs[6 + c, l] = grads[2][c] * scale

    def motion_next(self, l, j):
        image = self.elastic(self.parts(self.zs, j), l, j)
        for c in range(3):
            self.ps[3 * j + c, l] = image[c] * self.einv[c, l]

    def stages(self):
        self.run(4, self.press_faces, 1)
        self.run(4, self.press_start)
        self.run(3, self.press_next)
        self.run(2, self.motion_faces, 1)
        self.lead(2, lambda l: self.first_push(self.parts(self.motion, 0), l, 0))
        self.run(2, self.motion_start)
        for j in range(3):
            self.lead(1, lambda l: self.first_push(self.parts(self.zs, j), l, j))
            self.run(1, lambda l: self.motion_next(l, j))

    def finish(self, l, acc, mask):
        own = self.own

        def add(index, value):
            acc[index] = acc[index] + self.fold(value, mask)

        def total(pairs):
            out = None
            for a, b in pairs:
                out = a * b if out is None else out + a * b
            return out

        a, b = own(self.z0[l]), own(self.p0[l])
        diag = own(self.pdiag[l])
        scaled = diag * b
        add(0, diag * a * a)
        add(1, scaled * a)
        add(2, scaled * b)
        energy = own(self.react[l]) * b * b
        for face, step in zip((self.tx, self.ty, self.tz), self.steps(self.p0, l)):
            step = own(step)
            energy = energy + own(face[l]) * step * step
        add(3, energy)
        diags = [own(self.ediag[c, l]) for c in range(3)]
        faces = [own(ref[l]) for ref in (self.mx, self.my, self.mz)]
        weight = own(self.heft[l])
        za, pa, dz, dp, steps, heavy = [], [], [], [], [], []
        for j in range(3):
            zj, pj = self.parts(self.zs, j), self.parts(self.ps, j)
            za.append([own(ref[l]) for ref in zj])
            pa.append([own(ref[l]) for ref in pj])
            dz.append([d * v for d, v in zip(diags, za[j])])
            dp.append([d * v for d, v in zip(diags, pa[j])])
            moved = [[own(v) for v in self.steps(ref, l)] for ref in pj]
            div = moved[0][0] + moved[1][1] + moved[2][2]
            flat = [(faces[d], moved[c][d]) for c in range(3) for d in range(3)]
            steps.append([v for _, v in flat] + [div] + pa[j])
            heavy.append([f * v for f, v in flat] + [weight * div])
            heavy[j] = heavy[j] + [support * v for v in pa[j]]
        for i, (j, k) in enumerate(PAIRS):
            add(4 + i, total(zip(dz[j], za[k])))
            add(10 + i, total(zip(dp[k], za[j])))
            add(16 + i, total(zip(dp[j], pa[k])))
            add(22 + i, total(zip(heavy[j], steps[k])))

    @staticmethod
    def loop(start, count, body, unroll=UNROLL):
        if not isinstance(count, int):
            unroll = 1
        chunks = count // unroll

        def step(i, carry):
            for u in range(unroll):
                body(start + i * unroll + u)
            return carry

        if isinstance(chunks, int) and chunks == 1:
            step(0, 0)
        else:
            lax.fori_loop(0, chunks, step, 0)
        if isinstance(count, int):
            for u in range(chunks * unroll, count):
                body(start + u)


class Brick(Domain):
    def nxt(self, ref, l):
        return ref[l + 1]

    def prv(self, ref, l):
        return ref[l - 1]

    def yp(self, v):
        return pltpu.roll(v, v.shape[0] - 1, 0)

    def ym(self, v):
        return pltpu.roll(v, 1, 0)

    def zp(self, v):
        return pltpu.roll(v, v.shape[1] - 1, 1)

    def zm(self, v):
        return pltpu.roll(v, 1, 1)

    def back_x(self, faces, step, ref, l, push=None):
        out = faces[l - 1] * (ref[l] - ref[l - 1]) - faces[l] * step
        if push:
            out = out + (self.push[push[0], l - 1] - push[1])
        return out

    def keep_push(self, j, l, value):
        self.push[j, l] = value

    def first_push(self, refs, l, j):
        dx, dy, dz = [self.steps(ref, l)[i] for i, ref in enumerate(refs)]
        self.push[j, l] = self.heft[l] * (dx + dy + dz)

    def own(self, v):
        return v[: self.ny]

    def fold(self, value, mask):
        total = value[:TILE]
        for start in range(TILE, value.shape[0], TILE):
            total = total + value[start : start + TILE]
        total = jnp.where(mask, total, 0.0)
        folded = total[:, :LANES]
        for start in range(LANES, value.shape[1], LANES):
            folded = folded + total[:, start : start + LANES]
        return folded

    def first(self, halo):
        return W - halo * self.has_below

    def reach(self, halo):
        if self.pair:
            return halo
        return halo * (self.has_below + self.has_above)

    def run(self, halo, body, before=0):
        self.loop(self.first(halo) - before, self.nx + self.reach(halo) + before, body)

    def lead(self, halo, body):
        body(self.first(halo) - 1)

    def narrow(self, v):
        ny = self.ny
        upper, lower = v[ny : ny + TILE], v[ny + TILE :]
        both = jnp.where(iota(upper.shape, 0) < TILE // 2, upper, lower)
        return jnp.concatenate([v[:ny], both], axis=0)

    def press_faces(self, l):
        own = self.perm[l]
        self.tx[l] = harmonic(own, self.nxt(self.perm, l))
        tall = self.perm_tall[l]
        face = harmonic(tall, self.yp(tall))
        self.ty_tall[l] = face
        self.ty[l] = self.narrow(face)
        self.tz[l] = harmonic(own, self.zp(own))

    def y_terms(self, l):
        face = self.ty_tall[l]
        own, middle = self.tall[PRESS, l], self.tall[MOTION + 1, l]
        return (
            self.narrow(face + self.ym(face)),
            self.narrow(
                self.back_y(face * (self.yp(own) - own))
                + (0.5 * biot_coef) * (self.yp(middle) - self.ym(middle))
            ),
        )

    def assemble(self, l, x, fields, beside, tables):
        ny = self.ny
        rows = ny + 2 * TILE
        gap = jnp.zeros((2 * TILE, fields.shape[3]), jnp.float32)
        narrow_rows = ny + TILE
        slim = (self.load, self.drain) + tuple(self.body.at[c] for c in range(3))
        for f in range(NF):
            width = WIDTHS[f]
            below, above = beside.read(f, x)
            if f < WIDE:
                self.tall[f, l, :ny, :] = fields[f, x]
                self.tall[f, l, ny:, :] = gap
                self.tall[f, l, ny : ny + width, :] = above
                self.tall[f, l, rows - width :, :] = below
            else:
                ref = slim[f - WIDE]
                ref[l, :ny, :] = fields[f, x]
                ref[l, ny:, :] = gap[:TILE]
                ref[l, ny : ny + width, :] = above
                ref[l, narrow_rows - width :, :] = below
        tall_zone = self.tall[ZONE, l]
        (perm,) = lookup(tall_zone, tables[:1])
        self.perm_tall[l] = perm
        self.perm[l] = self.narrow(perm)
        zone = self.narrow(tall_zone)
        self.zone[l] = zone
        lame, shear = lookup(zone, tables[1:])
        self.heft[l] = lame + shear
        self.shear[l] = shear
        self.fixed[l] = fixed_term(zone, lame, shear)
        self.press[l] = self.narrow(self.tall[PRESS, l])
        for c in range(3):
            self.motion[c, l] = self.narrow(self.tall[MOTION + c, l])


def brick_kernel(peers, *refs):
    table, fields, below, above = refs[:4]
    rows = [Rows(*refs[i : i + 2], peers) for i in (4, 6, 8)]
    outs, acc, scratch = refs[10 : 10 + len(KEPT)], refs[10 + len(KEPT)], refs[11 + len(KEPT) :]
    inner = len(ARRAYS) - len(KEPT)
    names = [name for name, _ in ARRAYS if name not in KEPT]
    domain = Brick(dict(zip(names, scratch[:inner])))
    domain.__dict__.update(zip(KEPT, outs))
    domain.tall, domain.perm_tall, domain.ty_tall = scratch[inner:]
    tables = [(table, i) for i in range(3)]
    _, nx, ny, nz = fields.shape
    domain.nx, domain.ny = nx, ny
    at = lax.axis_index("gx")
    domain.has_below = (at > 0).astype(jnp.int32)
    domain.has_above = (at < peers[0] - 1).astype(jnp.int32)
    domain.pair = peers[0] == 2

    empty = jnp.zeros((ny + TILE, nz), jnp.float32)
    for l in (W - 1, W + nx):
        for name in ("perm", "heft", "shear", "press", "z0", "p0"):
            getattr(domain, name)[l] = empty
        for c in range(3):
            domain.motion[c, l] = empty
        for i in range(9):
            domain.zs[i, l] = empty
            domain.ps[i, l] = empty
        domain.perm_tall[l] = jnp.zeros((ny + 2 * TILE, nz), jnp.float32)

    def block(start, count, shift, *source):
        domain.loop(
            start, count, lambda l: domain.assemble(l, l + shift, *source, tables)
        )

    block(W, nx, -W, fields, rows[0])
    if domain.pair:
        start = jnp.where(at > 0, 0, W + nx)
        shift = jnp.where(at > 0, nx - W, -W - nx)
        block(start, W, shift, below, rows[1])
    else:
        block(0, W * domain.has_below, nx - W, below, rows[1])
        block(W + nx, W * domain.has_above, -W - nx, above, rows[2])
    domain.stages()
    acc[...] = jnp.zeros(acc.shape, jnp.float32)
    column = iota((TILE, nz), 1)
    mask = (column >= W) & (column < nz - W)
    domain.loop(W, nx, lambda l: domain.finish(l, acc, mask))


class Ends(Domain):
    def roll(self, v, shift):
        return pltpu.roll(v, shift % LANES, v.ndim - 1)

    def nxt(self, ref, l):
        moved = self.roll(ref[pl.ds(l.start, l.size + 1)], -self.row)
        lane = iota(moved[1:].shape, 2)
        return jnp.where(lane < LANES - self.row, moved[:-1], moved[1:])

    def before(self, v):
        moved = self.roll(v, self.row)
        back = jnp.concatenate([jnp.zeros_like(moved[:1]), moved[:-1]], axis=0)
        return jnp.where(iota(moved.shape, 2) >= self.row, moved, back)

    def prv(self, ref, l):
        return self.before(ref[l])

    def back_x(self, faces, step, ref, l, push=None):
        value = faces[l] * step
        if push:
            value = value + push[1]
        return self.before(value) - value

    def keep_push(self, j, l, value):
        pass

    def yp(self, v):
        return self.roll(v, -1)

    def ym(self, v):
        return self.roll(v, 1)

    def zp(self, v):
        return pltpu.roll(v, ENDS - 1, 1)

    def zm(self, v):
        return pltpu.roll(v, 1, 1)

    def own(self, v):
        return v

    def fold(self, value, mask):
        total = None
        for g in range(value.shape[0]):
            part = jnp.where(mask, value[g], 0.0)
            for start in range(0, value.shape[1], TILE):
                piece = part[start : start + TILE]
                total = piece if total is None else total + piece
        return total

    def run(self, halo, body, before=0):
        body(pl.ds(0, self.groups))

    def lead(self, halo, body):
        pass

    def assemble(self, l, g, keep, ends, left, right, keep_left, keep_right):
        for f in range(NF):
            width, offset = WIDTHS[f], OFFSETS[f]
            self.raw[f, l] = ends[f, g] * keep
            self.raw[f, l, W - width : W, :] = left[g, offset : offset + width, :] * (
                keep_left * keep
            )
            self.raw[f, l, ENDS - W : ENDS - W + width, :] = right[
                g, offset : offset + width, :
            ] * (keep_right * keep)

    def materials(self, tables):
        for g in range(self.groups):
            zone = self.raw[ZONE, g]
            perm, lame, shear = lookup(zone, tables)
            self.perm[g] = perm
            self.heft[g] = lame + shear
            self.shear[g] = shear
            self.fixed[g] = fixed_term(zone, lame, shear)


def own_groups(count, peers):
    return count * lax.axis_index("gx") if peers[0] == 2 else count


def ends_kernel(peers, tall, *refs):
    table, ends, below, above, left, right = refs[:6]
    left_below, right_below, left_above, right_above, added = refs[6:11]
    raw, z0, p0, zs, ps, partial = refs[11:17]
    acc, scratch = refs[17], refs[18:]
    names = [name for name, _ in ARRAYS[6:] if name not in KEPT]
    domain = Ends(dict(zip(names, scratch)))
    domain.raw, domain.z0, domain.p0, domain.zs, domain.ps = raw, z0, p0, zs, ps
    domain.zone, domain.press = raw.at[ZONE], raw.at[PRESS]
    domain.motion = raw.at[MOTION : MOTION + 3]
    domain.load, domain.drain = raw.at[SOURCE], raw.at[DRAIN]
    domain.body = raw.at[BODY : BODY + 3]
    domain.row = tall
    count = ends.shape[1]
    domain.groups = groups = raw.shape[1] - 1
    at = lax.axis_index("gx")
    keep = keeps("gz", peers[2])
    empty = jnp.zeros((ENDS, LANES), jnp.float32)
    for ref in (raw, zs, ps):
        for i in range(ref.shape[0]):
            ref[i, groups] = empty
    for ref in (domain.perm, domain.shear, z0, p0):
        ref[groups] = empty
    mine = own_groups(count, peers)
    if peers[0] == 2:
        blocks = [
            (mine, 1.0, ends, left, right),
            (count * (1 - at), 1.0, below, left_below, right_below),
        ]
    else:
        keep_below, keep_above = keeps("gx", peers[0])
        blocks = [
            (0, keep_below, below, left_below, right_below),
            (mine, 1.0, ends, left, right),
            (mine + count, keep_above, above, left_above, right_above),
        ]
    for start, keep_block, *source in blocks:
        for g in range(count):
            domain.assemble(start + g, g, keep_block, *source, *keep)
    domain.materials([(table, i) for i in range(3)])
    domain.stages()
    acc[...] = added[...]
    shape = (ENDS, LANES)
    column, row = iota(shape, 0), iota(shape, 1) % tall
    at_end = ((column >= W) & (column < 2 * W)) | (
        (column >= ENDS - 2 * W) & (column < ENDS - W)
    )
    mask = at_end & (row >= TILE) & (row < tall - TILE)
    domain.finish(pl.ds(mine, count), acc, mask)

    sums = jnp.concatenate(
        [jnp.sum(acc[i], axis=0, keepdims=True) for i in range(acc.shape[0])], axis=0
    )
    totals = jnp.sum(sums, axis=1, keepdims=True)
    spread = jnp.where(iota(sums.shape, 0) == iota(sums.shape, 1), totals, 0.0)
    line = jnp.sum(spread, axis=0, keepdims=True)
    partial[...] = jnp.broadcast_to(line, partial.shape)


def step_sizes(gamma, delta, cross, energy):
    first = gamma / delta
    gamma_new = gamma - 2.0 * first * delta + first * first * cross
    curved = delta - 2.0 * first * cross + first * first * energy
    ratio = gamma_new / gamma
    second = gamma_new / (curved - ratio * gamma_new / first)
    return first + second * (1.0 + ratio), -first * second


def combine(peers, tall, *refs):
    sums, (old, z0, p0, zs, ps), fields = refs[0], refs[1:6], refs[6]
    raw, ends_z0, ends_p0, ends_zs, ends_ps = refs[7:12]
    pressure, motion, strain, moved, ends_moved, turned = refs[12:]
    line = jnp.sum(sums[...], axis=0, keepdims=True)
    lane = iota(line.shape, 1)

    def value(index):
        return jnp.sum(jnp.where(lane == index, line, 0.0), axis=1, keepdims=True)

    c1, c2 = step_sizes(*[value(i) for i in range(4)])
    weights = (jnp.ones_like(c1), c1, c2)

    def form(start):
        total = 0.0
        for i, (j, k) in enumerate(PAIRS):
            scale = 1.0 if j == k else 2.0
            total = total + scale * weights[j] * weights[k] * value(start + i)
        return total

    d1, d2 = step_sizes(form(4), form(10), form(16), form(22))
    on_z = [d1 * w for w in weights]
    on_p = [d2 * w for w in weights]

    def new_motion(start, z_part, p_part, c, i):
        total = start
        for j in range(3):
            total = total + on_z[j] * z_part[3 * j + c, i]
            total = total + on_p[j] * p_part[3 * j + c, i]
        return total

    nx, ny, nz = pressure.shape
    pack = LANES // tall
    ends = Ends(dict(row=tall))
    groups = raw.shape[1] - 1
    count = groups // (2 if peers[0] == 2 else 3)
    mine = own_groups(count, peers)
    every = pl.ds(0, groups)
    for c in range(3):
        for g in range(groups):
            ends_moved[c, g] = new_motion(raw[MOTION + c, g], ends_zs, ends_ps, c, g)
        ends_moved[c, groups] = jnp.zeros((ENDS, LANES), jnp.float32)
    along_y, along_z = ends_moved[1, every], ends_moved[2, every]
    first = ends_moved.at[0]
    ends_moved[3, every] = 0.5 * (
        (ends.nxt(first, every) - ends.prv(first, every))
        + (ends.yp(along_y) - ends.ym(along_y))
        + (ends.zp(along_z) - ends.zm(along_z))
    )
    for c in range(3):
        around = 1 if c == 0 else 0
        for l in range(W - around, W + nx + around):
            moved[c, l] = new_motion(old[c, l], zs, ps, c, l)
    brick = Brick({})
    outs = [pressure] + [motion.at[c] for c in range(3)] + [strain]
    for g in range(count):
        at = mine + g
        edges = [raw[PRESS, at] + c1 * ends_z0[at] + c2 * ends_p0[at]]
        edges = edges + [ends_moved[c, at] for c in range(4)]
        flipped = []
        for o, edge in enumerate(edges):
            slot = g * len(outs) + o
            turned[slot, :W, :] = edge[W : 2 * W]
            turned[slot, LANES - W :, :] = edge[ENDS - 2 * W : ENDS - W]
            flipped.append(turned[slot].T)
        for i in range(pack):
            x = g * pack + i
            l = W + x
            top = i * tall + TILE
            column = iota((ny, LANES), 1)
            u = [moved[c, l] for c in range(3)]
            change = (
                (moved[0, l + 1] - moved[0, l - 1])
                + (brick.yp(u[1]) - brick.ym(u[1]))
                + (brick.zp(u[2]) - brick.zm(u[2]))
            )
            results = [fields[PRESS, x] + c1 * z0[l, :ny, :] + c2 * p0[l, :ny, :]]
            results = results + [v[:ny] for v in u] + [0.5 * change[:ny]]
            for out, result, edge in zip(outs, results, flipped):
                edge = edge[top : top + ny]
                if nz == LANES:
                    inner = (column >= W) & (column < LANES - W)
                    out[x] = jnp.where(inner, result, edge)
                else:
                    out[x] = result
                    out[x, :, :LANES] = jnp.where(column >= W, result[:, :LANES], edge)
                    out[x, :, nz - LANES :] = jnp.where(
                        column < LANES - W, result[:, nz - LANES :], edge
                    )


def f32(*shape):
    return jax.ShapeDtypeStruct(shape, jnp.float32)


def vmem(*shape):
    return pltpu.VMEM(shape, jnp.float32)


def call(kernel, outs, *args, smem=0, space=pltpu.VMEM, scratch=(), limit=8, cost=None):
    specs = [
        pl.BlockSpec(memory_space=pltpu.SMEM if i < smem else space)
        for i in range(len(args))
    ]
    return pl.pallas_call(
        kernel,
        out_shape=outs,
        in_specs=specs,
        scratch_shapes=scratch,
        cost_estimate=cost,
        compiler_params=pltpu.CompilerParams(vmem_limit_bytes=limit * MIB),
    )(*args)


def ring(value, axis, step):
    peers = lax.axis_size(axis)
    return lax.ppermute(value, axis, [(i, (i + step) % peers) for i in range(peers)])


def pairs(value, axis, start):
    peers = lax.axis_size(axis)
    swaps = [(i, i) for i in range(start)]
    for i in range(start, peers - 1, 2):
        swaps += [(i, i + 1), (i + 1, i)]
    swaps += [(i, i) for i in range(len(swaps), peers)]
    return lax.ppermute(value, axis, swaps)


def x_neighbours(value):
    peers = lax.axis_size("gx")
    above = ring(value, "gx", -1)
    below = above if peers == 2 else ring(value, "gx", 1)
    return below, above


def shards(
    source,
    pressure_old,
    strain_prev,
    motion_old,
    body_force,
    zone_ids,
    drained,
    perm_table,
    lame_table,
    shear_table,
):
    nx, ny, nz = source.shape
    peers = [lax.axis_size(a) for a in AXES]
    total = peers[0] * peers[1] * peers[2]
    table = jnp.stack([perm_table, lame_table, shear_table])
    tall = ny + 2 * TILE
    groups = nx * tall // LANES

    def with_peers(kernel, *more):
        return lambda *refs: kernel(peers, *more, *refs)

    raw = (
        source,
        pressure_old,
        strain_prev,
        motion_old,
        body_force,
        zone_ids,
        drained,
    )
    fields, first, second = call(
        pack_rows,
        [f32(NF, nx, ny, nz), f32(nx, MSG_ROWS, nz), f32(nx, MSG_ROWS, nz)],
        *raw,
        space=pltpu.HBM,
        scratch=[pltpu.VMEM(a.shape, a.dtype) for a in raw]
        + [pltpu.SemaphoreType.DMA((len(raw),))],
        limit=PACK_LIMIT,
    )
    fields_below, fields_above = x_neighbours(fields)
    first = pairs(first, "gy", 0)
    second = pairs(second, "gy", 1)
    first_below, first_above = x_neighbours(first)
    second_below, second_above = x_neighbours(second)
    ends, rightward, leftward = call(
        with_peers(pack_ends),
        [
            f32(NF, groups, ENDS, LANES),
            f32(groups, MSG_ROWS, LANES),
            f32(groups, MSG_ROWS, LANES),
        ],
        fields,
        first,
        second,
        scratch=[vmem(NF * groups, LANES, nz)],
    )
    left = ring(rightward, "gz", 1)
    right = ring(leftward, "gz", -1)
    ends_below, ends_above = x_neighbours(ends)
    depth = nx + 2 * W
    cells = depth * ny * nz

    def shaped(lead, *shape):
        return (lead,) * (lead > 0) + shape

    leads = dict(ARRAYS)
    sums_shape = (up_to(SUMS, TILE), TILE, LANES)
    *kept, added = call(
        with_peers(brick_kernel),
        [f32(*shaped(leads[name], depth, ny + TILE, nz)) for name in KEPT]
        + [f32(*sums_shape)],
        table,
        fields,
        fields_below,
        fields_above,
        first,
        second,
        first_below,
        second_below,
        first_above,
        second_above,
        smem=1,
        scratch=[
            vmem(*shaped(lead, depth, ny + TILE, nz))
            for name, lead in ARRAYS
            if name not in KEPT
        ]
        + [vmem(WIDE, depth, tall, nz), vmem(depth, tall, nz), vmem(depth, tall, nz)],
        limit=24,
        cost=pl.CostEstimate(
            flops=2000 * cells, transcendentals=0, bytes_accessed=400 * cells
        ),
    )
    left, right, added = lax.optimization_barrier((left, right, added))
    left_below, left_above = x_neighbours(left)
    right_below, right_above = x_neighbours(right)
    span = (2 if peers[0] == 2 else 3) * groups + 1
    *ends_kept, partial = call(
        with_peers(ends_kernel, tall),
        [f32(NF, span, ENDS, LANES)]
        + [f32(*shaped(leads[name], span, ENDS, LANES)) for name in KEPT[1:]]
        + [f32(total, LANES)],
        table,
        ends,
        ends_below,
        ends_above,
        left,
        right,
        left_below,
        right_below,
        left_above,
        right_above,
        added,
        smem=1,
        scratch=[vmem(*sums_shape)]
        + [
            vmem(*shaped(lead, span, ENDS, LANES))
            for name, lead in ARRAYS[6:]
            if name not in KEPT
        ],
        limit=16,
    )
    sums = lax.all_to_all(partial, AXES, 0, 0, tiled=True)
    return tuple(
        call(
            with_peers(combine, tall),
            [f32(nx, ny, nz), f32(3, nx, ny, nz), f32(nx, ny, nz)],
            sums,
            *kept,
            fields,
            *ends_kept,
            scratch=[
                vmem(3, depth, ny + TILE, nz),
                vmem(4, span, ENDS, LANES),
                vmem(5 * groups, LANES, LANES),
            ],
            limit=16,
        )
    )


def solution(mesh):
    placed = (
        P("gx", "gy", "gz"),
        P("gx", "gy", "gz"),
        P("gx", "gy", "gz"),
        P(None, "gx", "gy", "gz"),
        P(None, "gx", "gy", "gz"),
        P("gx", "gy", "gz"),
        P("gx", "gy", "gz"),
        P(),
        P(),
        P(),
    )
    return jax.shard_map(
        shards,
        mesh=mesh,
        in_specs=placed,
        out_specs=(P("gx", "gy", "gz"), P(None, "gx", "gy", "gz"), P("gx", "gy", "gz")),
        check_vma=False,
    )
```

```python
import jax
import jax.numpy as jnp
from jax import lax
from jax.experimental import pallas as pl
from jax.experimental.pallas import tpu as pltpu
from jax.sharding import PartitionSpec as P


ZONES = 8

storage = 0.2
biot_coef = 0.8
leakage = 2.0
support = 1.0

AXES = ("gx", "gy", "gz")
LANES = 128
TILE = 8
MIB = 2**20

ZONE, PRESS, MOTION, SOURCE, DRAIN, BODY = 0, 1, 2, 5, 6, 7
WIDTHS = (5, 5, 5, 5, 5, 4, 4, 2, 2, 2)
NF = len(WIDTHS)
WIDE = 5
W = max(WIDTHS)
OFFSETS = tuple(sum(WIDTHS[:f]) for f in range(NF))
PAIRS = tuple((j, k) for j in range(3) for k in range(j, 3))
SUMS = 4 + 4 * len(PAIRS)
SEG = 16
ENDS = 2 * SEG
UNROLL = 4


def up_to(value, multiple):
    return -(-value // multiple) * multiple


MSG_ROWS = up_to(sum(WIDTHS), TILE)


def iota(shape, dim):
    return lax.broadcasted_iota(jnp.int32, shape, dim)


def field_of(raw, f, at):
    source, pressure, strain, motion, body, zones, drained = raw
    if f == ZONE:
        return zones[at].astype(jnp.float32) + 1.0
    if f == PRESS:
        return pressure[at]
    if f == SOURCE:
        return source[at] + biot_coef * strain[at]
    if f == DRAIN:
        return drained[at].astype(jnp.float32)
    return motion[f - MOTION, *at] if f < SOURCE else body[f - BODY, *at]


def fetch(sources, held, arrived):
    copies = [
        pltpu.make_async_copy(source, copy, arrived.at[i])
        for i, (source, copy) in enumerate(zip(sources, held))
    ]
    for copy in copies:
        copy.start()
    for copy in copies:
        copy.wait()


def pack_rows(*refs):
    sources, (first, second, table), held, arrived = refs[:10], refs[10:13], refs[13:23], refs[23]
    fetch(sources, held, arrived)
    raw, tables = held[:7], held[7:]
    nx, ny, nz = raw[0].shape
    spare = MSG_ROWS - sum(WIDTHS)

    def messages(upward, downward):
        for x in range(nx):
            for f in range(NF):
                width, offset = WIDTHS[f], OFFSETS[f]
                value = field_of(raw, f, (x, slice(None)))
                upward[x, offset : offset + width, :] = value[ny - width :]
                downward[x, offset : offset + width, :] = value[:width]
            if spare:
                empty = jnp.zeros((spare, nz), jnp.float32)
                upward[x, MSG_ROWS - spare :, :] = empty
                downward[x, MSG_ROWS - spare :, :] = empty

    even = lax.axis_index("gy") % 2 == 0
    pl.when(even)(lambda: messages(first, second))
    pl.when(jnp.logical_not(even))(lambda: messages(second, first))
    shape = (TILE, LANES)
    tile = jnp.zeros(shape, jnp.float32)
    for t in range(len(tables)):
        for zone in range(ZONES):
            here = (iota(shape, 0) == t) & (iota(shape, 1) == zone + 1)
            tile = jnp.where(here, tables[t][zone], tile)
    table[...] = tile


def pack_fields(*refs):
    sources, fields, held, arrived = refs[:7], refs[8], refs[9:16], refs[16]
    fetch(sources, held, arrived)
    for x in range(fields.shape[1]):
        for f in range(NF):
            fields[f, x] = field_of(held, f, (x, slice(None)))


def keeps(axis, peers):
    at = lax.axis_index(axis)
    return jnp.where(at > 0, 1.0, 0.0), jnp.where(at < peers - 1, 1.0, 0.0)


def blocks_of(peers):
    at = lax.axis_index("gx")
    if peers[0] == 2:
        return [(at, 1.0), (1 - at, 1.0)]
    keep_below, keep_above = keeps("gx", peers[0])
    return [(1, 1.0), (0, keep_below), (2, keep_above)]


class Rows:
    def __init__(self, first, second, peers):
        self.refs = first, second
        self.even = lax.axis_index("gy") % 2 == 0
        self.keep = keeps("gy", peers[1])

    def read(self, f, x):
        width, offset = WIDTHS[f], OFFSETS[f]
        a, b = [ref[x, offset : offset + width, :] for ref in self.refs]
        low, high = jnp.where(self.even, b, a), jnp.where(self.even, a, b)
        return low * self.keep[0], high * self.keep[1]


def keeps(axis, peers):
    at = lax.axis_index(axis)
    return jnp.where(at > 0, 1.0, 0.0), jnp.where(at < peers - 1, 1.0, 0.0)


def pack_ends(peers, *refs):
    ends, rightward, leftward, stage = refs[-4:]
    blocks = blocks_of(peers)
    _, nx, ny, nz = refs[0].shape
    tall = ny + 2 * TILE
    pack = LANES // tall
    count = nx // pack
    gap = jnp.zeros((TILE, nz), jnp.float32)
    zeros = jnp.zeros((TILE, LANES), jnp.float32)
    inner = SEG - W
    spare = MSG_ROWS - sum(WIDTHS)
    for b, (start, keep) in enumerate(blocks):
        fields = refs[b]
        first, second = refs[len(blocks) + 2 * b : len(blocks) + 2 * b + 2]
        rows = Rows(first, second, peers)
        for i in range(count):
            g = start * count + i
            if spare:
                rightward[g, MSG_ROWS - spare :, :] = zeros[:spare]
                leftward[g, MSG_ROWS - spare :, :] = zeros[:spare]
            for f in range(NF):
                width, offset = WIDTHS[f], OFFSETS[f]
                slot = (b * count + i) * NF + f
                for p in range(pack):
                    x = i * pack + p
                    top = p * tall
                    stage[slot, top : top + TILE, :] = gap
                    stage[slot, top + TILE + ny : top + tall, :] = gap
                    stage[slot, top + TILE : top + TILE + ny, :] = fields[f, x]
                    low, high = rows.read(f, x)
                    stage[slot, top + TILE - width : top + TILE, :] = low
                    stage[slot, top + TILE + ny : top + TILE + ny + width, :] = high
                begin = stage[slot, :, :LANES].T
                finish = begin if nz == LANES else stage[slot, :, nz - LANES :].T
                if len(blocks) > 2:
                    begin, finish = begin * keep, finish * keep
                rightward[g, offset : offset + width, :] = finish[LANES - width :]
                leftward[g, offset : offset + width, :] = begin[:width]
                ends[f, g, :TILE, :] = zeros
                ends[f, g, ENDS - TILE :, :] = zeros
                ends[f, g, W:SEG, :] = begin[:inner]
                ends[f, g, SEG : ENDS - W, :] = finish[LANES - inner :]


def harmonic(a, b):
    return 2.0 * a * b / jnp.maximum(a + b, 1e-30)


def lookup(zone, table, row):
    entries = jnp.broadcast_to(table[row : row + 1, :], zone.shape[:-1] + (LANES,))
    index = zone.astype(jnp.int32)
    picked = [
        jnp.take_along_axis(
            entries, index[:, start : start + LANES], axis=1, mode="promise_in_bounds"
        )
        for start in range(0, zone.shape[1], LANES)
    ]
    return picked[0] if len(picked) == 1 else jnp.concatenate(picked, axis=1)


def fixed_term(zone, lame, shear):
    scale = jnp.maximum(lame + 2.0 * shear / 3.0, 1e-30)
    return jnp.where(zone > 0.0, biot_coef * biot_coef / scale, 0.0)


KEPT = ("motion", "z0", "p0", "zs", "ps")
ARRAYS = (
    ("zone", 0),
    ("press", 0),
    ("motion", 3),
    ("load", 0),
    ("drain", 0),
    ("body", 3),
    ("perm", 0),
    ("heft", 0),
    ("shear", 0),
    ("fixed", 0),
    ("tx", 0),
    ("ty", 0),
    ("tz", 0),
    ("mx", 0),
    ("my", 0),
    ("mz", 0),
    ("react", 0),
    ("pdiag", 0),
    ("pinv", 0),
    ("z0", 0),
    ("p0", 0),
    ("ediag", 3),
    ("einv", 3),
    ("push", 3),
    ("zs", 9),
    ("ps", 9),
)


class Domain:
    def __init__(self, arrays):
        self.__dict__.update(arrays)

    def press_faces(self, l):
        own = self.perm[l]
        self.tx[l] = harmonic(own, self.nxt(self.perm, l))
        self.ty[l] = harmonic(own, self.yp(own))
        self.tz[l] = harmonic(own, self.zp(own))

    def motion_faces(self, l):
        own = self.shear[l]
        self.mx[l] = harmonic(own, self.nxt(self.shear, l))
        self.my[l] = harmonic(own, self.yp(own))
        self.mz[l] = harmonic(own, self.zp(own))

    def steps(self, ref, l):
        own = ref[l]
        return self.nxt(ref, l) - own, self.yp(own) - own, self.zp(own) - own

    def back_y(self, value):
        return self.ym(value) - value

    def back_z(self, value):
        return self.zm(value) - value

    def press_flux(self, ref, l, along_y=True):
        dx, dy, dz = self.steps(ref, l)
        total = self.back_x(self.tx, dx, ref, l) + self.back_z(self.tz[l] * dz)
        return total + self.back_y(self.ty[l] * dy) if along_y else total

    def y_terms(self, l):
        face = self.ty[l]
        own, middle = self.press[l], self.motion[1, l]
        return (
            face + self.ym(face),
            self.back_y(face * (self.yp(own) - own))
            + (0.5 * biot_coef) * (self.yp(middle) - self.ym(middle)),
        )

    def press_start(self, l):
        face_sum, y_part = self.y_terms(l)
        face = self.tz[l]
        leak = leakage * self.drain[l]
        reaction = storage + self.fixed[l] + leak
        diag = (
            reaction
            + self.tx[l]
            + self.prv(self.tx, l)
            + face_sum
            + (face + self.zm(face))
        )
        inverse = jnp.where(self.zone[l] > 0.0, 1.0 / diag, 0.0)
        along_x, along_z = self.motion.at[0], self.motion[2, l]
        change = (self.nxt(along_x, l) - self.prv(along_x, l)) + (
            self.zp(along_z) - self.zm(along_z)
        )
        residual = (
            self.load[l]
            - (0.5 * biot_coef) * change
            - leak * self.press[l]
            - self.press_flux(self.press, l, False)
            - y_part
        )
        self.react[l] = reaction
        self.pdiag[l] = diag
        self.pinv[l] = inverse
        self.z0[l] = residual * inverse

    def press_next(self, l):
        image = self.react[l] * self.z0[l] + self.press_flux(self.z0, l)
        self.p0[l] = image * self.pinv[l]

    @staticmethod
    def parts(ref, j):
        return [ref.at[3 * j + c] for c in range(3)]

    def elastic(self, refs, l, j):
        steps = [self.steps(ref, l) for ref in refs]
        pushed = self.heft[l] * (steps[0][0] + steps[1][1] + steps[2][2])
        self.keep_push(j, l, pushed)
        out = []
        for c in range(3):
            dx, dy, dz = steps[c]
            step_y, step_z = self.my[l] * dy, self.mz[l] * dz
            if c == 1:
                step_y = step_y + pushed
            if c == 2:
                step_z = step_z + pushed
            push = (j, pushed) if c == 0 else None
            out.append(
                support * refs[c][l]
                + self.back_x(self.mx, dx, refs[c], l, push)
                + self.back_y(step_y)
                + self.back_z(step_z)
            )
        return out

    def gradient(self, ref, l):
        own = ref[l]
        return (
            0.5 * (self.nxt(ref, l) - self.prv(ref, l)),
            0.5 * (self.yp(own) - self.ym(own)),
            0.5 * (self.zp(own) - self.zm(own)),
        )

    def motion_start(self, l):
        weight = self.heft[l]
        along_y, along_z = self.my[l], self.mz[l]
        base = (
            support
            + self.mx[l]
            + self.prv(self.mx, l)
            + (along_y + self.ym(along_y))
            + (along_z + self.zm(along_z))
            + weight
        )
        inside = self.zone[l] > 0.0
        beside = (self.prv(self.heft, l), self.ym(weight), self.zm(weight))
        image = self.elastic(self.parts(self.motion, 0), l, 0)
        grads = [self.gradient(ref, l) for ref in (self.press, self.z0, self.p0)]
        for c in range(3):
            diag = base + beside[c]
            inverse = jnp.where(inside, 1.0 / diag, 0.0)
            self.ediag[c, l] = diag
            self.einv[c, l] = inverse
            start = self.body[c, l] - biot_coef * grads[0][c] - image[c]
            self.zs[c, l] = start * inverse
            scale = -biot_coef * inverse
            self.zs[3 + c, l] = grads[1][c] * scale
            self.zs[6 + c, l] = grads[2][c] * scale

    def motion_next(self, l, j):
        image = self.elastic(self.parts(self.zs, j), l, j)
        for c in range(3):
            self.ps[3 * j + c, l] = image[c] * self.einv[c, l]

    def stages(self):
        self.run(4, self.press_faces, 1)
        self.run(4, self.press_start)
        self.run(3, self.press_next)
        self.run(2, self.motion_faces, 1)
        self.lead(2, lambda l: self.first_push(self.parts(self.motion, 0), l, 0))
        self.run(2, self.motion_start)
        for j in range(3):
            self.lead(1, lambda l: self.first_push(self.parts(self.zs, j), l, j))
            self.run(1, lambda l: self.motion_next(l, j))

    def finish(self, l, acc, mask):
        own = self.own

        def add(index, value):
            acc[index] = acc[index] + self.fold(value, mask)

        def total(pairs):
            out = None
            for a, b in pairs:
                out = a * b if out is None else out + a * b
            return out

        a, b = own(self.z0[l]), own(self.p0[l])
        diag = own(self.pdiag[l])
        scaled = diag * b
        add(0, diag * a * a)
        add(1, scaled * a)
        add(2, scaled * b)
        energy = own(self.react[l]) * b * b
        for face, step in zip((self.tx, self.ty, self.tz), self.steps(self.p0, l)):
            step = own(step)
            energy = energy + own(face[l]) * step * step
        add(3, energy)
        diags = [own(self.ediag[c, l]) for c in range(3)]
        faces = [own(ref[l]) for ref in (self.mx, self.my, self.mz)]
        weight = own(self.heft[l])
        za, pa, dz, dp, steps, heavy = [], [], [], [], [], []
        for j in range(3):
            zj, pj = self.parts(self.zs, j), self.parts(self.ps, j)
            za.append([own(ref[l]) for ref in zj])
            pa.append([own(ref[l]) for ref in pj])
            dz.append([d * v for d, v in zip(diags, za[j])])
            dp.append([d * v for d, v in zip(diags, pa[j])])
            moved = [[own(v) for v in self.steps(ref, l)] for ref in pj]
            div = moved[0][0] + moved[1][1] + moved[2][2]
            flat = [(faces[d], moved[c][d]) for c in range(3) for d in range(3)]
            steps.append([v for _, v in flat] + [div] + pa[j])
            heavy.append([f * v for f, v in flat] + [weight * div])
            heavy[j] = heavy[j] + [support * v for v in pa[j]]
        for i, (j, k) in enumerate(PAIRS):
            add(4 + i, total(zip(dz[j], za[k])))
            add(10 + i, total(zip(dp[k], za[j])))
            add(16 + i, total(zip(dp[j], pa[k])))
            add(22 + i, total(zip(heavy[j], steps[k])))

    @staticmethod
    def loop(start, count, body, unroll=UNROLL):
        if not isinstance(count, int):
            unroll = 1
        chunks = count // unroll

        def step(i, carry):
            for u in range(unroll):
                body(start + i * unroll + u)
            return carry

        if isinstance(chunks, int) and chunks == 1:
            step(0, 0)
        else:
            lax.fori_loop(0, chunks, step, 0)
        if isinstance(count, int):
            for u in range(chunks * unroll, count):
                body(start + u)


class Brick(Domain):
    def nxt(self, ref, l):
        return ref[l + 1]

    def prv(self, ref, l):
        return ref[l - 1]

    def yp(self, v):
        return pltpu.roll(v, v.shape[0] - 1, 0)

    def ym(self, v):
        return pltpu.roll(v, 1, 0)

    def zp(self, v):
        return pltpu.roll(v, v.shape[1] - 1, 1)

    def zm(self, v):
        return pltpu.roll(v, 1, 1)

    def back_x(self, faces, step, ref, l, push=None):
        out = faces[l - 1] * (ref[l] - ref[l - 1]) - faces[l] * step
        if push:
            out = out + (self.push[push[0], l - 1] - push[1])
        return out

    def keep_push(self, j, l, value):
        self.push[j, l] = value

    def first_push(self, refs, l, j):
        dx, dy, dz = [self.steps(ref, l)[i] for i, ref in enumerate(refs)]
        self.push[j, l] = self.heft[l] * (dx + dy + dz)

    def own(self, v):
        return v[: self.ny]

    def fold(self, value, mask):
        total = value[:TILE]
        for start in range(TILE, value.shape[0], TILE):
            total = total + value[start : start + TILE]
        total = jnp.where(mask, total, 0.0)
        folded = total[:, :LANES]
        for start in range(LANES, value.shape[1], LANES):
            folded = folded + total[:, start : start + LANES]
        return folded

    def first(self, halo):
        return W - halo * self.has_below

    def reach(self, halo):
        if self.pair:
            return halo
        return halo * (self.has_below + self.has_above)

    def run(self, halo, body, before=0):
        self.loop(self.first(halo) - before, self.nx + self.reach(halo) + before, body)

    def lead(self, halo, body):
        body(self.first(halo) - 1)

    def narrow(self, v):
        ny = self.ny
        upper, lower = v[ny : ny + TILE], v[ny + TILE :]
        both = jnp.where(iota(upper.shape, 0) < TILE // 2, upper, lower)
        return jnp.concatenate([v[:ny], both], axis=0)

    def press_faces(self, l):
        own = self.perm[l]
        self.tx[l] = harmonic(own, self.nxt(self.perm, l))
        tall = self.perm_tall[l]
        face = harmonic(tall, self.yp(tall))
        self.ty_tall[l] = face
        self.ty[l] = self.narrow(face)
        self.tz[l] = harmonic(own, self.zp(own))

    def y_terms(self, l):
        face = self.ty_tall[l]
        own, middle = self.tall[PRESS, l], self.tall[MOTION + 1, l]
        return (
            self.narrow(face + self.ym(face)),
            self.narrow(
                self.back_y(face * (self.yp(own) - own))
                + (0.5 * biot_coef) * (self.yp(middle) - self.ym(middle))
            ),
        )

    def assemble(self, l, x, fields, beside, table):
        ny = self.ny
        rows = ny + 2 * TILE
        gap = jnp.zeros((2 * TILE, fields.shape[3]), jnp.float32)
        narrow_rows = ny + TILE
        slim = (self.load, self.drain) + tuple(self.body.at[c] for c in range(3))
        for f in range(NF):
            width = WIDTHS[f]
            below, above = beside.read(f, x)
            if f < WIDE:
                self.tall[f, l, :ny, :] = fields[f, x]
                self.tall[f, l, ny:, :] = gap
                self.tall[f, l, ny : ny + width, :] = above
                self.tall[f, l, rows - width :, :] = below
            else:
                ref = slim[f - WIDE]
                ref[l, :ny, :] = fields[f, x]
                ref[l, ny:, :] = gap[:TILE]
                ref[l, ny : ny + width, :] = above
                ref[l, narrow_rows - width :, :] = below
        tall_zone = self.tall[ZONE, l]
        perm = lookup(tall_zone, table, 0)
        self.perm_tall[l] = perm
        self.perm[l] = self.narrow(perm)
        zone = self.narrow(tall_zone)
        self.zone[l] = zone
        lame, shear = lookup(zone, table, 1), lookup(zone, table, 2)
        self.heft[l] = lame + shear
        self.shear[l] = shear
        self.fixed[l] = fixed_term(zone, lame, shear)
        self.press[l] = self.narrow(self.tall[PRESS, l])
        for c in range(3):
            self.motion[c, l] = self.narrow(self.tall[MOTION + c, l])


def brick_kernel(peers, *refs):
    table, fields, below, above = refs[:4]
    rows = [Rows(*refs[i : i + 2], peers) for i in (4, 6, 8)]
    outs, acc, scratch = refs[10 : 10 + len(KEPT)], refs[10 + len(KEPT)], refs[11 + len(KEPT) :]
    inner = len(ARRAYS) - len(KEPT)
    names = [name for name, _ in ARRAYS if name not in KEPT]
    domain = Brick(dict(zip(names, scratch[:inner])))
    domain.__dict__.update(zip(KEPT, outs))
    domain.tall, domain.perm_tall, domain.ty_tall = scratch[inner:]
    _, nx, ny, nz = fields.shape
    domain.nx, domain.ny = nx, ny
    at = lax.axis_index("gx")
    domain.has_below = (at > 0).astype(jnp.int32)
    domain.has_above = (at < peers[0] - 1).astype(jnp.int32)
    domain.pair = peers[0] == 2

    empty = jnp.zeros((ny + TILE, nz), jnp.float32)
    for l in (W - 1, W + nx):
        for name in ("perm", "heft", "shear", "press", "z0", "p0"):
            getattr(domain, name)[l] = empty
        for c in range(3):
            domain.motion[c, l] = empty
        for i in range(9):
            domain.zs[i, l] = empty
            domain.ps[i, l] = empty
        domain.perm_tall[l] = jnp.zeros((ny + 2 * TILE, nz), jnp.float32)

    def block(start, count, shift, *source):
        domain.loop(
            start, count, lambda l: domain.assemble(l, l + shift, *source, table)
        )

    block(W, nx, -W, fields, rows[0])
    if domain.pair:
        start = jnp.where(at > 0, 0, W + nx)
        shift = jnp.where(at > 0, nx - W, -W - nx)
        block(start, W, shift, below, rows[1])
    else:
        block(0, W * domain.has_below, nx - W, below, rows[1])
        block(W + nx, W * domain.has_above, -W - nx, above, rows[2])
    domain.stages()
    acc[...] = jnp.zeros(acc.shape, jnp.float32)
    column = iota((TILE, nz), 1)
    mask = (column >= W) & (column < nz - W)
    domain.loop(W, nx, lambda l: domain.finish(l, acc, mask))


class Ends(Domain):
    def roll(self, v, shift):
        return pltpu.roll(v, shift % LANES, v.ndim - 1)

    def nxt(self, ref, l):
        moved = self.roll(ref[pl.ds(l.start, l.size + 1)], -self.row)
        lane = iota(moved[1:].shape, 2)
        return jnp.where(lane < LANES - self.row, moved[:-1], moved[1:])

    def before(self, v):
        moved = self.roll(v, self.row)
        back = jnp.concatenate([jnp.zeros_like(moved[:1]), moved[:-1]], axis=0)
        return jnp.where(iota(moved.shape, 2) >= self.row, moved, back)

    def prv(self, ref, l):
        return self.before(ref[l])

    def back_x(self, faces, step, ref, l, push=None):
        value = faces[l] * step
        if push:
            value = value + push[1]
        return self.before(value) - value

    def keep_push(self, j, l, value):
        pass

    def yp(self, v):
        return self.roll(v, -1)

    def ym(self, v):
        return self.roll(v, 1)

    def zp(self, v):
        return pltpu.roll(v, ENDS - 1, 1)

    def zm(self, v):
        return pltpu.roll(v, 1, 1)

    def own(self, v):
        return v

    def fold(self, value, mask):
        total = None
        for g in range(value.shape[0]):
            part = jnp.where(mask, value[g], 0.0)
            for start in range(0, value.shape[1], TILE):
                piece = part[start : start + TILE]
                total = piece if total is None else total + piece
        return total

    def run(self, halo, body, before=0):
        body(pl.ds(0, self.groups))

    def lead(self, halo, body):
        pass

    def assemble(self, ends, left, right, keep_left, keep_right, table):
        for g in range(self.groups):
            for f in range(NF):
                width, offset = WIDTHS[f], OFFSETS[f]
                rows = slice(offset, offset + width)
                self.raw[f, g] = ends[f, g]
                self.raw[f, g, W - width : W, :] = left[g, rows, :] * keep_left
                self.raw[f, g, ENDS - W : ENDS - W + width, :] = (
                    right[g, rows, :] * keep_right
                )
            zone = self.raw[ZONE, g]
            lame, shear = lookup(zone, table, 1), lookup(zone, table, 2)
            self.perm[g] = lookup(zone, table, 0)
            self.heft[g] = lame + shear
            self.shear[g] = shear
            self.fixed[g] = fixed_term(zone, lame, shear)


def own_groups(count, peers):
    return count * blocks_of(peers)[0][0]


def ends_kernel(peers, tall, *refs):
    table, ends, left, right, added = refs[:5]
    raw, z0, p0, zs, ps, partial = refs[5:11]
    acc, scratch = refs[11], refs[12:]
    names = [name for name, _ in ARRAYS[6:] if name not in KEPT]
    domain = Ends(dict(zip(names, scratch)))
    domain.raw, domain.z0, domain.p0, domain.zs, domain.ps = raw, z0, p0, zs, ps
    domain.zone, domain.press = raw.at[ZONE], raw.at[PRESS]
    domain.motion = raw.at[MOTION : MOTION + 3]
    domain.load, domain.drain = raw.at[SOURCE], raw.at[DRAIN]
    domain.body = raw.at[BODY : BODY + 3]
    domain.row = tall
    domain.groups = groups = raw.shape[1] - 1
    count = groups // len(blocks_of(peers))
    keep = keeps("gz", peers[2])
    empty = jnp.zeros((ENDS, LANES), jnp.float32)
    for ref in (raw, zs, ps):
        for i in range(ref.shape[0]):
            ref[i, groups] = empty
    for ref in (domain.perm, domain.shear, z0, p0):
        ref[groups] = empty
    mine = own_groups(count, peers)
    domain.assemble(ends, left, right, *keep, table)
    domain.stages()
    acc[...] = added[...]
    shape = (ENDS, LANES)
    column, row = iota(shape, 0), iota(shape, 1) % tall
    at_end = ((column >= W) & (column < 2 * W)) | (
        (column >= ENDS - 2 * W) & (column < ENDS - W)
    )
    mask = at_end & (row >= TILE) & (row < tall - TILE)
    domain.finish(pl.ds(mine, count), acc, mask)

    sums = jnp.concatenate(
        [jnp.sum(acc[i], axis=0, keepdims=True) for i in range(acc.shape[0])], axis=0
    )
    totals = jnp.sum(sums, axis=1, keepdims=True)
    spread = jnp.where(iota(sums.shape, 0) == iota(sums.shape, 1), totals, 0.0)
    line = jnp.sum(spread, axis=0, keepdims=True)
    partial[...] = jnp.broadcast_to(line, partial.shape)


def step_sizes(gamma, delta, cross, energy):
    first = gamma / delta
    gamma_new = gamma - 2.0 * first * delta + first * first * cross
    curved = delta - 2.0 * first * cross + first * first * energy
    ratio = gamma_new / gamma
    second = gamma_new / (curved - ratio * gamma_new / first)
    return first + second * (1.0 + ratio), -first * second


def combine(peers, tall, *refs):
    sums, (old, z0, p0, zs, ps), fields = refs[0], refs[1:6], refs[6]
    raw, ends_z0, ends_p0, ends_zs, ends_ps = refs[7:12]
    pressure, motion, strain, moved, ends_moved, turned = refs[12:]
    line = jnp.sum(sums[...], axis=0, keepdims=True)
    lane = iota(line.shape, 1)

    def value(index):
        return jnp.sum(jnp.where(lane == index, line, 0.0), axis=1, keepdims=True)

    c1, c2 = step_sizes(*[value(i) for i in range(4)])
    weights = (jnp.ones_like(c1), c1, c2)

    def form(start):
        total = 0.0
        for i, (j, k) in enumerate(PAIRS):
            scale = 1.0 if j == k else 2.0
            total = total + scale * weights[j] * weights[k] * value(start + i)
        return total

    d1, d2 = step_sizes(form(4), form(10), form(16), form(22))
    on_z = [d1 * w for w in weights]
    on_p = [d2 * w for w in weights]

    def new_motion(start, z_part, p_part, c, i):
        total = start
        for j in range(3):
            total = total + on_z[j] * z_part[3 * j + c, i]
            total = total + on_p[j] * p_part[3 * j + c, i]
        return total

    nx, ny, nz = pressure.shape
    pack = LANES // tall
    ends = Ends(dict(row=tall))
    groups = raw.shape[1] - 1
    count = groups // len(blocks_of(peers))
    mine = own_groups(count, peers)
    every = pl.ds(0, groups)
    for c in range(3):
        for g in range(groups):
            ends_moved[c, g] = new_motion(raw[MOTION + c, g], ends_zs, ends_ps, c, g)
        ends_moved[c, groups] = jnp.zeros((ENDS, LANES), jnp.float32)
    along_y, along_z = ends_moved[1, every], ends_moved[2, every]
    first = ends_moved.at[0]
    ends_moved[3, every] = 0.5 * (
        (ends.nxt(first, every) - ends.prv(first, every))
        + (ends.yp(along_y) - ends.ym(along_y))
        + (ends.zp(along_z) - ends.zm(along_z))
    )
    for c in range(3):
        around = 1 if c == 0 else 0
        for l in range(W - around, W + nx + around):
            moved[c, l] = new_motion(old[c, l], zs, ps, c, l)
    brick = Brick({})
    outs = [pressure] + [motion.at[c] for c in range(3)] + [strain]
    for g in range(count):
        at = mine + g
        edges = [raw[PRESS, at] + c1 * ends_z0[at] + c2 * ends_p0[at]]
        edges = edges + [ends_moved[c, at] for c in range(4)]
        flipped = []
        for o, edge in enumerate(edges):
            slot = g * len(outs) + o
            turned[slot, :W, :] = edge[W : 2 * W]
            turned[slot, LANES - W :, :] = edge[ENDS - 2 * W : ENDS - W]
            flipped.append(turned[slot].T)
        for i in range(pack):
            x = g * pack + i
            l = W + x
            top = i * tall + TILE
            column = iota((ny, LANES), 1)
            u = [moved[c, l] for c in range(3)]
            change = (
                (moved[0, l + 1] - moved[0, l - 1])
                + (brick.yp(u[1]) - brick.ym(u[1]))
                + (brick.zp(u[2]) - brick.zm(u[2]))
            )
            results = [fields[PRESS, x] + c1 * z0[l, :ny, :] + c2 * p0[l, :ny, :]]
            results = results + [v[:ny] for v in u] + [0.5 * change[:ny]]
            for out, result, edge in zip(outs, results, flipped):
                edge = edge[top : top + ny]
                if nz == LANES:
                    inner = (column >= W) & (column < LANES - W)
                    out[x] = jnp.where(inner, result, edge)
                else:
                    out[x] = result
                    out[x, :, :LANES] = jnp.where(column >= W, result[:, :LANES], edge)
                    out[x, :, nz - LANES :] = jnp.where(
                        column < LANES - W, result[:, nz - LANES :], edge
                    )


def f32(*shape):
    return jax.ShapeDtypeStruct(shape, jnp.float32)


def vmem(*shape):
    return pltpu.VMEM(shape, jnp.float32)


def call(kernel, outs, *args, unread=0, space=pltpu.VMEM, scratch=(), limit=8, cost=None):
    specs = [
        pl.BlockSpec(memory_space=space if i < len(args) - unread else pl.ANY)
        for i in range(len(args))
    ]
    return pl.pallas_call(
        kernel,
        out_shape=outs,
        in_specs=specs,
        scratch_shapes=scratch,
        cost_estimate=cost,
        compiler_params=pltpu.CompilerParams(vmem_limit_bytes=limit * MIB),
    )(*args)


def ring(value, axis, step):
    peers = lax.axis_size(axis)
    return lax.ppermute(value, axis, [(i, (i + step) % peers) for i in range(peers)])


def pairs(value, axis, start):
    peers = lax.axis_size(axis)
    swaps = [(i, i) for i in range(start)]
    for i in range(start, peers - 1, 2):
        swaps += [(i, i + 1), (i + 1, i)]
    swaps += [(i, i) for i in range(len(swaps), peers)]
    return lax.ppermute(value, axis, swaps)


def x_neighbours(value):
    peers = lax.axis_size("gx")
    above = ring(value, "gx", -1)
    below = above if peers == 2 else ring(value, "gx", 1)
    return below, above


def shards(
    source,
    pressure_old,
    strain_prev,
    motion_old,
    body_force,
    zone_ids,
    drained,
    perm_table,
    lame_table,
    shear_table,
):
    nx, ny, nz = source.shape
    peers = [lax.axis_size(a) for a in AXES]
    total = peers[0] * peers[1] * peers[2]
    tall = ny + 2 * TILE
    groups = nx * tall // LANES

    def with_peers(kernel, *more):
        return lambda *refs: kernel(peers, *more, *refs)

    raw = (
        source,
        pressure_old,
        strain_prev,
        motion_old,
        body_force,
        zone_ids,
        drained,
    )
    raw = [pltpu.with_memory_space_constraint(a, pltpu.HBM) for a in raw]
    held = [pltpu.VMEM(a.shape, a.dtype) for a in raw]
    tables = [
        pltpu.with_memory_space_constraint(a, pltpu.HBM)
        for a in (perm_table, lame_table, shear_table)
    ]
    message = f32(nx, MSG_ROWS, nz)
    first, second, table = call(
        pack_rows,
        [message, message, f32(TILE, LANES)],
        *raw,
        *tables,
        space=pltpu.HBM,
        scratch=held
        + [pltpu.SMEM(a.shape, a.dtype) for a in tables]
        + [pltpu.SemaphoreType.DMA((len(raw) + len(tables),))],
    )
    (fields,) = call(
        pack_fields,
        [f32(NF, nx, ny, nz)],
        *raw,
        table,
        space=pltpu.HBM,
        unread=1,
        scratch=held + [pltpu.SemaphoreType.DMA((len(raw),))],
    )
    fields_below, fields_above = x_neighbours(fields)
    first = pairs(first, "gy", 0)
    second = pairs(second, "gy", 1)
    first_below, first_above = x_neighbours(first)
    second_below, second_above = x_neighbours(second)
    blocks = [
        (fields, first, second),
        (fields_below, first_below, second_below),
        (fields_above, first_above, second_above),
    ][: 2 if peers[0] == 2 else 3]
    span = len(blocks) * groups
    ends, rightward, leftward = call(
        with_peers(pack_ends),
        [
            f32(NF, span, ENDS, LANES),
            f32(span, MSG_ROWS, LANES),
            f32(span, MSG_ROWS, LANES),
        ],
        *[block[0] for block in blocks],
        *[rows for block in blocks for rows in block[1:]],
        scratch=[vmem(NF * span, LANES, nz)],
        limit=12,
    )
    left = ring(rightward, "gz", 1)
    right = ring(leftward, "gz", -1)
    depth = nx + 2 * W
    cells = depth * ny * nz

    def shaped(lead, *shape):
        return (lead,) * (lead > 0) + shape

    leads = dict(ARRAYS)
    sums_shape = (up_to(SUMS, TILE), TILE, LANES)
    *kept, added = call(
        with_peers(brick_kernel),
        [f32(*shaped(leads[name], depth, ny + TILE, nz)) for name in KEPT]
        + [f32(*sums_shape)],
        table,
        fields,
        fields_below,
        fields_above,
        first,
        second,
        first_below,
        second_below,
        first_above,
        second_above,
        scratch=[
            vmem(*shaped(lead, depth, ny + TILE, nz))
            for name, lead in ARRAYS
            if name not in KEPT
        ]
        + [vmem(WIDE, depth, tall, nz), vmem(depth, tall, nz), vmem(depth, tall, nz)],
        limit=24,
        cost=pl.CostEstimate(
            flops=2000 * cells, transcendentals=0, bytes_accessed=400 * cells
        ),
    )
    left, right, added = lax.optimization_barrier((left, right, added))
    span = span + 1
    *ends_kept, partial = call(
        with_peers(ends_kernel, tall),
        [f32(NF, span, ENDS, LANES)]
        + [f32(*shaped(leads[name], span, ENDS, LANES)) for name in KEPT[1:]]
        + [f32(total, LANES)],
        table,
        ends,
        left,
        right,
        added,
        scratch=[vmem(*sums_shape)]
        + [
            vmem(*shaped(lead, span, ENDS, LANES))
            for name, lead in ARRAYS[6:]
            if name not in KEPT
        ],
        limit=16,
    )
    sums = lax.all_to_all(partial, AXES, 0, 0, tiled=True)
    return tuple(
        call(
            with_peers(combine, tall),
            [f32(nx, ny, nz), f32(3, nx, ny, nz), f32(nx, ny, nz)],
            sums,
            *kept,
            fields,
            *ends_kept,
            scratch=[
                vmem(3, depth, ny + TILE, nz),
                vmem(4, span, ENDS, LANES),
                vmem(5 * groups, LANES, LANES),
            ],
            limit=16,
        )
    )


def solution(mesh):
    placed = (
        P("gx", "gy", "gz"),
        P("gx", "gy", "gz"),
        P("gx", "gy", "gz"),
        P(None, "gx", "gy", "gz"),
        P(None, "gx", "gy", "gz"),
        P("gx", "gy", "gz"),
        P("gx", "gy", "gz"),
        P(),
        P(),
        P(),
    )
    return jax.shard_map(
        shards,
        mesh=mesh,
        in_specs=placed,
        out_specs=(P("gx", "gy", "gz"), P(None, "gx", "gy", "gz"), P("gx", "gy", "gz")),
        check_vma=False,
    )
```

```python
import jax
import jax.numpy as jnp
from jax import lax
from jax.experimental import pallas as pl
from jax.experimental.pallas import tpu as pltpu
from jax.sharding import PartitionSpec as P


ZONES = 8

storage = 0.2
biot_coef = 0.8
leakage = 2.0
support = 1.0

AXES = ("gx", "gy", "gz")
LANES = 128
TILE = 8
MIB = 2**20

ZONE, PRESS, MOTION, SOURCE, DRAIN, BODY = 0, 1, 2, 5, 6, 7
WIDTHS = (5, 5, 5, 5, 5, 4, 4, 2, 2, 2)
NF = len(WIDTHS)
WIDE = 5
W = max(WIDTHS)
OFFSETS = tuple(sum(WIDTHS[:f]) for f in range(NF))
PAIRS = tuple((j, k) for j in range(3) for k in range(j, 3))
SUMS = 4 + 4 * len(PAIRS)
SEG = 16
ENDS = 2 * SEG
UNROLL = dict(assemble=8, faces=8, start=8, next=8, shear=8, motion=8, image=8, finish=8)


def up_to(value, multiple):
    return -(-value // multiple) * multiple


MSG_ROWS = up_to(sum(WIDTHS), TILE)


def iota(shape, dim):
    return lax.broadcasted_iota(jnp.int32, shape, dim)


def field_of(raw, f, at):
    source, pressure, strain, motion, body, zones, drained = raw
    if f == ZONE:
        return zones[at].astype(jnp.float32) + 1.0
    if f == PRESS:
        return pressure[at]
    if f == SOURCE:
        return source[at] + biot_coef * strain[at]
    if f == DRAIN:
        return drained[at].astype(jnp.float32)
    return motion[f - MOTION, *at] if f < SOURCE else body[f - BODY, *at]


class Fetch:
    def __init__(self, sources, held, arrived):
        self.held = held
        self.copies = [
            pltpu.make_async_copy(source, copy, arrived.at[i])
            for i, (source, copy) in enumerate(zip(sources, held))
        ]
        self.waiting = set(range(len(held)))
        for i in sorted(self.waiting, key=lambda i: FETCH_ORDER.index(i)):
            self.copies[i].start()

    def need(self, *which):
        for i in which:
            if i in self.waiting:
                self.waiting.remove(i)
                self.copies[i].wait()


FETCH_ORDER = (5, 1, 3, 0, 2, 6, 4, 7, 8, 9)
NEEDS = ((5,), (1,), (3,), (3,), (3,), (0, 2), (6,), (4,), (4,), (4,))


def pack_rows(*refs):
    sources, (first, second, table), held, arrived = refs[:10], refs[10:13], refs[13:23], refs[23]
    fetch = Fetch(sources, held, arrived)
    raw, tables = held[:7], held[7:]
    nx, ny, nz = raw[0].shape
    spare = MSG_ROWS - sum(WIDTHS)
    even = lax.axis_index("gy") % 2 == 0
    for f in range(NF):
        width, offset = WIDTHS[f], OFFSETS[f]
        rows = slice(offset, offset + width)
        fetch.need(*NEEDS[f])
        for x in range(nx):
            value = field_of(raw, f, (x, slice(None)))
            upward, downward = value[ny - width :], value[:width]
            first[x, rows, :] = jnp.where(even, upward, downward)
            second[x, rows, :] = jnp.where(even, downward, upward)
    if spare:
        for x in range(nx):
            for ref in (first, second):
                ref[x, MSG_ROWS - spare :, :] = jnp.zeros((spare, nz), jnp.float32)
    fetch.need(7, 8, 9)
    shape = (TILE, LANES)
    tile = jnp.zeros(shape, jnp.float32)
    for t in range(len(tables)):
        for zone in range(ZONES):
            here = (iota(shape, 0) == t) & (iota(shape, 1) == zone + 1)
            tile = jnp.where(here, tables[t][zone], tile)
    table[...] = tile


def pack_fields(*refs):
    sources, fields, held, arrived = refs[:7], refs[8], refs[9:16], refs[16]
    fetch = Fetch(sources, held, arrived)
    for f in range(NF):
        fetch.need(*NEEDS[f])
        for x in range(fields.shape[1]):
            fields[f, x] = field_of(held, f, (x, slice(None)))


def keeps(axis, peers):
    at = lax.axis_index(axis)
    return jnp.where(at > 0, 1.0, 0.0), jnp.where(at < peers - 1, 1.0, 0.0)


def blocks_of(peers):
    at = lax.axis_index("gx")
    if peers[0] == 2:
        return [(at, 1.0), (1 - at, 1.0)]
    keep_below, keep_above = keeps("gx", peers[0])
    return [(1, 1.0), (0, keep_below), (2, keep_above)]


class Rows:
    def __init__(self, first, second, peers):
        self.refs = first, second
        self.even = lax.axis_index("gy") % 2 == 0
        self.keep = keeps("gy", peers[1])

    def read(self, f, x):
        width, offset = WIDTHS[f], OFFSETS[f]
        a, b = [ref[x, offset : offset + width, :] for ref in self.refs]
        low, high = jnp.where(self.even, b, a), jnp.where(self.even, a, b)
        return low * self.keep[0], high * self.keep[1]


def keeps(axis, peers):
    at = lax.axis_index(axis)
    return jnp.where(at > 0, 1.0, 0.0), jnp.where(at < peers - 1, 1.0, 0.0)


def block_ends(peers, keep, fields, first, second, stage, put):
    _, nx, ny, nz = fields.shape
    tall = ny + 2 * TILE
    pack = LANES // tall
    count = nx // pack
    gap = jnp.zeros((TILE, nz), jnp.float32)
    rows = Rows(first, second, peers)
    for g in range(count):
        for f in range(NF):
            width = WIDTHS[f]
            slot = g * NF + f
            for p in range(pack):
                x = g * pack + p
                top = p * tall
                stage[slot, top : top + TILE, :] = gap
                stage[slot, top + TILE + ny : top + tall, :] = gap
                stage[slot, top + TILE : top + TILE + ny, :] = fields[f, x]
                low, high = rows.read(f, x)
                stage[slot, top + TILE - width : top + TILE, :] = low
                stage[slot, top + TILE + ny : top + TILE + ny + width, :] = high
            begin = stage[slot, :, :LANES].T
            finish = begin if nz == LANES else stage[slot, :, nz - LANES :].T
            if not isinstance(keep, float):
                begin, finish = begin * keep, finish * keep
            put(f, g, begin, finish)


def put_ends(ends, f, g, begin, finish):
    zeros = jnp.zeros((TILE, LANES), jnp.float32)
    inner = SEG - W
    ends[f, g, :TILE, :] = zeros
    ends[f, g, ENDS - TILE :, :] = zeros
    ends[f, g, W:SEG, :] = begin[:inner]
    ends[f, g, SEG : ENDS - W, :] = finish[LANES - inner :]


def put_message(peers, messages, f, g, begin, finish):
    rows = slice(OFFSETS[f], OFFSETS[f] + WIDTHS[f])
    rightward, leftward = finish[LANES - WIDTHS[f] :], begin[: WIDTHS[f]]
    if peers[0] == 2:
        first = lax.axis_index("gx") == 0
        messages[0][g, rows, :] = jnp.where(first, rightward, leftward)
    else:
        messages[0][g, rows, :] = rightward
        messages[1][g, rows, :] = leftward


def pack_own(peers, fields, first, second, ends, *refs):
    *messages, stage = refs

    def put(f, g, begin, finish):
        put_ends(ends, f, g, begin, finish)
        put_message(peers, messages, f, g, begin, finish)

    for message in messages:
        message[:, MSG_ROWS - TILE :, :] = jnp.zeros(
            (message.shape[0], TILE, LANES), jnp.float32
        )
    block_ends(peers, 1.0, fields, first, second, stage, put)


def pack_others(peers, *refs):
    blocks = blocks_of(peers)
    sides = 1 if peers[0] == 2 else 2
    own_ends, own = refs[0], refs[1 : 1 + sides]
    others = refs[1 + sides : 1 + sides + 3 * (len(blocks) - 1)]
    ends, *messages, stage = refs[1 + sides + 3 * (len(blocks) - 1) :]
    count = own_ends.shape[1]
    mine = blocks[0][0] * count
    for g in range(count):
        for f in range(NF):
            ends[f, mine + g] = own_ends[f, g]
        for message, part in zip(messages, own):
            message[mine + g] = part[g]
    for b, (start, keep) in enumerate(blocks[1:]):

        def put(f, g, begin, finish, start=start):
            put_ends(ends, f, start * count + g, begin, finish)
            put_message(peers, messages, f, start * count + g, begin, finish)

        for message in messages:
            for g in range(count):
                message[start * count + g, MSG_ROWS - TILE :, :] = jnp.zeros(
                    (TILE, LANES), jnp.float32
                )
        block_ends(peers, keep, *others[3 * b : 3 * b + 3], stage, put)


def times(value, factor):
    return value if factor == 1.0 else factor * value


def harmonic(a, b):
    return 2.0 * a * b / jnp.maximum(a + b, 1e-30)


def lookup(zone, table, row):
    entries = jnp.broadcast_to(table[row : row + 1, :], zone.shape[:-1] + (LANES,))
    index = zone.astype(jnp.int32)
    picked = [
        jnp.take_along_axis(
            entries, index[:, start : start + LANES], axis=1, mode="promise_in_bounds"
        )
        for start in range(0, zone.shape[1], LANES)
    ]
    return picked[0] if len(picked) == 1 else jnp.concatenate(picked, axis=1)


def fixed_term(zone, lame, shear):
    scale = jnp.maximum(lame + 2.0 * shear / 3.0, 1e-30)
    return jnp.where(zone > 0.0, biot_coef * biot_coef / scale, 0.0)


FIRST_IMAGES, SECOND_IMAGES = (0, 1), (2,)
KEPT = ("motion", "z0", "p0", "zs", "ps")
PASSED = ("heft", "mx", "my", "mz", "react", "tx", "ty", "tz", "pdiag", "ediag", "einv")
ARRAYS = (
    ("zone", 0),
    ("press", 0),
    ("motion", 3),
    ("load", 0),
    ("drain", 0),
    ("body", 3),
    ("perm", 0),
    ("heft", 0),
    ("shear", 0),
    ("fixed", 0),
    ("tx", 0),
    ("ty", 0),
    ("tz", 0),
    ("mx", 0),
    ("my", 0),
    ("mz", 0),
    ("react", 0),
    ("pdiag", 0),
    ("pinv", 0),
    ("z0", 0),
    ("p0", 0),
    ("ediag", 3),
    ("einv", 3),
    ("zs", 9),
    ("ps", 9),
)


class Domain:
    def __init__(self, arrays):
        self.__dict__.update(arrays)

    def press_faces(self, l):
        own = self.perm[l]
        self.tx[l] = harmonic(own, self.nxt(self.perm, l))
        self.ty[l] = harmonic(own, self.yp(own))
        self.tz[l] = harmonic(own, self.zp(own))

    def motion_faces(self, l):
        own = self.shear[l]
        self.mx[l] = harmonic(own, self.nxt(self.shear, l))
        self.my[l] = harmonic(own, self.yp(own))
        self.mz[l] = harmonic(own, self.zp(own))

    def steps(self, ref, l):
        own = ref[l]
        return self.nxt(ref, l) - own, self.yp(own) - own, self.zp(own) - own

    def back_y(self, value):
        return self.ym(value) - value

    def back_z(self, value):
        return self.zm(value) - value

    def press_flux(self, ref, l, along_y=True):
        dx, dy, dz = self.steps(ref, l)
        total = self.back_x(self.tx, dx, ref, l) + self.back_z(self.tz[l] * dz)
        return total + self.back_y(self.ty[l] * dy) if along_y else total

    def y_terms(self, l):
        face = self.ty[l]
        own, middle = self.press[l], self.motion[1, l]
        return (
            face + self.ym(face),
            self.back_y(face * (self.yp(own) - own))
            + (0.5 * biot_coef) * (self.yp(middle) - self.ym(middle)),
        )

    def press_start(self, l):
        face_sum, y_part = self.y_terms(l)
        face = self.tz[l]
        leak = leakage * self.drain[l]
        reaction = storage + self.fixed[l] + leak
        diag = (
            reaction
            + self.tx[l]
            + self.prv(self.tx, l)
            + face_sum
            + (face + self.zm(face))
        )
        inverse = jnp.where(self.zone[l] > 0.0, 1.0 / diag, 0.0)
        along_x, along_z = self.motion.at[0], self.motion[2, l]
        change = (self.nxt(along_x, l) - self.prv(along_x, l)) + (
            self.zp(along_z) - self.zm(along_z)
        )
        residual = (
            self.load[l]
            - (0.5 * biot_coef) * change
            - leak * self.press[l]
            - self.press_flux(self.press, l, False)
            - y_part
        )
        self.react[l] = reaction
        self.pdiag[l] = diag
        self.pinv[l] = inverse
        self.z0[l] = residual * inverse

    def press_next(self, l):
        image = self.react[l] * self.z0[l] + self.press_flux(self.z0, l)
        self.p0[l] = image * self.pinv[l]

    @staticmethod
    def parts(ref, j):
        return [ref.at[3 * j + c] for c in range(3)]

    def elastic(self, refs, l):
        steps = [self.steps(ref, l) for ref in refs]
        pushed = self.heft[l] * (steps[0][0] + steps[1][1] + steps[2][2])
        before = self.push_before(refs, l)
        self.carried = pushed
        out = []
        for c in range(3):
            dx, dy, dz = steps[c]
            step_y, step_z = self.my[l] * dy, self.mz[l] * dz
            if c == 1:
                step_y = step_y + pushed
            if c == 2:
                step_z = step_z + pushed
            push = (before, pushed) if c == 0 else None
            out.append(
                times(refs[c][l], support)
                + self.back_x(self.mx, dx, refs[c], l, push)
                + self.back_y(step_y)
                + self.back_z(step_z)
            )
        return out

    def gradient(self, ref, l):
        own = ref[l]
        return (
            0.5 * (self.nxt(ref, l) - self.prv(ref, l)),
            0.5 * (self.yp(own) - self.ym(own)),
            0.5 * (self.zp(own) - self.zm(own)),
        )

    def motion_start(self, l):
        weight = self.heft[l]
        along_y, along_z = self.my[l], self.mz[l]
        base = (
            support
            + self.mx[l]
            + self.prv(self.mx, l)
            + (along_y + self.ym(along_y))
            + (along_z + self.zm(along_z))
            + weight
        )
        inside = self.zone[l] > 0.0
        beside = (self.prv(self.heft, l), self.ym(weight), self.zm(weight))
        image = self.elastic(self.parts(self.motion, 0), l)
        grads = [self.gradient(ref, l) for ref in (self.press, self.z0, self.p0)]
        for c in range(3):
            diag = base + beside[c]
            inverse = jnp.where(inside, 1.0 / diag, 0.0)
            self.ediag[c, l] = diag
            self.einv[c, l] = inverse
            start = self.body[c, l] - biot_coef * grads[0][c] - image[c]
            self.zs[c, l] = start * inverse
            scale = -biot_coef * inverse
            self.zs[3 + c, l] = grads[1][c] * scale
            self.zs[6 + c, l] = grads[2][c] * scale

    def motion_next(self, l, j):
        image = self.elastic(self.parts(self.zs, j), l)
        for c in range(3):
            self.ps[3 * j + c, l] = image[c] * self.einv[c, l]

    def stages(self):
        self.first_half()
        self.second_half()

    def first_half(self):
        self.run(4, self.press_faces, "faces", 1)
        self.run(4, self.press_start, "start")
        self.run(3, self.press_next, "next")
        self.run(2, self.motion_faces, "shear", 1)
        self.run(2, self.motion_start, "motion")
        for j in FIRST_IMAGES:
            self.images(j)

    def second_half(self):
        for j in SECOND_IMAGES:
            self.images(j)

    def images(self, j):
        self.run(1, lambda l: self.motion_next(l, j), "image")

    def finish(self, l, acc, mask):
        own = self.own

        def add(index, value):
            acc[index] = acc[index] + self.fold(value, mask)

        def total(pairs):
            out = None
            for a, b in pairs:
                out = a * b if out is None else out + a * b
            return out

        a, b = own(self.z0[l]), own(self.p0[l])
        diag = own(self.pdiag[l])
        scaled = diag * b
        add(0, diag * a * a)
        add(1, scaled * a)
        add(2, scaled * b)
        energy = own(self.react[l]) * b * b
        for face, step in zip((self.tx, self.ty, self.tz), self.steps(self.p0, l)):
            step = own(step)
            energy = energy + own(face[l]) * step * step
        add(3, energy)
        diags = [own(self.ediag[c, l]) for c in range(3)]
        faces = [own(ref[l]) for ref in (self.mx, self.my, self.mz)]
        weight = own(self.heft[l])
        za, pa, dz, dp, steps, heavy = [], [], [], [], [], []
        for j in range(3):
            zj, pj = self.parts(self.zs, j), self.parts(self.ps, j)
            za.append([own(ref[l]) for ref in zj])
            pa.append([own(ref[l]) for ref in pj])
            dz.append([d * v for d, v in zip(diags, za[j])])
            dp.append([d * v for d, v in zip(diags, pa[j])])
            moved = [[own(v) for v in self.steps(ref, l)] for ref in pj]
            div = moved[0][0] + moved[1][1] + moved[2][2]
            flat = [(faces[d], moved[c][d]) for c in range(3) for d in range(3)]
            steps.append([v for _, v in flat] + [div] + pa[j])
            heavy.append([f * v for f, v in flat] + [weight * div])
            heavy[j] = heavy[j] + [times(v, support) for v in pa[j]]
        for i, (j, k) in enumerate(PAIRS):
            add(4 + i, total(zip(dz[j], za[k])))
            add(10 + i, total(zip(dp[k], za[j])))
            add(16 + i, total(zip(dp[j], pa[k])))
            add(22 + i, total(zip(heavy[j], steps[k])))

    def loop(self, start, count, body, stage):
        unroll = 1
        if isinstance(count, int):
            unroll = -(-count // -(-count // UNROLL[stage]))
        chunks = count // unroll

        def step(i, carry):
            self.carried = None
            for u in range(unroll):
                body(start + i * unroll + u)
            return carry

        if isinstance(chunks, int) and chunks == 1:
            step(0, 0)
        else:
            lax.fori_loop(0, chunks, step, 0)
            self.carried = None
        if isinstance(count, int):
            for u in range(chunks * unroll, count):
                body(start + u)


class Brick(Domain):
    def nxt(self, ref, l):
        return ref[l + 1]

    def prv(self, ref, l):
        return ref[l - 1]

    def yp(self, v):
        return pltpu.roll(v, v.shape[0] - 1, 0)

    def ym(self, v):
        return pltpu.roll(v, 1, 0)

    def zp(self, v):
        return pltpu.roll(v, v.shape[1] - 1, 1)

    def zm(self, v):
        return pltpu.roll(v, 1, 1)

    def back_x(self, faces, step, ref, l, push=None):
        out = faces[l - 1] * (ref[l] - ref[l - 1]) - faces[l] * step
        if push:
            out = out + (push[0] - push[1])
        return out

    def push_before(self, refs, l):
        if self.carried is not None:
            return self.carried
        a, b, c = refs
        own_b, own_c = b[l - 1], c[l - 1]
        change = (a[l] - a[l - 1]) + (self.yp(own_b) - own_b) + (self.zp(own_c) - own_c)
        return self.heft[l - 1] * change

    def own(self, v):
        return v[: self.ny]

    def fold(self, value, mask):
        total = value[:TILE]
        for start in range(TILE, value.shape[0], TILE):
            total = total + value[start : start + TILE]
        total = jnp.where(mask, total, 0.0)
        folded = total[:, :LANES]
        for start in range(LANES, value.shape[1], LANES):
            folded = folded + total[:, start : start + LANES]
        return folded

    def first(self, halo):
        return W - halo * self.has_below

    def reach(self, halo):
        if self.pair:
            return halo
        return halo * (self.has_below + self.has_above)

    def run(self, halo, body, stage, before=0):
        count = self.nx + self.reach(halo) + before
        self.loop(self.first(halo) - before, count, body, stage)

    def narrow(self, v):
        ny = self.ny
        upper, lower = v[ny : ny + TILE], v[ny + TILE :]
        both = jnp.where(iota(upper.shape, 0) < TILE // 2, upper, lower)
        return jnp.concatenate([v[:ny], both], axis=0)

    def press_faces(self, l):
        own = self.perm[l]
        self.tx[l] = harmonic(own, self.nxt(self.perm, l))
        tall = self.perm_tall[l]
        face = harmonic(tall, self.yp(tall))
        self.ty_tall[l] = face
        self.ty[l] = self.narrow(face)
        self.tz[l] = harmonic(own, self.zp(own))

    def y_terms(self, l):
        face = self.ty_tall[l]
        own, middle = self.tall[PRESS, l], self.tall[MOTION + 1, l]
        return (
            self.narrow(face + self.ym(face)),
            self.narrow(
                self.back_y(face * (self.yp(own) - own))
                + (0.5 * biot_coef) * (self.yp(middle) - self.ym(middle))
            ),
        )

    def assemble(self, l, x, fields, beside, table):
        ny = self.ny
        rows = ny + 2 * TILE
        gap = jnp.zeros((2 * TILE, fields.shape[3]), jnp.float32)
        narrow_rows = ny + TILE
        slim = (self.load, self.drain) + tuple(self.body.at[c] for c in range(3))
        for f in range(NF):
            width = WIDTHS[f]
            below, above = beside.read(f, x)
            if f < WIDE:
                self.tall[f, l, :ny, :] = fields[f, x]
                self.tall[f, l, ny:, :] = gap
                self.tall[f, l, ny : ny + width, :] = above
                self.tall[f, l, rows - width :, :] = below
            else:
                ref = slim[f - WIDE]
                ref[l, :ny, :] = fields[f, x]
                ref[l, ny:, :] = gap[:TILE]
                ref[l, ny : ny + width, :] = above
                ref[l, narrow_rows - width :, :] = below
        tall_zone = self.tall[ZONE, l]
        perm = lookup(tall_zone, table, 0)
        self.perm_tall[l] = perm
        self.perm[l] = self.narrow(perm)
        zone = self.narrow(tall_zone)
        self.zone[l] = zone
        lame, shear = lookup(zone, table, 1), lookup(zone, table, 2)
        self.heft[l] = lame + shear
        self.shear[l] = shear
        self.fixed[l] = fixed_term(zone, lame, shear)
        self.press[l] = self.narrow(self.tall[PRESS, l])
        for c in range(3):
            self.motion[c, l] = self.narrow(self.tall[MOTION + c, l])


def new_brick(peers, nx, ny):
    domain = Brick(dict(nx=nx, ny=ny, pair=peers[0] == 2))
    at = lax.axis_index("gx")
    domain.has_below = (at > 0).astype(jnp.int32)
    domain.has_above = (at < peers[0] - 1).astype(jnp.int32)
    return domain


FIRST_OUTS = ("motion", "z0", "p0", "zs") + PASSED
FIRST_SCRATCH = tuple(n for n, _ in ARRAYS if n not in FIRST_OUTS + ("ps",))


class Joined:
    def __init__(self, *refs):
        self.refs = refs
        self.at = self

    def __getitem__(self, index):
        first, *rest = index if isinstance(index, tuple) else (index,)
        for ref in self.refs:
            if first < ref.shape[0]:
                return ref[first, *rest] if rest else ref.at[first]
            first -= ref.shape[0]

    def __setitem__(self, index, value):
        self[index[0]][index[1:]] = value


def brick_first(peers, *refs):
    table, fields, below, above = refs[:4]
    rows = [Rows(*refs[i : i + 2], peers) for i in (4, 6, 8)]
    outs = refs[10 : 10 + len(FIRST_OUTS)]
    ps, *scratch = refs[10 + len(FIRST_OUTS) :]
    _, nx, ny, nz = fields.shape
    domain = new_brick(peers, nx, ny)
    domain.__dict__.update(zip(FIRST_OUTS, outs))
    domain.__dict__.update(zip(FIRST_SCRATCH, scratch))
    domain.tall, domain.perm_tall, domain.ty_tall = scratch[len(FIRST_SCRATCH) :]
    domain.ps = Joined(ps)

    empty = jnp.zeros((ny + TILE, nz), jnp.float32)
    for l in (W - 1, W + nx):
        for name in ("perm", "heft", "shear", "press", "z0", "p0"):
            getattr(domain, name)[l] = empty
        for c in range(3):
            domain.motion[c, l] = empty
        for i in range(9):
            domain.zs[i, l] = empty
        for i in range(ps.shape[0]):
            ps[i, l] = empty
        domain.perm_tall[l] = jnp.zeros((ny + 2 * TILE, nz), jnp.float32)

    def block(start, count, shift, *source):
        domain.loop(
            start,
            count,
            lambda l: domain.assemble(l, l + shift, *source, table),
            "assemble",
        )

    block(W, nx, -W, fields, rows[0])
    if domain.pair:
        at = lax.axis_index("gx")
        start = jnp.where(at > 0, 0, W + nx)
        shift = jnp.where(at > 0, nx - W, -W - nx)
        block(start, W, shift, below, rows[1])
    else:
        block(0, W * domain.has_below, nx - W, below, rows[1])
        block(W + nx, W * domain.has_above, -W - nx, above, rows[2])
    domain.first_half()


SECOND_INS = ("z0", "p0", "zs") + PASSED


def brick_second(peers, nx, ny, *refs):
    domain = new_brick(peers, nx, ny)
    domain.__dict__.update(zip(SECOND_INS, refs))
    ready, ps, acc = refs[len(SECOND_INS) :]
    domain.ps = Joined(ready, ps)
    nz = ps.shape[3]
    empty = jnp.zeros((ny + TILE, nz), jnp.float32)
    for l in (W - 1, W + nx):
        for i in range(ps.shape[0]):
            ps[i, l] = empty
    domain.second_half()
    acc[...] = jnp.zeros(acc.shape, jnp.float32)
    column = iota((TILE, nz), 1)
    mask = (column >= W) & (column < nz - W)
    domain.loop(W, nx, lambda l: domain.finish(l, acc, mask), "finish")


class Ends(Domain):
    def roll(self, v, shift):
        return pltpu.roll(v, shift % LANES, v.ndim - 1)

    def nxt(self, ref, l):
        moved = self.roll(ref[pl.ds(l.start, l.size + 1)], -self.row)
        lane = iota(moved[1:].shape, 2)
        return jnp.where(lane < LANES - self.row, moved[:-1], moved[1:])

    def before(self, v):
        moved = self.roll(v, self.row)
        back = jnp.concatenate([jnp.zeros_like(moved[:1]), moved[:-1]], axis=0)
        return jnp.where(iota(moved.shape, 2) >= self.row, moved, back)

    def prv(self, ref, l):
        return self.before(ref[l])

    def back_x(self, faces, step, ref, l, push=None):
        value = faces[l] * step
        if push:
            value = value + push[1]
        return self.before(value) - value

    def push_before(self, refs, l):
        return None

    def yp(self, v):
        return self.roll(v, -1)

    def ym(self, v):
        return self.roll(v, 1)

    def zp(self, v):
        return pltpu.roll(v, ENDS - 1, 1)

    def zm(self, v):
        return pltpu.roll(v, 1, 1)

    def own(self, v):
        return v

    def fold(self, value, mask):
        total = None
        for g in range(value.shape[0]):
            part = jnp.where(mask, value[g], 0.0)
            for start in range(0, value.shape[1], TILE):
                piece = part[start : start + TILE]
                total = piece if total is None else total + piece
        return total

    def run(self, halo, body, stage, before=0):
        body(pl.ds(0, self.groups) if halo > 3 else self.near)

    def assemble(self, ends, left, right, keep_left, keep_right, table):
        for g in range(self.groups):
            for f in range(NF):
                width, offset = WIDTHS[f], OFFSETS[f]
                rows = slice(offset, offset + width)
                self.raw[f, g] = ends[f, g]
                self.raw[f, g, W - width : W, :] = left[g, rows, :] * keep_left
                self.raw[f, g, ENDS - W : ENDS - W + width, :] = (
                    right[g, rows, :] * keep_right
                )
            zone = self.raw[ZONE, g]
            lame, shear = lookup(zone, table, 1), lookup(zone, table, 2)
            self.perm[g] = lookup(zone, table, 0)
            self.heft[g] = lame + shear
            self.shear[g] = shear
            self.fixed[g] = fixed_term(zone, lame, shear)


class Either:
    def __init__(self, condition, yes, no):
        self.condition, self.refs = condition, (yes, no)

    def __getitem__(self, index):
        return jnp.where(self.condition, *[ref[index] for ref in self.refs])


def own_groups(count, peers):
    return count * blocks_of(peers)[0][0]


def ends_kernel(peers, tall, *refs):
    table, ends, got, passed, added = refs[:5]
    left, right = got, passed
    if peers[0] == 2:
        first = lax.axis_index("gx") == 0
        left, right = Either(first, got, passed), Either(first, passed, got)
    raw, z0, p0, zs, ps, partial = refs[5:11]
    acc, scratch = refs[11], refs[12:]
    names = [name for name, _ in ARRAYS[6:] if name not in KEPT]
    domain = Ends(dict(zip(names, scratch)))
    domain.raw, domain.z0, domain.p0, domain.zs, domain.ps = raw, z0, p0, zs, ps
    domain.zone, domain.press = raw.at[ZONE], raw.at[PRESS]
    domain.motion = raw.at[MOTION : MOTION + 3]
    domain.load, domain.drain = raw.at[SOURCE], raw.at[DRAIN]
    domain.body = raw.at[BODY : BODY + 3]
    domain.row = tall
    domain.groups = groups = raw.shape[1] - 1
    count = groups // len(blocks_of(peers))
    domain.near = pl.ds(0, groups)
    if peers[0] == 2 and LANES // tall > 3:
        domain.near = pl.ds(lax.axis_index("gx") * (count - 1), count + 1)
    keep = keeps("gz", peers[2])
    empty = jnp.zeros((ENDS, LANES), jnp.float32)
    for ref in (raw, zs, ps):
        for i in range(ref.shape[0]):
            ref[i, groups] = empty
            if ref is not raw:
                ref[i, groups - 1] = empty
    for ref in (domain.perm, domain.shear, z0, p0):
        ref[groups] = empty
    p0[groups - 1] = empty
    mine = own_groups(count, peers)
    domain.assemble(ends, left, right, *keep, table)
    domain.stages()
    acc[...] = added[...]
    shape = (ENDS, LANES)
    column, row = iota(shape, 0), iota(shape, 1) % tall
    at_end = ((column >= W) & (column < 2 * W)) | (
        (column >= ENDS - 2 * W) & (column < ENDS - W)
    )
    mask = at_end & (row >= TILE) & (row < tall - TILE)
    domain.finish(pl.ds(mine, count), acc, mask)

    sums = jnp.concatenate(
        [jnp.sum(acc[i], axis=0, keepdims=True) for i in range(acc.shape[0])], axis=0
    )
    totals = jnp.sum(sums, axis=1, keepdims=True)
    spread = jnp.where(iota(sums.shape, 0) == iota(sums.shape, 1), totals, 0.0)
    line = jnp.sum(spread, axis=0, keepdims=True)
    partial[...] = jnp.broadcast_to(line, partial.shape)


def step_sizes(gamma, delta, cross, energy):
    first = gamma / delta
    gamma_new = gamma - 2.0 * first * delta + first * first * cross
    curved = delta - 2.0 * first * cross + first * first * energy
    ratio = gamma_new / gamma
    second = gamma_new / (curved - ratio * gamma_new / first)
    return first + second * (1.0 + ratio), -first * second


def combine(peers, tall, *refs):
    sums, (old, z0, p0, zs), ps, fields = refs[0], refs[1:5], Joined(*refs[5:7]), refs[7]
    raw, ends_z0, ends_p0, ends_zs, ends_ps = refs[8:13]
    pressure, motion, strain, moved, ends_moved, turned = refs[13:]
    line = jnp.sum(sums[...], axis=0, keepdims=True)
    lane = iota(line.shape, 1)

    def value(index):
        return jnp.sum(jnp.where(lane == index, line, 0.0), axis=1, keepdims=True)

    c1, c2 = step_sizes(*[value(i) for i in range(4)])
    weights = (jnp.ones_like(c1), c1, c2)

    def form(start):
        total = 0.0
        for i, (j, k) in enumerate(PAIRS):
            scale = 1.0 if j == k else 2.0
            total = total + scale * weights[j] * weights[k] * value(start + i)
        return total

    d1, d2 = step_sizes(form(4), form(10), form(16), form(22))
    on_z = [d1 * w for w in weights]
    on_p = [d2 * w for w in weights]

    def new_motion(start, z_part, p_part, c, i):
        total = start
        for j in range(3):
            total = total + on_z[j] * z_part[3 * j + c, i]
            total = total + on_p[j] * p_part[3 * j + c, i]
        return total

    nx, ny, nz = pressure.shape
    pack = LANES // tall
    ends = Ends(dict(row=tall))
    groups = raw.shape[1] - 1
    count = groups // len(blocks_of(peers))
    mine = own_groups(count, peers)
    every = pl.ds(0, groups)
    if peers[0] == 2 and pack > 3:
        every = pl.ds(lax.axis_index("gx") * (count - 1), count + 1)
    for c in range(3):
        for i in range(every.size):
            g = every.start + i
            ends_moved[c, g] = new_motion(raw[MOTION + c, g], ends_zs, ends_ps, c, g)
        ends_moved[c, every.start + every.size] = jnp.zeros((ENDS, LANES), jnp.float32)
    along_y, along_z = ends_moved[1, every], ends_moved[2, every]
    first = ends_moved.at[0]
    ends_moved[3, every] = 0.5 * (
        (ends.nxt(first, every) - ends.prv(first, every))
        + (ends.yp(along_y) - ends.ym(along_y))
        + (ends.zp(along_z) - ends.zm(along_z))
    )
    for c in range(3):
        around = 1 if c == 0 else 0
        for l in range(W - around, W + nx + around):
            moved[c, l] = new_motion(old[c, l], zs, ps, c, l)
    brick = Brick({})
    outs = [pressure] + [motion.at[c] for c in range(3)] + [strain]
    for g in range(count):
        at = mine + g
        edges = [raw[PRESS, at] + c1 * ends_z0[at] + c2 * ends_p0[at]]
        edges = edges + [ends_moved[c, at] for c in range(4)]
        flipped = []
        for o, edge in enumerate(edges):
            slot = g * len(outs) + o
            turned[slot, :W, :] = edge[W : 2 * W]
            turned[slot, LANES - W :, :] = edge[ENDS - 2 * W : ENDS - W]
            flipped.append(turned[slot].T)
        for i in range(pack):
            x = g * pack + i
            l = W + x
            top = i * tall + TILE
            column = iota((ny, LANES), 1)
            u = [moved[c, l] for c in range(3)]
            change = (
                (moved[0, l + 1] - moved[0, l - 1])
                + (brick.yp(u[1]) - brick.ym(u[1]))
                + (brick.zp(u[2]) - brick.zm(u[2]))
            )
            results = [fields[PRESS, x] + c1 * z0[l, :ny, :] + c2 * p0[l, :ny, :]]
            results = results + [v[:ny] for v in u] + [0.5 * change[:ny]]
            for out, result, edge in zip(outs, results, flipped):
                edge = edge[top : top + ny]
                if nz == LANES:
                    inner = (column >= W) & (column < LANES - W)
                    out[x] = jnp.where(inner, result, edge)
                else:
                    out[x] = result
                    out[x, :, :LANES] = jnp.where(column >= W, result[:, :LANES], edge)
                    out[x, :, nz - LANES :] = jnp.where(
                        column < LANES - W, result[:, nz - LANES :], edge
                    )


def f32(*shape):
    return jax.ShapeDtypeStruct(shape, jnp.float32)


def vmem(*shape):
    return pltpu.VMEM(shape, jnp.float32)


def call(kernel, outs, *args, unread=0, space=pltpu.VMEM, scratch=(), limit=8, cost=None):
    specs = [
        pl.BlockSpec(memory_space=space if i < len(args) - unread else pl.ANY)
        for i in range(len(args))
    ]
    return pl.pallas_call(
        kernel,
        out_shape=outs,
        in_specs=specs,
        scratch_shapes=scratch,
        cost_estimate=cost,
        compiler_params=pltpu.CompilerParams(vmem_limit_bytes=limit * MIB),
    )(*args)


def ring(value, axis, step):
    peers = lax.axis_size(axis)
    return lax.ppermute(value, axis, [(i, (i + step) % peers) for i in range(peers)])


def pairs(value, axis, start):
    peers = lax.axis_size(axis)
    swaps = [(i, i) for i in range(start)]
    for i in range(start, peers - 1, 2):
        swaps += [(i, i + 1), (i + 1, i)]
    swaps += [(i, i) for i in range(len(swaps), peers)]
    return lax.ppermute(value, axis, swaps)


def x_neighbours(value):
    peers = lax.axis_size("gx")
    above = ring(value, "gx", -1)
    below = above if peers == 2 else ring(value, "gx", 1)
    return below, above


def shards(
    source,
    pressure_old,
    strain_prev,
    motion_old,
    body_force,
    zone_ids,
    drained,
    perm_table,
    lame_table,
    shear_table,
):
    nx, ny, nz = source.shape
    peers = [lax.axis_size(a) for a in AXES]
    total = peers[0] * peers[1] * peers[2]
    pair = peers[0] == 2
    tall = ny + 2 * TILE
    groups = nx * tall // LANES

    def with_peers(kernel, *more):
        return lambda *refs: kernel(peers, *more, *refs)

    raw = (
        source,
        pressure_old,
        strain_prev,
        motion_old,
        body_force,
        zone_ids,
        drained,
    )
    raw = [pltpu.with_memory_space_constraint(a, pltpu.HBM) for a in raw]
    held = [pltpu.VMEM(a.shape, a.dtype) for a in raw]
    tables = [
        pltpu.with_memory_space_constraint(a, pltpu.HBM)
        for a in (perm_table, lame_table, shear_table)
    ]
    message = f32(nx, MSG_ROWS, nz)
    first, second, table = call(
        pack_rows,
        [message, message, f32(TILE, LANES)],
        *raw,
        *tables,
        space=pltpu.HBM,
        scratch=held
        + [pltpu.SMEM(a.shape, a.dtype) for a in tables]
        + [pltpu.SemaphoreType.DMA((len(raw) + len(tables),))],
    )
    (fields,) = call(
        pack_fields,
        [f32(NF, nx, ny, nz)],
        *raw,
        table,
        space=pltpu.HBM,
        unread=1,
        scratch=held + [pltpu.SemaphoreType.DMA((len(raw),))],
    )
    fields_below, fields_above = x_neighbours(fields)
    first = pairs(first, "gy", 0)
    second = pairs(second, "gy", 1)
    first_below, first_above = x_neighbours(first)
    second_below, second_above = x_neighbours(second)
    others = [
        (fields_below, first_below, second_below),
        (fields_above, first_above, second_above),
    ][: 1 if pair else 2]
    sides = 1 if pair else 2
    own_ends, *own_messages = call(
        with_peers(pack_own),
        [f32(NF, groups, ENDS, LANES)] + [f32(groups, MSG_ROWS, LANES)] * sides,
        fields,
        first,
        second,
        scratch=[vmem(NF * groups, LANES, nz)],
    )
    span = (1 + len(others)) * groups
    ends, *messages = call(
        with_peers(pack_others),
        [f32(NF, span, ENDS, LANES)] + [f32(span, MSG_ROWS, LANES)] * sides,
        own_ends,
        *own_messages,
        *[array for block in others for array in block],
        scratch=[vmem(NF * groups, LANES, nz)],
        limit=12,
    )
    if pair:
        n = peers[2]
        hops = [(i, (i + 1) % n) for i in range(n)]
        hops += [(n + i, n + (i - 1) % n) for i in range(n)]
        got = lax.ppermute(messages[0], ("gx", "gz"), hops)
    else:
        got, passed = ring(messages[0], "gz", 1), ring(messages[1], "gz", -1)
    depth = nx + 2 * W
    cells = depth * ny * nz

    def shaped(lead, *shape):
        return (lead,) * (lead > 0) + shape

    leads = dict(ARRAYS)
    sums_shape = (up_to(SUMS, TILE), TILE, LANES)

    def layers_of(name):
        return shaped(leads[name], depth, ny + TILE, nz)

    *halves, ps = call(
        with_peers(brick_first),
        [f32(*layers_of(name)) for name in FIRST_OUTS]
        + [f32(3 * len(FIRST_IMAGES), depth, ny + TILE, nz)],
        table,
        fields,
        fields_below,
        fields_above,
        first,
        second,
        first_below,
        second_below,
        first_above,
        second_above,
        scratch=[vmem(*layers_of(name)) for name in FIRST_SCRATCH]
        + [vmem(WIDE, depth, tall, nz), vmem(depth, tall, nz), vmem(depth, tall, nz)],
        limit=16,
    )
    half = dict(zip(FIRST_OUTS, halves))
    if pair:
        passed = ring(got, "gx", -1)
    last, added = call(
        with_peers(brick_second, nx, ny),
        [f32(3 * len(SECOND_IMAGES), depth, ny + TILE, nz), f32(*sums_shape)],
        *[half[name] for name in SECOND_INS],
        ps,
    )
    kept = [half[name] for name in KEPT[:-1]] + [ps, last]
    span = span + 1
    *ends_kept, partial = call(
        with_peers(ends_kernel, tall),
        [f32(NF, span, ENDS, LANES)]
        + [f32(*shaped(leads[name], span, ENDS, LANES)) for name in KEPT[1:]]
        + [f32(total, LANES)],
        table,
        ends,
        got,
        passed,
        added,
        scratch=[vmem(*sums_shape)]
        + [
            vmem(*shaped(lead, span, ENDS, LANES))
            for name, lead in ARRAYS[6:]
            if name not in KEPT
        ],
        limit=16,
    )
    sums = lax.all_to_all(partial, AXES, 0, 0, tiled=True)
    return tuple(
        call(
            with_peers(combine, tall),
            [f32(nx, ny, nz), f32(3, nx, ny, nz), f32(nx, ny, nz)],
            sums,
            *kept,
            fields,
            *ends_kept,
            scratch=[
                vmem(3, depth, ny + TILE, nz),
                vmem(4, span, ENDS, LANES),
                vmem(5 * groups, LANES, LANES),
            ],
            limit=16,
        )
    )


def solution(mesh):
    placed = (
        P("gx", "gy", "gz"),
        P("gx", "gy", "gz"),
        P("gx", "gy", "gz"),
        P(None, "gx", "gy", "gz"),
        P(None, "gx", "gy", "gz"),
        P("gx", "gy", "gz"),
        P("gx", "gy", "gz"),
        P(),
        P(),
        P(),
    )
    return jax.shard_map(
        shards,
        mesh=mesh,
        in_specs=placed,
        out_specs=(P("gx", "gy", "gz"), P(None, "gx", "gy", "gz"), P("gx", "gy", "gz")),
        check_vma=False,
    )
```

```python
import jax
import jax.numpy as jnp
from jax import lax
from jax.experimental import pallas as pl
from jax.experimental.pallas import tpu as pltpu
from jax.sharding import PartitionSpec as P


ZONES = 8

storage = 0.2
biot_coef = 0.8
leakage = 2.0
support = 1.0

AXES = ("gx", "gy", "gz")
LANES = 128
TILE = 8
MIB = 2**20

ZONE, PRESS, MOTION, SOURCE, DRAIN, BODY = 0, 1, 2, 5, 6, 7
WIDTHS = (5, 5, 5, 5, 5, 4, 4, 2, 2, 2)
NF = len(WIDTHS)
W = max(WIDTHS)
OFFSETS = tuple(sum(WIDTHS[:f]) for f in range(NF))
ROW_WIDTHS = (5, 4, 4, 3, 4, 4, 4, 2, 2, 2)
ROW_OFFSETS = tuple(sum(ROW_WIDTHS[:f]) for f in range(NF))
ROWS_EACH = sum(ROW_WIDTHS)
PAIRS = tuple((j, k) for j in range(3) for k in range(j, 3))
SUMS = 4 + 4 * len(PAIRS)
SEG = 16
ENDS = 2 * SEG
UNROLL = dict(faces=8, start=8, next=8, shear=8, motion=8, image=8, finish=8)


def up_to(value, multiple):
    return -(-value // multiple) * multiple


MSG_ROWS = up_to(sum(WIDTHS), TILE)


def iota(shape, dim):
    return lax.broadcasted_iota(jnp.int32, shape, dim)


def field_of(raw, f, at):
    source, pressure, strain, motion, body, zones, drained = raw
    if f == ZONE:
        return zones[at].astype(jnp.float32) + 1.0
    if f == PRESS:
        return pressure[at]
    if f == SOURCE:
        return source[at] + biot_coef * strain[at]
    if f == DRAIN:
        return drained[at].astype(jnp.float32)
    return motion[f - MOTION, *at] if f < SOURCE else body[f - BODY, *at]


class Fetch:
    def __init__(self, sources, held, arrived):
        self.held = held
        self.copies = [
            pltpu.make_async_copy(source, copy, arrived.at[i])
            for i, (source, copy) in enumerate(zip(sources, held))
        ]
        self.waiting = set(range(len(held)))
        for i in sorted(self.waiting, key=lambda i: FETCH_ORDER.index(i)):
            self.copies[i].start()

    def need(self, *which):
        for i in which:
            if i in self.waiting:
                self.waiting.remove(i)
                self.copies[i].wait()


FETCH_ORDER = (5, 1, 3, 0, 2, 6, 4, 7, 8, 9)
NEEDS = ((5,), (1,), (3,), (3,), (3,), (0, 2), (6,), (4,), (4,), (4,))


def pack_rows(*refs):
    sources, (first, second, table), held, arrived = refs[:10], refs[10:13], refs[13:23], refs[23]
    fetch = Fetch(sources, held, arrived)
    raw, tables = held[:7], held[7:]
    nx, ny, nz = raw[0].shape
    even = lax.axis_index("gy") % 2 == 0
    fetch.need(7, 8, 9)
    shape = (TILE, LANES)
    tile = jnp.zeros(shape, jnp.float32)
    for t in range(len(tables)):
        for zone in range(ZONES):
            here = (iota(shape, 0) == t) & (iota(shape, 1) == zone + 1)
            tile = jnp.where(here, tables[t][zone], tile)
    table[...] = tile
    inner = iota((ny, nz), 0) < ny - 1
    for f in range(NF):
        width = ROW_WIDTHS[f]
        fetch.need(*NEEDS[f])
        for x in range(nx):
            at = (x, slice(None))
            value = field_of(raw, f, at)
            if f == SOURCE:
                zone, press, middle = [field_of(raw, g, at) for g in (ZONE, PRESS, MOTION + 1)]
                perm = lookup(zone, tile, 0)
                face = jnp.where(inner, harmonic(perm, rows_up(perm)), 0.0)
                value = value - y_part(face, press, middle, inner)
            upward, downward = value[ny - width :], value[:width]
            start = x * ROWS_EACH + ROW_OFFSETS[f]
            first[start : start + width, :] = jnp.where(even, upward, downward)
            second[start : start + width, :] = jnp.where(even, downward, upward)
    used = nx * ROWS_EACH
    for ref in (first, second):
        if ref.shape[0] > used:
            ref[used:, :] = jnp.zeros((ref.shape[0] - used, nz), jnp.float32)


def rows_up(v):
    return pltpu.roll(v, v.shape[0] - 1, 0)


def rows_down(v):
    return pltpu.roll(v, 1, 0)


def y_part(face, press, middle, marked, up=rows_up, down=rows_down):
    step = jnp.where(marked, face * (up(press) - press), 0.0)
    change = jnp.where(marked, up(middle), 0.0) - down(jnp.where(marked, middle, 0.0))
    return (down(step) - step) + (0.5 * biot_coef) * change


def pack_fields(*refs):
    sources, fields, held, arrived = refs[:7], refs[8], refs[9:16], refs[16]
    fetch = Fetch(sources, held, arrived)
    for f in range(NF):
        fetch.need(*NEEDS[f])
        for x in range(fields.shape[1]):
            fields[f, x] = field_of(held, f, (x, slice(None)))


def keeps(axis, peers):
    at = lax.axis_index(axis)
    return jnp.where(at > 0, 1.0, 0.0), jnp.where(at < peers - 1, 1.0, 0.0)


def blocks_of(peers):
    at = lax.axis_index("gx")
    if peers[0] == 2:
        return [(at, 1.0), (1 - at, 1.0)]
    keep_below, keep_above = keeps("gx", peers[0])
    return [(1, 1.0), (0, keep_below), (2, keep_above)]


class Rows:
    def __init__(self, first, second, peers):
        self.refs = first, second
        self.even = lax.axis_index("gy") % 2 == 0
        self.keep = keeps("gy", peers[1])

    def read(self, f, x):
        start = x * ROWS_EACH + ROW_OFFSETS[f]
        a, b = [ref[start : start + ROW_WIDTHS[f], :] for ref in self.refs]
        low, high = jnp.where(self.even, b, a), jnp.where(self.even, a, b)
        return low * self.keep[0], high * self.keep[1]


def keeps(axis, peers):
    at = lax.axis_index(axis)
    return jnp.where(at > 0, 1.0, 0.0), jnp.where(at < peers - 1, 1.0, 0.0)


def block_ends(peers, keep, fields, first, second, stage, put):
    _, nx, ny, nz = fields.shape
    tall = ny + 2 * TILE
    pack = LANES // tall
    count = nx // pack
    gap = jnp.zeros((TILE, nz), jnp.float32)
    rows = Rows(first, second, peers)
    for g in range(count):
        for f in range(NF):
            width = ROW_WIDTHS[f]
            slot = g * NF + f
            for p in range(pack):
                x = g * pack + p
                top = p * tall
                stage[slot, top : top + TILE, :] = gap
                stage[slot, top + TILE + ny : top + tall, :] = gap
                stage[slot, top + TILE : top + TILE + ny, :] = fields[f, x]
                low, high = rows.read(f, x)
                stage[slot, top + TILE - width : top + TILE, :] = low
                stage[slot, top + TILE + ny : top + TILE + ny + width, :] = high
            begin = stage[slot, :, :LANES].T
            finish = begin if nz == LANES else stage[slot, :, nz - LANES :].T
            if not isinstance(keep, float):
                begin, finish = begin * keep, finish * keep
            put(f, g, begin, finish)


def put_ends(ends, f, g, begin, finish):
    zeros = jnp.zeros((TILE, LANES), jnp.float32)
    inner = SEG - W
    ends[f, g, :TILE, :] = zeros
    ends[f, g, ENDS - TILE :, :] = zeros
    ends[f, g, W:SEG, :] = begin[:inner]
    ends[f, g, SEG : ENDS - W, :] = finish[LANES - inner :]


def put_message(peers, messages, f, g, begin, finish):
    rows = slice(OFFSETS[f], OFFSETS[f] + WIDTHS[f])
    rightward, leftward = finish[LANES - WIDTHS[f] :], begin[: WIDTHS[f]]
    if peers[0] == 2:
        first = lax.axis_index("gx") == 0
        messages[0][g, rows, :] = jnp.where(first, rightward, leftward)
    else:
        messages[0][g, rows, :] = rightward
        messages[1][g, rows, :] = leftward


def pack_own(peers, fields, first, second, ends, *refs):
    *messages, stage = refs

    def put(f, g, begin, finish):
        put_ends(ends, f, g, begin, finish)
        put_message(peers, messages, f, g, begin, finish)

    for message in messages:
        message[:, MSG_ROWS - TILE :, :] = jnp.zeros(
            (message.shape[0], TILE, LANES), jnp.float32
        )
    block_ends(peers, 1.0, fields, first, second, stage, put)


def pack_others(peers, *refs):
    blocks = blocks_of(peers)
    sides = 1 if peers[0] == 2 else 2
    own_ends, own = refs[0], refs[1 : 1 + sides]
    others = refs[1 + sides : 1 + sides + 3 * (len(blocks) - 1)]
    ends, *messages, stage = refs[1 + sides + 3 * (len(blocks) - 1) :]
    count = own_ends.shape[1]
    mine = blocks[0][0] * count
    for g in range(count):
        for f in range(NF):
            ends[f, mine + g] = own_ends[f, g]
        for message, part in zip(messages, own):
            message[mine + g] = part[g]
    for b, (start, keep) in enumerate(blocks[1:]):

        def put(f, g, begin, finish, start=start):
            put_ends(ends, f, start * count + g, begin, finish)
            put_message(peers, messages, f, start * count + g, begin, finish)

        for message in messages:
            for g in range(count):
                message[start * count + g, MSG_ROWS - TILE :, :] = jnp.zeros(
                    (TILE, LANES), jnp.float32
                )
        block_ends(peers, keep, *others[3 * b : 3 * b + 3], stage, put)


def times(value, factor):
    return value if factor == 1.0 else factor * value


def harmonic(a, b):
    return 2.0 * a * b / jnp.maximum(a + b, 1e-30)


def lookup(zone, table, row):
    entries = jnp.broadcast_to(table[row : row + 1, :], zone.shape[:-1] + (LANES,))
    index = zone.astype(jnp.int32)
    picked = [
        jnp.take_along_axis(
            entries, index[:, start : start + LANES], axis=1, mode="promise_in_bounds"
        )
        for start in range(0, zone.shape[1], LANES)
    ]
    return picked[0] if len(picked) == 1 else jnp.concatenate(picked, axis=1)


def fixed_term(zone, lame, shear):
    scale = jnp.maximum(lame + 2.0 * shear / 3.0, 1e-30)
    return jnp.where(zone > 0.0, biot_coef * biot_coef / scale, 0.0)


FIRST_IMAGES, SECOND_IMAGES = (0, 1), (2,)
KEPT = ("motion", "z0", "p0", "zs", "ps")
PASSED = ("heft", "mx", "my", "mz", "react", "tx", "ty", "tz", "pdiag", "ediag", "einv")
ARRAYS = (
    ("zone", 0),
    ("press", 0),
    ("motion", 3),
    ("load", 0),
    ("drain", 0),
    ("body", 3),
    ("perm", 0),
    ("heft", 0),
    ("shear", 0),
    ("fixed", 0),
    ("tx", 0),
    ("ty", 0),
    ("tz", 0),
    ("mx", 0),
    ("my", 0),
    ("mz", 0),
    ("react", 0),
    ("pdiag", 0),
    ("pinv", 0),
    ("z0", 0),
    ("p0", 0),
    ("ediag", 3),
    ("einv", 3),
    ("zs", 9),
    ("ps", 9),
)


class Domain:
    def __init__(self, arrays):
        self.__dict__.update(arrays)

    def press_faces(self, l):
        own = self.perm[l]
        self.tx[l] = harmonic(own, self.nxt(self.perm, l))
        self.ty[l] = harmonic(own, self.yp(own))
        self.tz[l] = harmonic(own, self.zp(own))

    def motion_faces(self, l):
        own = self.shear[l]
        self.mx[l] = harmonic(own, self.nxt(self.shear, l))
        self.my[l] = harmonic(own, self.yp(own))
        self.mz[l] = harmonic(own, self.zp(own))

    def steps(self, ref, l):
        own = ref[l]
        return self.nxt(ref, l) - own, self.yp(own) - own, self.zp(own) - own

    def back_y(self, value):
        return self.ym(value) - value

    def back_z(self, value):
        return self.zm(value) - value

    def press_flux(self, ref, l, along_y=True):
        dx, dy, dz = self.steps(ref, l)
        total = self.back_x(self.tx, dx, ref, l) + self.back_z(self.tz[l] * dz)
        return total + self.back_y(self.ty[l] * dy) if along_y else total

    def y_terms(self, l):
        face = self.ty[l]
        marked = self.near_faces(face.shape)
        part = y_part(face, self.press[l], self.motion[1, l], marked, self.yp, self.ym)
        return self.y_sum(l), part

    def press_start(self, l):
        face_sum, y_part = self.y_terms(l)
        face = self.tz[l]
        leak = leakage * self.drain[l]
        reaction = storage + self.fixed[l] + leak
        diag = (
            reaction
            + self.tx[l]
            + self.prv(self.tx, l)
            + face_sum
            + (face + self.zm(face))
        )
        inverse = jnp.where(self.zone[l] > 0.0, 1.0 / diag, 0.0)
        along_x, along_z = self.motion.at[0], self.motion[2, l]
        change = (self.nxt(along_x, l) - self.prv(along_x, l)) + (
            self.zp(along_z) - self.zm(along_z)
        )
        residual = (
            self.load[l]
            - (0.5 * biot_coef) * change
            - leak * self.press[l]
            - self.press_flux(self.press, l, False)
            - y_part
        )
        self.react[l] = reaction
        self.pdiag[l] = diag
        self.pinv[l] = inverse
        self.z0[l] = residual * inverse

    def press_next(self, l):
        image = self.react[l] * self.z0[l] + self.press_flux(self.z0, l)
        self.p0[l] = image * self.pinv[l]

    @staticmethod
    def parts(ref, j):
        return [ref.at[3 * j + c] for c in range(3)]

    def elastic(self, refs, l):
        steps = [self.steps(ref, l) for ref in refs]
        pushed = self.heft[l] * (steps[0][0] + steps[1][1] + steps[2][2])
        before = self.push_before(refs, l)
        self.carried = pushed
        out = []
        for c in range(3):
            dx, dy, dz = steps[c]
            step_y, step_z = self.my[l] * dy, self.mz[l] * dz
            if c == 1:
                step_y = step_y + pushed
            if c == 2:
                step_z = step_z + pushed
            push = (before, pushed) if c == 0 else None
            out.append(
                times(refs[c][l], support)
                + self.back_x(self.mx, dx, refs[c], l, push)
                + self.back_y(step_y)
                + self.back_z(step_z)
            )
        return out

    def gradient(self, ref, l):
        own = ref[l]
        return (
            0.5 * (self.nxt(ref, l) - self.prv(ref, l)),
            0.5 * (self.yp(own) - self.ym(own)),
            0.5 * (self.zp(own) - self.zm(own)),
        )

    def motion_start(self, l):
        weight = self.heft[l]
        along_y, along_z = self.my[l], self.mz[l]
        base = (
            support
            + self.mx[l]
            + self.prv(self.mx, l)
            + (along_y + self.ym(along_y))
            + (along_z + self.zm(along_z))
            + weight
        )
        inside = self.zone[l] > 0.0
        beside = (self.prv(self.heft, l), self.ym(weight), self.zm(weight))
        image = self.elastic(self.parts(self.motion, 0), l)
        grads = [self.gradient(ref, l) for ref in (self.press, self.z0, self.p0)]
        for c in range(3):
            diag = base + beside[c]
            inverse = jnp.where(inside, 1.0 / diag, 0.0)
            self.ediag[c, l] = diag
            self.einv[c, l] = inverse
            start = self.body[c, l] - biot_coef * grads[0][c] - image[c]
            self.zs[c, l] = start * inverse
            scale = -biot_coef * inverse
            self.zs[3 + c, l] = grads[1][c] * scale
            self.zs[6 + c, l] = grads[2][c] * scale

    def motion_next(self, l, j):
        image = self.elastic(self.parts(self.zs, j), l)
        for c in range(3):
            self.ps[3 * j + c, l] = image[c] * self.einv[c, l]

    def stages(self):
        self.first_half()
        self.second_half()

    def first_half(self):
        self.run(4, self.press_faces, "faces", 1)
        self.run(4, self.press_start, "start")
        self.run(3, self.press_next, "next")
        self.run(2, self.motion_faces, "shear", 1)
        self.run(2, self.motion_start, "motion")
        for j in FIRST_IMAGES:
            self.images(j)

    def second_half(self):
        for j in SECOND_IMAGES:
            self.images(j)

    def images(self, j):
        self.run(1, lambda l: self.motion_next(l, j), "image")

    def finish(self, l, acc, mask):
        own = self.own

        def add(index, value):
            acc[index] = acc[index] + self.fold(value, mask)

        def total(pairs):
            out = None
            for a, b in pairs:
                out = a * b if out is None else out + a * b
            return out

        a, b = own(self.z0[l]), own(self.p0[l])
        diag = own(self.pdiag[l])
        scaled = diag * b
        add(0, diag * a * a)
        add(1, scaled * a)
        add(2, scaled * b)
        energy = own(self.react[l]) * b * b
        for face, step in zip((self.tx, self.ty, self.tz), self.steps(self.p0, l)):
            step = own(step)
            energy = energy + own(face[l]) * step * step
        add(3, energy)
        diags = [own(self.ediag[c, l]) for c in range(3)]
        faces = [own(ref[l]) for ref in (self.mx, self.my, self.mz)]
        weight = own(self.heft[l])
        za, pa, dz, dp, steps, heavy = [], [], [], [], [], []
        for j in range(3):
            zj, pj = self.parts(self.zs, j), self.parts(self.ps, j)
            za.append([own(ref[l]) for ref in zj])
            pa.append([own(ref[l]) for ref in pj])
            dz.append([d * v for d, v in zip(diags, za[j])])
            dp.append([d * v for d, v in zip(diags, pa[j])])
            moved = [[own(v) for v in self.steps(ref, l)] for ref in pj]
            div = moved[0][0] + moved[1][1] + moved[2][2]
            flat = [(faces[d], moved[c][d]) for c in range(3) for d in range(3)]
            steps.append([v for _, v in flat] + [div] + pa[j])
            heavy.append([f * v for f, v in flat] + [weight * div])
            heavy[j] = heavy[j] + [times(v, support) for v in pa[j]]
        for i, (j, k) in enumerate(PAIRS):
            add(4 + i, total(zip(dz[j], za[k])))
            add(10 + i, total(zip(dp[k], za[j])))
            add(16 + i, total(zip(dp[j], pa[k])))
            add(22 + i, total(zip(heavy[j], steps[k])))

    def loop(self, start, count, body, stage):
        unroll = 1
        if isinstance(count, int):
            unroll = -(-count // -(-count // UNROLL[stage]))
        chunks = count // unroll

        def step(i, carry):
            self.carried = None
            for u in range(unroll):
                body(start + i * unroll + u)
            return carry

        if isinstance(chunks, int) and chunks == 1:
            step(0, 0)
        else:
            lax.fori_loop(0, chunks, step, 0)
            self.carried = None
        if isinstance(count, int):
            for u in range(chunks * unroll, count):
                body(start + u)


class Brick(Domain):
    def nxt(self, ref, l):
        return ref[l + 1]

    def prv(self, ref, l):
        return ref[l - 1]

    def yp(self, v):
        return pltpu.roll(v, v.shape[0] - 1, 0)

    def ym(self, v):
        return pltpu.roll(v, 1, 0)

    def zp(self, v):
        return pltpu.roll(v, v.shape[1] - 1, 1)

    def zm(self, v):
        return pltpu.roll(v, 1, 1)

    def back_x(self, faces, step, ref, l, push=None):
        out = faces[l - 1] * (ref[l] - ref[l - 1]) - faces[l] * step
        if push:
            out = out + (push[0] - push[1])
        return out

    def push_before(self, refs, l):
        if self.carried is not None:
            return self.carried
        a, b, c = refs
        own_b, own_c = b[l - 1], c[l - 1]
        change = (a[l] - a[l - 1]) + (self.yp(own_b) - own_b) + (self.zp(own_c) - own_c)
        return self.heft[l - 1] * change

    def own(self, v):
        return v[: self.ny]

    def fold(self, value, mask):
        total = value[:TILE]
        for start in range(TILE, value.shape[0], TILE):
            total = total + value[start : start + TILE]
        total = jnp.where(mask, total, 0.0)
        folded = total[:, :LANES]
        for start in range(LANES, value.shape[1], LANES):
            folded = folded + total[:, start : start + LANES]
        return folded

    def first(self, halo):
        return W - halo * self.has_below

    def reach(self, halo):
        if self.pair:
            return halo
        return halo * (self.has_below + self.has_above)

    def run(self, halo, body, stage, before=0):
        count = self.nx + self.reach(halo) + before
        self.loop(self.first(halo) - before, count, body, stage)

    def narrow(self, v):
        ny = self.ny
        upper, lower = v[ny : ny + TILE], v[ny + TILE :]
        both = jnp.where(iota(upper.shape, 0) < TILE // 2, upper, lower)
        return jnp.concatenate([v[:ny], both], axis=0)

    def press_faces(self, l):
        own = self.perm[l]
        self.tx[l] = harmonic(own, self.nxt(self.perm, l))
        tall = self.perm_tall[l]
        face = harmonic(tall, self.yp(tall))
        self.ty[l] = self.narrow(face)
        self.face_sum[l] = self.narrow(face + self.ym(face))
        self.tz[l] = harmonic(own, self.zp(own))

    def y_sum(self, l):
        return self.face_sum[l]

    def near_faces(self, shape):
        row = iota(shape, 0)
        return (row < self.ny) | (row == shape[0] - 1)

    def assemble(self, l, x, fields, beside, table, keep=None):
        ny = self.ny
        gap = jnp.zeros((2 * TILE, fields.shape[3]), jnp.float32)
        refs = [self.zone_tall, self.press] + [self.motion.at[c] for c in range(3)]
        refs += [self.load, self.drain] + [self.body.at[c] for c in range(3)]
        for f, ref in enumerate(refs):
            width, rows = ROW_WIDTHS[f], ref.shape[1]
            below, above = beside(f)
            middle = fields[f, x]
            if keep is not None:
                below, above, middle = below * keep, above * keep, middle * keep
            ref[l, :ny, :] = middle
            ref[l, ny:, :] = gap[: rows - ny]
            ref[l, ny : ny + width, :] = above
            ref[l, rows - width :, :] = below
        tall_zone = self.zone_tall[l]
        perm = lookup(tall_zone, table, 0)
        self.perm_tall[l] = perm
        self.perm[l] = self.narrow(perm)
        zone = self.narrow(tall_zone)
        self.zone[l] = zone
        lame, shear = lookup(zone, table, 1), lookup(zone, table, 2)
        self.heft[l] = lame + shear
        self.shear[l] = shear
        self.fixed[l] = fixed_term(zone, lame, shear)


def new_brick(peers, nx, ny):
    domain = Brick(dict(nx=nx, ny=ny, pair=peers[0] == 2))
    at = lax.axis_index("gx")
    domain.has_below = (at > 0).astype(jnp.int32)
    domain.has_above = (at < peers[0] - 1).astype(jnp.int32)
    return domain


FIRST_OUTS = ("motion", "z0", "p0", "zs") + PASSED
FIRST_SCRATCH = tuple(n for n, _ in ARRAYS if n not in FIRST_OUTS + ("ps",))


class Joined:
    def __init__(self, *refs):
        self.refs = refs
        self.at = self

    def __getitem__(self, index):
        first, *rest = index if isinstance(index, tuple) else (index,)
        for ref in self.refs:
            if first < ref.shape[0]:
                return ref[first, *rest] if rest else ref.at[first]
            first -= ref.shape[0]

    def __setitem__(self, index, value):
        self[index[0]][index[1:]] = value


def brick_first(peers, *refs):
    table, fields, below, above = refs[:4]
    rows = [Rows(*refs[i : i + 2], peers) for i in (4, 6, 8)]
    outs = refs[10 : 10 + len(FIRST_OUTS)]
    ps, *scratch = refs[10 + len(FIRST_OUTS) :]
    _, nx, ny, nz = fields.shape
    domain = new_brick(peers, nx, ny)
    domain.__dict__.update(zip(FIRST_OUTS, outs))
    domain.__dict__.update(zip(FIRST_SCRATCH, scratch))
    domain.zone_tall, domain.perm_tall, domain.face_sum = scratch[len(FIRST_SCRATCH) :]
    domain.ps = Joined(ps)

    empty = jnp.zeros((ny + TILE, nz), jnp.float32)
    for l in (W - 1, W + nx):
        for name in ("perm", "heft", "shear", "press", "z0", "p0"):
            getattr(domain, name)[l] = empty
        for c in range(3):
            domain.motion[c, l] = empty
        for i in range(9):
            domain.zs[i, l] = empty
        for i in range(ps.shape[0]):
            ps[i, l] = empty
        domain.perm_tall[l] = jnp.zeros((ny + 2 * TILE, nz), jnp.float32)

    for x in range(nx):
        domain.assemble(W + x, x, fields, lambda f, x=x: rows[0].read(f, x), table)
    if domain.pair:
        upper = lax.axis_index("gx") > 0
        for u in range(W):

            def beside(f, u=u):
                ending, starting = rows[1].read(f, nx - W + u), rows[1].read(f, u)
                return [jnp.where(upper, a, b) for a, b in zip(ending, starting)]

            l = jnp.where(upper, u, W + nx + u)
            x = jnp.where(upper, nx - W + u, u)
            domain.assemble(l, x, below, beside, table)
    else:
        keep_below, keep_above = keeps("gx", peers[0])
        for u in range(W):
            x = nx - W + u
            domain.assemble(u, x, below, lambda f, x=x: rows[1].read(f, x), table, keep_below)
            l = W + nx + u
            domain.assemble(l, u, above, lambda f, u=u: rows[2].read(f, u), table, keep_above)
    domain.first_half()


SECOND_INS = ("z0", "p0", "zs") + PASSED


def brick_second(peers, nx, ny, *refs):
    domain = new_brick(peers, nx, ny)
    domain.__dict__.update(zip(SECOND_INS, refs))
    ready, ps, acc = refs[len(SECOND_INS) :]
    domain.ps = Joined(ready, ps)
    nz = ps.shape[3]
    empty = jnp.zeros((ny + TILE, nz), jnp.float32)
    for l in (W - 1, W + nx):
        for i in range(ps.shape[0]):
            ps[i, l] = empty
    domain.second_half()
    acc[...] = jnp.zeros(acc.shape, jnp.float32)
    column = iota((TILE, nz), 1)
    mask = (column >= W) & (column < nz - W)
    domain.loop(W, nx, lambda l: domain.finish(l, acc, mask), "finish")


class Ends(Domain):
    def roll(self, v, shift):
        return pltpu.roll(v, shift % LANES, v.ndim - 1)

    def nxt(self, ref, l):
        moved = self.roll(ref[pl.ds(l.start, l.size + 1)], -self.row)
        lane = iota(moved[1:].shape, 2)
        return jnp.where(lane < LANES - self.row, moved[:-1], moved[1:])

    def before(self, v):
        moved = self.roll(v, self.row)
        back = jnp.concatenate([jnp.zeros_like(moved[:1]), moved[:-1]], axis=0)
        return jnp.where(iota(moved.shape, 2) >= self.row, moved, back)

    def prv(self, ref, l):
        return self.before(ref[l])

    def back_x(self, faces, step, ref, l, push=None):
        value = faces[l] * step
        if push:
            value = value + push[1]
        return self.before(value) - value

    def push_before(self, refs, l):
        return None

    def yp(self, v):
        return self.roll(v, -1)

    def ym(self, v):
        return self.roll(v, 1)

    def zp(self, v):
        return pltpu.roll(v, ENDS - 1, 1)

    def zm(self, v):
        return pltpu.roll(v, 1, 1)

    def y_sum(self, l):
        face = self.ty[l]
        return face + self.ym(face)

    def near_faces(self, shape):
        row = iota(shape, len(shape) - 1) % self.row
        return (row >= TILE - 1) & (row < self.row - TILE)

    def own(self, v):
        return v

    def fold(self, value, mask):
        total = None
        for g in range(value.shape[0]):
            part = jnp.where(mask, value[g], 0.0)
            for start in range(0, value.shape[1], TILE):
                piece = part[start : start + TILE]
                total = piece if total is None else total + piece
        return total

    def run(self, halo, body, stage, before=0):
        body(pl.ds(0, self.groups) if halo > 3 else self.near)

    def assemble(self, ends, left, right, keep_left, keep_right, table):
        for g in range(self.groups):
            for f in range(NF):
                width, offset = WIDTHS[f], OFFSETS[f]
                rows = slice(offset, offset + width)
                self.raw[f, g] = ends[f, g]
                self.raw[f, g, W - width : W, :] = left[g, rows, :] * keep_left
                self.raw[f, g, ENDS - W : ENDS - W + width, :] = (
                    right[g, rows, :] * keep_right
                )
            zone = self.raw[ZONE, g]
            lame, shear = lookup(zone, table, 1), lookup(zone, table, 2)
            self.perm[g] = lookup(zone, table, 0)
            self.heft[g] = lame + shear
            self.shear[g] = shear
            self.fixed[g] = fixed_term(zone, lame, shear)


class Either:
    def __init__(self, condition, yes, no):
        self.condition, self.refs = condition, (yes, no)

    def __getitem__(self, index):
        return jnp.where(self.condition, *[ref[index] for ref in self.refs])


def own_groups(count, peers):
    return count * blocks_of(peers)[0][0]


def ends_kernel(peers, tall, *refs):
    table, ends, got, passed, added = refs[:5]
    left, right = got, passed
    if peers[0] == 2:
        first = lax.axis_index("gx") == 0
        left, right = Either(first, got, passed), Either(first, passed, got)
    raw, z0, p0, zs, ps, partial = refs[5:11]
    acc, scratch = refs[11], refs[12:]
    names = [name for name, _ in ARRAYS[6:] if name not in KEPT]
    domain = Ends(dict(zip(names, scratch)))
    domain.raw, domain.z0, domain.p0, domain.zs, domain.ps = raw, z0, p0, zs, ps
    domain.zone, domain.press = raw.at[ZONE], raw.at[PRESS]
    domain.motion = raw.at[MOTION : MOTION + 3]
    domain.load, domain.drain = raw.at[SOURCE], raw.at[DRAIN]
    domain.body = raw.at[BODY : BODY + 3]
    domain.row = tall
    domain.groups = groups = raw.shape[1] - 1
    count = groups // len(blocks_of(peers))
    domain.near = pl.ds(0, groups)
    if peers[0] == 2 and LANES // tall > 3:
        domain.near = pl.ds(lax.axis_index("gx") * (count - 1), count + 1)
    keep = keeps("gz", peers[2])
    empty = jnp.zeros((ENDS, LANES), jnp.float32)
    for ref in (raw, zs, ps):
        for i in range(ref.shape[0]):
            ref[i, groups] = empty
            if ref is not raw:
                ref[i, groups - 1] = empty
    for ref in (domain.perm, domain.shear, z0, p0):
        ref[groups] = empty
    p0[groups - 1] = empty
    mine = own_groups(count, peers)
    domain.assemble(ends, left, right, *keep, table)
    domain.stages()
    acc[...] = added[...]
    shape = (ENDS, LANES)
    column, row = iota(shape, 0), iota(shape, 1) % tall
    at_end = ((column >= W) & (column < 2 * W)) | (
        (column >= ENDS - 2 * W) & (column < ENDS - W)
    )
    mask = at_end & (row >= TILE) & (row < tall - TILE)
    domain.finish(pl.ds(mine, count), acc, mask)

    sums = jnp.concatenate(
        [jnp.sum(acc[i], axis=0, keepdims=True) for i in range(acc.shape[0])], axis=0
    )
    totals = jnp.sum(sums, axis=1, keepdims=True)
    spread = jnp.where(iota(sums.shape, 0) == iota(sums.shape, 1), totals, 0.0)
    line = jnp.sum(spread, axis=0, keepdims=True)
    partial[...] = jnp.broadcast_to(line, partial.shape)


def step_sizes(gamma, delta, cross, energy):
    first = gamma / delta
    gamma_new = gamma - 2.0 * first * delta + first * first * cross
    curved = delta - 2.0 * first * cross + first * first * energy
    ratio = gamma_new / gamma
    second = gamma_new / (curved - ratio * gamma_new / first)
    return first + second * (1.0 + ratio), -first * second


def combine(peers, tall, *refs):
    sums, (old, z0, p0, zs), ps, fields = refs[0], refs[1:5], Joined(*refs[5:7]), refs[7]
    raw, ends_z0, ends_p0, ends_zs, ends_ps = refs[8:13]
    pressure, motion, strain, moved, ends_moved, turned = refs[13:]
    line = jnp.sum(sums[...], axis=0, keepdims=True)
    lane = iota(line.shape, 1)

    def value(index):
        return jnp.sum(jnp.where(lane == index, line, 0.0), axis=1, keepdims=True)

    c1, c2 = step_sizes(*[value(i) for i in range(4)])
    weights = (jnp.ones_like(c1), c1, c2)

    def form(start):
        total = 0.0
        for i, (j, k) in enumerate(PAIRS):
            scale = 1.0 if j == k else 2.0
            total = total + scale * weights[j] * weights[k] * value(start + i)
        return total

    d1, d2 = step_sizes(form(4), form(10), form(16), form(22))
    on_z = [d1 * w for w in weights]
    on_p = [d2 * w for w in weights]

    def new_motion(start, z_part, p_part, c, i):
        total = start
        for j in range(3):
            total = total + on_z[j] * z_part[3 * j + c, i]
            total = total + on_p[j] * p_part[3 * j + c, i]
        return total

    nx, ny, nz = pressure.shape
    pack = LANES // tall
    ends = Ends(dict(row=tall))
    groups = raw.shape[1] - 1
    count = groups // len(blocks_of(peers))
    mine = own_groups(count, peers)
    every = pl.ds(0, groups)
    if peers[0] == 2 and pack > 3:
        every = pl.ds(lax.axis_index("gx") * (count - 1), count + 1)
    for c in range(3):
        for i in range(every.size):
            g = every.start + i
            ends_moved[c, g] = new_motion(raw[MOTION + c, g], ends_zs, ends_ps, c, g)
        ends_moved[c, every.start + every.size] = jnp.zeros((ENDS, LANES), jnp.float32)
    along_y, along_z = ends_moved[1, every], ends_moved[2, every]
    first = ends_moved.at[0]
    ends_moved[3, every] = 0.5 * (
        (ends.nxt(first, every) - ends.prv(first, every))
        + (ends.yp(along_y) - ends.ym(along_y))
        + (ends.zp(along_z) - ends.zm(along_z))
    )
    for c in range(3):
        around = 1 if c == 0 else 0
        for l in range(W - around, W + nx + around):
            moved[c, l] = new_motion(old[c, l], zs, ps, c, l)
    brick = Brick({})
    outs = [pressure] + [motion.at[c] for c in range(3)] + [strain]
    for g in range(count):
        at = mine + g
        edges = [raw[PRESS, at] + c1 * ends_z0[at] + c2 * ends_p0[at]]
        edges = edges + [ends_moved[c, at] for c in range(4)]
        flipped = []
        for o, edge in enumerate(edges):
            slot = g * len(outs) + o
            turned[slot, :W, :] = edge[W : 2 * W]
            turned[slot, LANES - W :, :] = edge[ENDS - 2 * W : ENDS - W]
            flipped.append(turned[slot].T)
        for i in range(pack):
            x = g * pack + i
            l = W + x
            top = i * tall + TILE
            column = iota((ny, LANES), 1)
            u = [moved[c, l] for c in range(3)]
            change = (
                (moved[0, l + 1] - moved[0, l - 1])
                + (brick.yp(u[1]) - brick.ym(u[1]))
                + (brick.zp(u[2]) - brick.zm(u[2]))
            )
            results = [fields[PRESS, x] + c1 * z0[l, :ny, :] + c2 * p0[l, :ny, :]]
            results = results + [v[:ny] for v in u] + [0.5 * change[:ny]]
            for out, result, edge in zip(outs, results, flipped):
                edge = edge[top : top + ny]
                if nz == LANES:
                    inner = (column >= W) & (column < LANES - W)
                    out[x] = jnp.where(inner, result, edge)
                else:
                    out[x] = result
                    out[x, :, :LANES] = jnp.where(column >= W, result[:, :LANES], edge)
                    out[x, :, nz - LANES :] = jnp.where(
                        column < LANES - W, result[:, nz - LANES :], edge
                    )


def f32(*shape):
    return jax.ShapeDtypeStruct(shape, jnp.float32)


def vmem(*shape):
    return pltpu.VMEM(shape, jnp.float32)


def call(kernel, outs, *args, unread=0, space=pltpu.VMEM, scratch=(), limit=8, cost=None):
    specs = [
        pl.BlockSpec(memory_space=space if i < len(args) - unread else pl.ANY)
        for i in range(len(args))
    ]
    return pl.pallas_call(
        kernel,
        out_shape=outs,
        in_specs=specs,
        scratch_shapes=scratch,
        cost_estimate=cost,
        compiler_params=pltpu.CompilerParams(vmem_limit_bytes=limit * MIB),
    )(*args)


def ring(value, axis, step):
    peers = lax.axis_size(axis)
    return lax.ppermute(value, axis, [(i, (i + step) % peers) for i in range(peers)])


def pairs(value, axis, start):
    peers = lax.axis_size(axis)
    swaps = [(i, i) for i in range(start)]
    for i in range(start, peers - 1, 2):
        swaps += [(i, i + 1), (i + 1, i)]
    swaps += [(i, i) for i in range(len(swaps), peers)]
    return lax.ppermute(value, axis, swaps)


def x_neighbours(value):
    peers = lax.axis_size("gx")
    above = ring(value, "gx", -1)
    below = above if peers == 2 else ring(value, "gx", 1)
    return below, above


def shards(
    source,
    pressure_old,
    strain_prev,
    motion_old,
    body_force,
    zone_ids,
    drained,
    perm_table,
    lame_table,
    shear_table,
):
    nx, ny, nz = source.shape
    peers = [lax.axis_size(a) for a in AXES]
    total = peers[0] * peers[1] * peers[2]
    pair = peers[0] == 2
    tall = ny + 2 * TILE
    groups = nx * tall // LANES

    def with_peers(kernel, *more):
        return lambda *refs: kernel(peers, *more, *refs)

    raw = (
        source,
        pressure_old,
        strain_prev,
        motion_old,
        body_force,
        zone_ids,
        drained,
    )
    raw = [pltpu.with_memory_space_constraint(a, pltpu.HBM) for a in raw]
    held = [pltpu.VMEM(a.shape, a.dtype) for a in raw]
    tables = [
        pltpu.with_memory_space_constraint(a, pltpu.HBM)
        for a in (perm_table, lame_table, shear_table)
    ]
    message = f32(up_to(nx * ROWS_EACH, TILE), nz)
    first, second, table = call(
        pack_rows,
        [message, message, f32(TILE, LANES)],
        *raw,
        *tables,
        space=pltpu.HBM,
        scratch=held
        + [pltpu.SMEM(a.shape, a.dtype) for a in tables]
        + [pltpu.SemaphoreType.DMA((len(raw) + len(tables),))],
    )
    (fields,) = call(
        pack_fields,
        [f32(NF, nx, ny, nz)],
        *raw,
        table,
        space=pltpu.HBM,
        unread=1,
        scratch=held + [pltpu.SemaphoreType.DMA((len(raw),))],
    )
    fields_below, fields_above = x_neighbours(fields)
    first = pairs(first, "gy", 0)
    second = pairs(second, "gy", 1)
    first_below, first_above = x_neighbours(first)
    second_below, second_above = x_neighbours(second)
    others = [
        (fields_below, first_below, second_below),
        (fields_above, first_above, second_above),
    ][: 1 if pair else 2]
    sides = 1 if pair else 2
    own_ends, *own_messages = call(
        with_peers(pack_own),
        [f32(NF, groups, ENDS, LANES)] + [f32(groups, MSG_ROWS, LANES)] * sides,
        fields,
        first,
        second,
        scratch=[vmem(NF * groups, LANES, nz)],
    )
    span = (1 + len(others)) * groups
    ends, *messages = call(
        with_peers(pack_others),
        [f32(NF, span, ENDS, LANES)] + [f32(span, MSG_ROWS, LANES)] * sides,
        own_ends,
        *own_messages,
        *[array for block in others for array in block],
        scratch=[vmem(NF * groups, LANES, nz)],
        limit=12,
    )
    if pair:
        n = peers[2]
        hops = [(i, (i + 1) % n) for i in range(n)]
        hops += [(n + i, n + (i - 1) % n) for i in range(n)]
        got = lax.ppermute(messages[0], ("gx", "gz"), hops)
    else:
        got, passed = ring(messages[0], "gz", 1), ring(messages[1], "gz", -1)
    depth = nx + 2 * W
    cells = depth * ny * nz

    def shaped(lead, *shape):
        return (lead,) * (lead > 0) + shape

    leads = dict(ARRAYS)
    sums_shape = (up_to(SUMS, TILE), TILE, LANES)

    def layers_of(name):
        return shaped(leads[name], depth, ny + TILE, nz)

    *halves, ps = call(
        with_peers(brick_first),
        [f32(*layers_of(name)) for name in FIRST_OUTS]
        + [f32(3 * len(FIRST_IMAGES), depth, ny + TILE, nz)],
        table,
        fields,
        fields_below,
        fields_above,
        first,
        second,
        first_below,
        second_below,
        first_above,
        second_above,
        scratch=[vmem(*layers_of(name)) for name in FIRST_SCRATCH]
        + [vmem(depth, tall, nz), vmem(depth, tall, nz), vmem(depth, ny + TILE, nz)],
        limit=16,
    )
    half = dict(zip(FIRST_OUTS, halves))
    if pair:
        passed = ring(got, "gx", -1)
    last, added = call(
        with_peers(brick_second, nx, ny),
        [f32(3 * len(SECOND_IMAGES), depth, ny + TILE, nz), f32(*sums_shape)],
        *[half[name] for name in SECOND_INS],
        ps,
    )
    kept = [half[name] for name in KEPT[:-1]] + [ps, last]
    span = span + 1
    *ends_kept, partial = call(
        with_peers(ends_kernel, tall),
        [f32(NF, span, ENDS, LANES)]
        + [f32(*shaped(leads[name], span, ENDS, LANES)) for name in KEPT[1:]]
        + [f32(total, LANES)],
        table,
        ends,
        got,
        passed,
        added,
        scratch=[vmem(*sums_shape)]
        + [
            vmem(*shaped(lead, span, ENDS, LANES))
            for name, lead in ARRAYS[6:]
            if name not in KEPT
        ],
        limit=16,
    )
    sums = lax.all_to_all(partial, AXES, 0, 0, tiled=True)
    return tuple(
        call(
            with_peers(combine, tall),
            [f32(nx, ny, nz), f32(3, nx, ny, nz), f32(nx, ny, nz)],
            sums,
            *kept,
            fields,
            *ends_kept,
            scratch=[
                vmem(3, depth, ny + TILE, nz),
                vmem(4, span, ENDS, LANES),
                vmem(5 * groups, LANES, LANES),
            ],
            limit=16,
        )
    )


def solution(mesh):
    placed = (
        P("gx", "gy", "gz"),
        P("gx", "gy", "gz"),
        P("gx", "gy", "gz"),
        P(None, "gx", "gy", "gz"),
        P(None, "gx", "gy", "gz"),
        P("gx", "gy", "gz"),
        P("gx", "gy", "gz"),
        P(),
        P(),
        P(),
    )
    return jax.shard_map(
        shards,
        mesh=mesh,
        in_specs=placed,
        out_specs=(P("gx", "gy", "gz"), P(None, "gx", "gy", "gz"), P("gx", "gy", "gz")),
        check_vma=False,
    )
```

```python
import jax
import jax.numpy as jnp
from jax import lax
from jax.experimental import pallas as pl
from jax.experimental.pallas import tpu as pltpu
from jax.sharding import PartitionSpec as P


ZONES = 8

storage = 0.2
biot_coef = 0.8
leakage = 2.0
support = 1.0

AXES = ("gx", "gy", "gz")
LANES = 128
TILE = 8
MIB = 2**20

ZONE, PRESS, MOTION, SOURCE, DRAIN, BODY = 0, 1, 2, 5, 6, 7
WIDTHS = (5, 5, 5, 5, 5, 4, 4, 2, 2, 2)
NF = len(WIDTHS)
W = max(WIDTHS)
OFFSETS = tuple(sum(WIDTHS[:f]) for f in range(NF))
ROW_WIDTHS = (5, 4, 4, 3, 4, 4, 4, 2, 2, 2)
ROW_OFFSETS = tuple(sum(ROW_WIDTHS[:f]) for f in range(NF))
ROWS_EACH = sum(ROW_WIDTHS)
PAIRS = tuple((j, k) for j in range(3) for k in range(j, 3))
SUMS = 4 + 4 * len(PAIRS)
SEG = 16
ENDS = 2 * SEG
UNROLL = dict(faces=8, start=8, next=8, shear=8, motion=8, image=3, finish=8)


def up_to(value, multiple):
    return -(-value // multiple) * multiple


MSG_ROWS = up_to(sum(WIDTHS), TILE)


def iota(shape, dim):
    return lax.broadcasted_iota(jnp.int32, shape, dim)


def field_of(raw, f, at):
    source, pressure, strain, motion, body, zones, drained = raw
    if f == ZONE:
        return zones[at].astype(jnp.float32) + 1.0
    if f == PRESS:
        return pressure[at]
    if f == SOURCE:
        return source[at] + biot_coef * strain[at]
    if f == DRAIN:
        return drained[at].astype(jnp.float32)
    return motion[f - MOTION, *at] if f < SOURCE else body[f - BODY, *at]


class Fetch:
    def __init__(self, sources, held, arrived):
        self.held = held
        self.copies = [
            pltpu.make_async_copy(source, copy, arrived.at[i])
            for i, (source, copy) in enumerate(zip(sources, held))
        ]
        self.waiting = set(range(len(held)))
        for i in sorted(self.waiting, key=lambda i: FETCH_ORDER.index(i)):
            self.copies[i].start()

    def need(self, *which):
        for i in which:
            if i in self.waiting:
                self.waiting.remove(i)
                self.copies[i].wait()


FETCH_ORDER = (5, 1, 3, 0, 2, 6, 4, 7, 8, 9)
NEEDS = ((5,), (1,), (3,), (3,), (3,), (0, 2), (6,), (4,), (4,), (4,))


def pack_rows(*refs):
    sources, (first, second, table), held, arrived = refs[:10], refs[10:13], refs[13:23], refs[23]
    fetch = Fetch(sources, held, arrived)
    raw, tables = held[:7], held[7:]
    nx, ny, nz = raw[0].shape
    even = lax.axis_index("gy") % 2 == 0
    fetch.need(7, 8, 9)
    shape = (TILE, LANES)
    tile = jnp.zeros(shape, jnp.float32)
    for t in range(len(tables)):
        for zone in range(ZONES):
            here = (iota(shape, 0) == t) & (iota(shape, 1) == zone + 1)
            tile = jnp.where(here, tables[t][zone], tile)
    table[...] = tile
    inner = iota((ny, nz), 0) < ny - 1
    for f in range(NF):
        width = ROW_WIDTHS[f]
        fetch.need(*NEEDS[f])
        for x in range(nx):
            at = (x, slice(None))
            value = field_of(raw, f, at)
            if f == SOURCE:
                zone, press, middle = [field_of(raw, g, at) for g in (ZONE, PRESS, MOTION + 1)]
                perm = lookup(zone, tile, 0)
                face = jnp.where(inner, harmonic(perm, rows_up(perm)), 0.0)
                value = value - y_part(face, press, middle, inner)
            upward, downward = value[ny - width :], value[:width]
            start = x * ROWS_EACH + ROW_OFFSETS[f]
            first[start : start + width, :] = jnp.where(even, upward, downward)
            second[start : start + width, :] = jnp.where(even, downward, upward)
    used = nx * ROWS_EACH
    for ref in (first, second):
        if ref.shape[0] > used:
            ref[used:, :] = jnp.zeros((ref.shape[0] - used, nz), jnp.float32)


def rows_up(v):
    return pltpu.roll(v, v.shape[0] - 1, 0)


def rows_down(v):
    return pltpu.roll(v, 1, 0)


def y_part(face, press, middle, marked, up=rows_up, down=rows_down):
    step = jnp.where(marked, face * (up(press) - press), 0.0)
    change = jnp.where(marked, up(middle), 0.0) - down(jnp.where(marked, middle, 0.0))
    return (down(step) - step) + (0.5 * biot_coef) * change


def pack_fields(*refs):
    sources, fields, held, arrived = refs[:7], refs[8], refs[9:16], refs[16]
    fetch = Fetch(sources, held, arrived)
    for f in range(NF):
        fetch.need(*NEEDS[f])
        for x in range(fields.shape[1]):
            fields[f, x] = field_of(held, f, (x, slice(None)))


def keeps(axis, peers):
    at = lax.axis_index(axis)
    return jnp.where(at > 0, 1.0, 0.0), jnp.where(at < peers - 1, 1.0, 0.0)


def blocks_of(peers):
    at = lax.axis_index("gx")
    if peers[0] == 2:
        return [(at, 1.0), (1 - at, 1.0)]
    keep_below, keep_above = keeps("gx", peers[0])
    return [(1, 1.0), (0, keep_below), (2, keep_above)]


class Rows:
    def __init__(self, first, second, peers):
        self.refs = first, second
        self.even = lax.axis_index("gy") % 2 == 0
        self.keep = keeps("gy", peers[1])

    def read(self, f, x):
        start = x * ROWS_EACH + ROW_OFFSETS[f]
        a, b = [ref[start : start + ROW_WIDTHS[f], :] for ref in self.refs]
        low, high = jnp.where(self.even, b, a), jnp.where(self.even, a, b)
        return low * self.keep[0], high * self.keep[1]


def keeps(axis, peers):
    at = lax.axis_index(axis)
    return jnp.where(at > 0, 1.0, 0.0), jnp.where(at < peers - 1, 1.0, 0.0)


def block_ends(peers, keep, fields, first, second, stage, put):
    _, nx, ny, nz = fields.shape
    tall = ny + 2 * TILE
    pack = LANES // tall
    count = nx // pack
    gap = jnp.zeros((TILE, nz), jnp.float32)
    rows = Rows(first, second, peers)
    for g in range(count):
        for f in range(NF):
            width = ROW_WIDTHS[f]
            slot = g * NF + f
            for p in range(pack):
                x = g * pack + p
                top = p * tall
                stage[slot, top : top + TILE, :] = gap
                stage[slot, top + TILE + ny : top + tall, :] = gap
                stage[slot, top + TILE : top + TILE + ny, :] = fields[f, x]
                low, high = rows.read(f, x)
                stage[slot, top + TILE - width : top + TILE, :] = low
                stage[slot, top + TILE + ny : top + TILE + ny + width, :] = high
            begin = stage[slot, :, :LANES].T
            finish = begin if nz == LANES else stage[slot, :, nz - LANES :].T
            if not isinstance(keep, float):
                begin, finish = begin * keep, finish * keep
            put(f, g, begin, finish)


def put_ends(ends, f, g, begin, finish):
    zeros = jnp.zeros((TILE, LANES), jnp.float32)
    inner = SEG - W
    ends[f, g, :TILE, :] = zeros
    ends[f, g, ENDS - TILE :, :] = zeros
    ends[f, g, W:SEG, :] = begin[:inner]
    ends[f, g, SEG : ENDS - W, :] = finish[LANES - inner :]


def put_message(peers, messages, f, g, begin, finish):
    rows = slice(OFFSETS[f], OFFSETS[f] + WIDTHS[f])
    rightward, leftward = finish[LANES - WIDTHS[f] :], begin[: WIDTHS[f]]
    if peers[0] == 2:
        first = lax.axis_index("gx") == 0
        messages[0][g, rows, :] = jnp.where(first, rightward, leftward)
    else:
        messages[0][g, rows, :] = rightward
        messages[1][g, rows, :] = leftward


def pack_own(peers, fields, first, second, ends, *refs):
    *messages, stage = refs

    def put(f, g, begin, finish):
        put_ends(ends, f, g, begin, finish)
        put_message(peers, messages, f, g, begin, finish)

    for message in messages:
        message[:, MSG_ROWS - TILE :, :] = jnp.zeros(
            (message.shape[0], TILE, LANES), jnp.float32
        )
    block_ends(peers, 1.0, fields, first, second, stage, put)


def pack_others(peers, *refs):
    blocks = blocks_of(peers)
    sides = 1 if peers[0] == 2 else 2
    own_ends, own = refs[0], refs[1 : 1 + sides]
    others = refs[1 + sides : 1 + sides + 3 * (len(blocks) - 1)]
    ends, *messages, stage = refs[1 + sides + 3 * (len(blocks) - 1) :]
    count = own_ends.shape[1]
    mine = blocks[0][0] * count
    for g in range(count):
        for f in range(NF):
            ends[f, mine + g] = own_ends[f, g]
        for message, part in zip(messages, own):
            message[mine + g] = part[g]
    for b, (start, keep) in enumerate(blocks[1:]):

        def put(f, g, begin, finish, start=start):
            put_ends(ends, f, start * count + g, begin, finish)
            put_message(peers, messages, f, start * count + g, begin, finish)

        for message in messages:
            for g in range(count):
                message[start * count + g, MSG_ROWS - TILE :, :] = jnp.zeros(
                    (TILE, LANES), jnp.float32
                )
        block_ends(peers, keep, *others[3 * b : 3 * b + 3], stage, put)


def times(value, factor):
    return value if factor == 1.0 else factor * value


def harmonic(a, b):
    return 2.0 * a * b / jnp.maximum(a + b, 1e-30)


def lookup(zone, table, row):
    entries = jnp.broadcast_to(table[row : row + 1, :], zone.shape[:-1] + (LANES,))
    index = zone.astype(jnp.int32)
    picked = [
        jnp.take_along_axis(
            entries, index[:, start : start + LANES], axis=1, mode="promise_in_bounds"
        )
        for start in range(0, zone.shape[1], LANES)
    ]
    return picked[0] if len(picked) == 1 else jnp.concatenate(picked, axis=1)


def fixed_term(zone, lame, shear):
    scale = jnp.maximum(lame + 2.0 * shear / 3.0, 1e-30)
    return jnp.where(zone > 0.0, biot_coef * biot_coef / scale, 0.0)


FIRST_IMAGES, SECOND_IMAGES = (0, 1, 2), ()
KEPT = ("motion", "z0", "p0", "zs", "ps")
PASSED = ("heft", "mx", "my", "mz", "react", "tx", "ty", "tz", "pdiag", "ediag", "einv")
ARRAYS = (
    ("zone", 0),
    ("press", 0),
    ("motion", 3),
    ("load", 0),
    ("drain", 0),
    ("body", 3),
    ("perm", 0),
    ("heft", 0),
    ("shear", 0),
    ("fixed", 0),
    ("tx", 0),
    ("ty", 0),
    ("tz", 0),
    ("mx", 0),
    ("my", 0),
    ("mz", 0),
    ("react", 0),
    ("pdiag", 0),
    ("pinv", 0),
    ("z0", 0),
    ("p0", 0),
    ("ediag", 3),
    ("einv", 3),
    ("zs", 9),
    ("ps", 9),
)


class Domain:
    def __init__(self, arrays):
        self.__dict__.update(arrays)

    def press_faces(self, l):
        own = self.perm[l]
        self.tx[l] = harmonic(own, self.nxt(self.perm, l))
        self.ty[l] = harmonic(own, self.yp(own))
        self.tz[l] = harmonic(own, self.zp(own))

    def motion_faces(self, l):
        own = self.shear[l]
        self.mx[l] = harmonic(own, self.nxt(self.shear, l))
        self.my[l] = harmonic(own, self.yp(own))
        self.mz[l] = harmonic(own, self.zp(own))

    def steps(self, ref, l):
        own = ref[l]
        return self.nxt(ref, l) - own, self.yp(own) - own, self.zp(own) - own

    def back_y(self, value):
        return self.ym(value) - value

    def back_z(self, value):
        return self.zm(value) - value

    def press_flux(self, ref, l, along_y=True):
        dx, dy, dz = self.steps(ref, l)
        (part,) = self.back_x(
            [self.tx[l] * dx],
            lambda: [self.tx[l - 1] * (ref[l] - ref[l - 1])],
        )
        total = part + self.back_z(self.tz[l] * dz)
        return total + self.back_y(self.ty[l] * dy) if along_y else total

    def y_terms(self, l):
        face = self.ty[l]
        marked = self.near_faces(face.shape)
        part = y_part(face, self.press[l], self.motion[1, l], marked, self.yp, self.ym)
        return self.y_sum(l), part

    def press_start(self, l):
        face_sum, y_part = self.y_terms(l)
        face = self.tz[l]
        leak = leakage * self.drain[l]
        reaction = storage + self.fixed[l] + leak
        diag = (
            reaction
            + self.tx[l]
            + self.prv(self.tx, l)
            + face_sum
            + (face + self.zm(face))
        )
        inverse = jnp.where(self.zone[l] > 0.0, 1.0 / diag, 0.0)
        along_x, along_z = self.motion.at[0], self.motion[2, l]
        change = (self.nxt(along_x, l) - self.prv(along_x, l)) + (
            self.zp(along_z) - self.zm(along_z)
        )
        residual = (
            self.load[l]
            - (0.5 * biot_coef) * change
            - leak * self.press[l]
            - self.press_flux(self.press, l, False)
            - y_part
        )
        self.react[l] = reaction
        self.pdiag[l] = diag
        self.pinv[l] = inverse
        self.z0[l] = residual * inverse

    def press_next(self, l):
        image = self.react[l] * self.z0[l] + self.press_flux(self.z0, l)
        self.p0[l] = image * self.pinv[l]

    @staticmethod
    def parts(ref, j):
        return [ref.at[3 * j + c] for c in range(3)]

    def elastic(self, refs, l):
        steps = [self.steps(ref, l) for ref in refs]
        pushed = self.heft[l] * (steps[0][0] + steps[1][1] + steps[2][2])
        face = self.mx[l]
        along_x = [face * steps[c][0] for c in range(3)]
        along_x[0] = along_x[0] + pushed
        parts_x = self.back_x(along_x, lambda: self.motion_fluxes(refs, l - 1))
        out = []
        for c in range(3):
            _, dy, dz = steps[c]
            step_y, step_z = self.my[l] * dy, self.mz[l] * dz
            if c == 1:
                step_y = step_y + pushed
            if c == 2:
                step_z = step_z + pushed
            out.append(
                times(refs[c][l], support)
                + parts_x[c]
                + self.back_y(step_y)
                + self.back_z(step_z)
            )
        return out

    def motion_fluxes(self, refs, l):
        a, b, c = [ref[l] for ref in refs]
        steps = [self.nxt(ref, l) - own for ref, own in zip(refs, (a, b, c))]
        face = self.mx[l]
        pushed = self.heft[l] * (steps[0] + (self.yp(b) - b) + (self.zp(c) - c))
        return [face * steps[0] + pushed, face * steps[1], face * steps[2]]

    def gradient(self, ref, l):
        own = ref[l]
        return (
            self.nxt(ref, l) - self.prv(ref, l),
            self.yp(own) - self.ym(own),
            self.zp(own) - self.zm(own),
        )

    def motion_start(self, l):
        weight = self.heft[l]
        along_y, along_z = self.my[l], self.mz[l]
        base = (
            support
            + self.mx[l]
            + self.prv(self.mx, l)
            + (along_y + self.ym(along_y))
            + (along_z + self.zm(along_z))
            + weight
        )
        inside = self.zone[l] > 0.0
        beside = (self.prv(self.heft, l), self.ym(weight), self.zm(weight))
        image = self.elastic(self.parts(self.motion, 0), l)
        grads = [self.gradient(ref, l) for ref in (self.press, self.z0, self.p0)]
        for c in range(3):
            diag = base + beside[c]
            inverse = jnp.where(inside, 1.0 / diag, 0.0)
            self.ediag[c, l] = diag
            self.einv[c, l] = inverse
            start = self.body[c, l] - (0.5 * biot_coef) * grads[0][c] - image[c]
            self.zs[c, l] = start * inverse
            scale = (-0.5 * biot_coef) * inverse
            self.zs[3 + c, l] = grads[1][c] * scale
            self.zs[6 + c, l] = grads[2][c] * scale

    def motion_next(self, l, j):
        image = self.elastic(self.parts(self.zs, j), l)
        for c in range(3):
            self.ps[3 * j + c, l] = image[c] * self.einv[c, l]

    def stages(self):
        self.first_half()
        self.second_half()

    def first_half(self):
        self.run(4, self.press_faces, "faces", 1)
        self.run(4, self.press_start, "start")
        self.run(3, self.press_next, "next")
        self.run(2, self.motion_faces, "shear", 1)
        self.run(2, self.motion_start, "motion")
        for j in FIRST_IMAGES:
            self.images(j)

    def second_half(self):
        for j in SECOND_IMAGES:
            self.images(j)

    def images(self, j):
        self.run(1, lambda l: self.motion_next(l, j), "image")

    def finish(self, l, acc, mask):
        own = self.own

        def add(index, value):
            acc[index] = acc[index] + self.fold(value, mask)

        def total(pairs):
            out = None
            for a, b in pairs:
                out = a * b if out is None else out + a * b
            return out

        a, b = own(self.z0[l]), own(self.p0[l])
        diag = own(self.pdiag[l])
        scaled = diag * b
        add(0, diag * a * a)
        add(1, scaled * a)
        add(2, scaled * b)
        energy = own(self.react[l]) * b * b
        for face, step in zip((self.tx, self.ty, self.tz), self.steps(self.p0, l)):
            step = own(step)
            energy = energy + own(face[l]) * step * step
        add(3, energy)
        diags = [own(self.ediag[c, l]) for c in range(3)]
        faces = [own(ref[l]) for ref in (self.mx, self.my, self.mz)]
        weight = own(self.heft[l])
        za, pa, dz, dp, steps, heavy = [], [], [], [], [], []
        for j in range(3):
            zj, pj = self.parts(self.zs, j), self.parts(self.ps, j)
            za.append([own(ref[l]) for ref in zj])
            pa.append([own(ref[l]) for ref in pj])
            dz.append([d * v for d, v in zip(diags, za[j])])
            dp.append([d * v for d, v in zip(diags, pa[j])])
            moved = [[own(v) for v in self.steps(ref, l)] for ref in pj]
            div = moved[0][0] + moved[1][1] + moved[2][2]
            flat = [(faces[d], moved[c][d]) for c in range(3) for d in range(3)]
            steps.append([v for _, v in flat] + [div] + pa[j])
            heavy.append([f * v for f, v in flat] + [weight * div])
            heavy[j] = heavy[j] + [times(v, support) for v in pa[j]]
        for i, (j, k) in enumerate(PAIRS):
            add(4 + i, total(zip(dz[j], za[k])))
            add(10 + i, total(zip(dp[k], za[j])))
            add(16 + i, total(zip(dp[j], pa[k])))
            add(22 + i, total(zip(heavy[j], steps[k])))

    def loop(self, start, count, body, stage):
        unroll = 1
        if isinstance(count, int):
            unroll = -(-count // -(-count // UNROLL[stage]))
        chunks = count // unroll

        def step(i, carry):
            self.carried = None
            for u in range(unroll):
                body(start + i * unroll + u)
            return carry

        if isinstance(chunks, int) and chunks == 1:
            step(0, 0)
        else:
            lax.fori_loop(0, chunks, step, 0)
            self.carried = None
        if isinstance(count, int):
            for u in range(chunks * unroll, count):
                body(start + u)


class Brick(Domain):
    def nxt(self, ref, l):
        return ref[l + 1]

    def prv(self, ref, l):
        return ref[l - 1]

    def yp(self, v):
        return pltpu.roll(v, v.shape[0] - 1, 0)

    def ym(self, v):
        return pltpu.roll(v, 1, 0)

    def zp(self, v):
        return pltpu.roll(v, v.shape[1] - 1, 1)

    def zm(self, v):
        return pltpu.roll(v, 1, 1)

    def back_x(self, values, again):
        before = again() if self.carried is None else self.carried
        self.carried = values
        return [a - b for a, b in zip(before, values)]

    def own(self, v):
        return v[: self.ny]

    def fold(self, value, mask):
        total = value[:TILE]
        for start in range(TILE, value.shape[0], TILE):
            total = total + value[start : start + TILE]
        nz = value.shape[1]
        if nz > LANES:
            column = iota(total.shape, 1)
            total = jnp.where((column >= W) & (column < nz - W), total, 0.0)
        folded = total[:, :LANES]
        for start in range(LANES, nz, LANES):
            folded = folded + total[:, start : start + LANES]
        return folded

    def first(self, halo):
        return W - halo * self.has_below

    def reach(self, halo):
        if self.pair:
            return halo
        return halo * (self.has_below + self.has_above)

    def run(self, halo, body, stage, before=0):
        count = self.nx + self.reach(halo) + before
        self.loop(self.first(halo) - before, count, body, stage)

    def narrow(self, v):
        ny = self.ny
        upper, lower = v[ny : ny + TILE], v[ny + TILE :]
        both = jnp.where(iota(upper.shape, 0) < TILE // 2, upper, lower)
        return jnp.concatenate([v[:ny], both], axis=0)

    def press_faces(self, l):
        own = self.perm[l]
        self.tx[l] = harmonic(own, self.nxt(self.perm, l))
        tall = self.perm_tall[l]
        face = harmonic(tall, self.yp(tall))
        self.ty[l] = self.narrow(face)
        self.face_sum[l] = self.narrow(face + self.ym(face))
        self.tz[l] = harmonic(own, self.zp(own))

    def y_sum(self, l):
        return self.face_sum[l]

    def near_faces(self, shape):
        row = iota(shape, 0)
        return (row < self.ny) | (row == shape[0] - 1)

    def assemble(self, l, x, fields, beside, table, keep=None):
        ny = self.ny
        gap = jnp.zeros((2 * TILE, fields.shape[3]), jnp.float32)
        refs = [self.zone_tall, self.press] + [self.motion.at[c] for c in range(3)]
        refs += [self.load, self.drain] + [self.body.at[c] for c in range(3)]
        for f, ref in enumerate(refs):
            width, rows = ROW_WIDTHS[f], ref.shape[1]
            below, above = beside(f)
            middle = fields[f, x]
            if keep is not None:
                below, above, middle = below * keep, above * keep, middle * keep
            ref[l, :ny, :] = middle
            ref[l, ny:, :] = gap[: rows - ny]
            ref[l, ny : ny + width, :] = above
            ref[l, rows - width :, :] = below
        tall_zone = self.zone_tall[l]
        perm = lookup(tall_zone, table, 0)
        self.perm_tall[l] = perm
        self.perm[l] = self.narrow(perm)
        zone = self.narrow(tall_zone)
        self.zone[l] = zone
        lame, shear = lookup(zone, table, 1), lookup(zone, table, 2)
        self.heft[l] = lame + shear
        self.shear[l] = shear
        self.fixed[l] = fixed_term(zone, lame, shear)


def new_brick(peers, nx, ny):
    domain = Brick(dict(nx=nx, ny=ny, pair=peers[0] == 2))
    at = lax.axis_index("gx")
    domain.has_below = (at > 0).astype(jnp.int32)
    domain.has_above = (at < peers[0] - 1).astype(jnp.int32)
    return domain


FIRST_OUTS = ("motion", "z0", "p0", "zs") + PASSED
FIRST_SCRATCH = tuple(n for n, _ in ARRAYS if n not in FIRST_OUTS + ("ps",))


class Joined:
    def __init__(self, *refs):
        self.refs = refs
        self.at = self

    def __getitem__(self, index):
        first, *rest = index if isinstance(index, tuple) else (index,)
        for ref in self.refs:
            if first < ref.shape[0]:
                return ref[first, *rest] if rest else ref.at[first]
            first -= ref.shape[0]

    def __setitem__(self, index, value):
        self[index[0]][index[1:]] = value


def brick_first(peers, *refs):
    table, fields, below, above = refs[:4]
    rows = [Rows(*refs[i : i + 2], peers) for i in (4, 6, 8)]
    outs = refs[10 : 10 + len(FIRST_OUTS)]
    ps, *scratch = refs[10 + len(FIRST_OUTS) :]
    _, nx, ny, nz = fields.shape
    domain = new_brick(peers, nx, ny)
    domain.__dict__.update(zip(FIRST_OUTS, outs))
    domain.__dict__.update(zip(FIRST_SCRATCH, scratch))
    domain.zone_tall, domain.perm_tall, domain.face_sum = scratch[len(FIRST_SCRATCH) :]
    domain.ps = Joined(ps)

    empty = jnp.zeros((ny + TILE, nz), jnp.float32)
    for l in (W - 1, W + nx):
        for name in ("perm", "heft", "shear", "press", "z0", "p0"):
            getattr(domain, name)[l] = empty
        for c in range(3):
            domain.motion[c, l] = empty
        for i in range(9):
            domain.zs[i, l] = empty
        for i in range(ps.shape[0]):
            ps[i, l] = empty
        domain.perm_tall[l] = jnp.zeros((ny + 2 * TILE, nz), jnp.float32)

    for x in range(nx):
        domain.assemble(W + x, x, fields, lambda f, x=x: rows[0].read(f, x), table)
    if domain.pair:
        upper = lax.axis_index("gx") > 0
        for u in range(W):

            def beside(f, u=u):
                ending, starting = rows[1].read(f, nx - W + u), rows[1].read(f, u)
                return [jnp.where(upper, a, b) for a, b in zip(ending, starting)]

            l = jnp.where(upper, u, W + nx + u)
            x = jnp.where(upper, nx - W + u, u)
            domain.assemble(l, x, below, beside, table)
    else:
        keep_below, keep_above = keeps("gx", peers[0])
        for u in range(W):
            x = nx - W + u
            domain.assemble(u, x, below, lambda f, x=x: rows[1].read(f, x), table, keep_below)
            l = W + nx + u
            domain.assemble(l, u, above, lambda f, u=u: rows[2].read(f, u), table, keep_above)
    domain.first_half()


SECOND_INS = ("z0", "p0", "zs") + PASSED


def brick_second(peers, nx, ny, *refs):
    domain = new_brick(peers, nx, ny)
    domain.__dict__.update(zip(SECOND_INS, refs))
    ready, *made, acc = refs[len(SECOND_INS) :]
    domain.ps = Joined(ready, *made)
    nz = ready.shape[3]
    empty = jnp.zeros((ny + TILE, nz), jnp.float32)
    for ps in made:
        for l in (W - 1, W + nx):
            for i in range(ps.shape[0]):
                ps[i, l] = empty
    domain.second_half()
    acc[...] = jnp.zeros(acc.shape, jnp.float32)
    domain.loop(W, nx, lambda l: domain.finish(l, acc, None), "finish")
    if nz == LANES:
        column = iota((TILE, LANES), 1)
        mask = (column >= W) & (column < nz - W)
        for i in range(SUMS):
            acc[i] = jnp.where(mask, acc[i], 0.0)


class Ends(Domain):
    def roll(self, v, shift):
        return pltpu.roll(v, shift % LANES, v.ndim - 1)

    def nxt(self, ref, l):
        moved = self.roll(ref[pl.ds(l.start, l.size + 1)], -self.row)
        lane = iota(moved[1:].shape, 2)
        return jnp.where(lane < LANES - self.row, moved[:-1], moved[1:])

    def before(self, v):
        moved = self.roll(v, self.row)
        back = jnp.concatenate([jnp.zeros_like(moved[:1]), moved[:-1]], axis=0)
        return jnp.where(iota(moved.shape, 2) >= self.row, moved, back)

    def prv(self, ref, l):
        return self.before(ref[l])

    def back_x(self, values, again):
        return [self.before(value) - value for value in values]

    def yp(self, v):
        return self.roll(v, -1)

    def ym(self, v):
        return self.roll(v, 1)

    def zp(self, v):
        return pltpu.roll(v, ENDS - 1, 1)

    def zm(self, v):
        return pltpu.roll(v, 1, 1)

    def y_sum(self, l):
        face = self.ty[l]
        return face + self.ym(face)

    def near_faces(self, shape):
        row = iota(shape, len(shape) - 1) % self.row
        return (row >= TILE - 1) & (row < self.row - TILE)

    def own(self, v):
        return v

    def fold(self, value, mask):
        total = None
        for g in range(value.shape[0]):
            part = jnp.where(mask, value[g], 0.0)
            for start in range(0, value.shape[1], TILE):
                piece = part[start : start + TILE]
                total = piece if total is None else total + piece
        return total

    def run(self, halo, body, stage, before=0):
        body(pl.ds(0, self.groups) if halo > 3 else self.near)

    def assemble(self, ends, left, right, keep_left, keep_right, table):
        for g in range(self.groups):
            for f in range(NF):
                width, offset = WIDTHS[f], OFFSETS[f]
                rows = slice(offset, offset + width)
                self.raw[f, g] = ends[f, g]
                self.raw[f, g, W - width : W, :] = left[g, rows, :] * keep_left
                self.raw[f, g, ENDS - W : ENDS - W + width, :] = (
                    right[g, rows, :] * keep_right
                )
            zone = self.raw[ZONE, g]
            lame, shear = lookup(zone, table, 1), lookup(zone, table, 2)
            self.perm[g] = lookup(zone, table, 0)
            self.heft[g] = lame + shear
            self.shear[g] = shear
            self.fixed[g] = fixed_term(zone, lame, shear)


class Either:
    def __init__(self, condition, yes, no):
        self.condition, self.refs = condition, (yes, no)

    def __getitem__(self, index):
        return jnp.where(self.condition, *[ref[index] for ref in self.refs])


def own_groups(count, peers):
    return count * blocks_of(peers)[0][0]


def ends_kernel(peers, tall, *refs):
    table, ends, got, passed, added = refs[:5]
    left, right = got, passed
    if peers[0] == 2:
        first = lax.axis_index("gx") == 0
        left, right = Either(first, got, passed), Either(first, passed, got)
    raw, z0, p0, zs, ps, partial = refs[5:11]
    acc, scratch = refs[11], refs[12:]
    names = [name for name, _ in ARRAYS[6:] if name not in KEPT]
    domain = Ends(dict(zip(names, scratch)))
    domain.raw, domain.z0, domain.p0, domain.zs, domain.ps = raw, z0, p0, zs, ps
    domain.zone, domain.press = raw.at[ZONE], raw.at[PRESS]
    domain.motion = raw.at[MOTION : MOTION + 3]
    domain.load, domain.drain = raw.at[SOURCE], raw.at[DRAIN]
    domain.body = raw.at[BODY : BODY + 3]
    domain.row = tall
    domain.groups = groups = raw.shape[1] - 1
    count = groups // len(blocks_of(peers))
    domain.near = pl.ds(0, groups)
    if peers[0] == 2 and LANES // tall > 3:
        domain.near = pl.ds(lax.axis_index("gx") * (count - 1), count + 1)
    keep = keeps("gz", peers[2])
    empty = jnp.zeros((ENDS, LANES), jnp.float32)
    for ref in (raw, zs, ps):
        for i in range(ref.shape[0]):
            ref[i, groups] = empty
            if ref is not raw:
                ref[i, groups - 1] = empty
    for ref in (domain.perm, domain.shear, z0, p0):
        ref[groups] = empty
    p0[groups - 1] = empty
    mine = own_groups(count, peers)
    domain.assemble(ends, left, right, *keep, table)
    domain.stages()
    acc[...] = added[...]
    shape = (ENDS, LANES)
    column, row = iota(shape, 0), iota(shape, 1) % tall
    at_end = ((column >= W) & (column < 2 * W)) | (
        (column >= ENDS - 2 * W) & (column < ENDS - W)
    )
    mask = at_end & (row >= TILE) & (row < tall - TILE)
    domain.finish(pl.ds(mine, count), acc, mask)

    sums = jnp.concatenate(
        [jnp.sum(acc[i], axis=0, keepdims=True) for i in range(acc.shape[0])], axis=0
    )
    totals = jnp.sum(sums, axis=1, keepdims=True)
    spread = jnp.where(iota(sums.shape, 0) == iota(sums.shape, 1), totals, 0.0)
    line = jnp.sum(spread, axis=0, keepdims=True)
    partial[...] = jnp.broadcast_to(line, partial.shape)


def step_sizes(gamma, delta, cross, energy):
    first = gamma / delta
    gamma_new = gamma - 2.0 * first * delta + first * first * cross
    curved = delta - 2.0 * first * cross + first * first * energy
    ratio = gamma_new / gamma
    second = gamma_new / (curved - ratio * gamma_new / first)
    return first + second * (1.0 + ratio), -first * second


def combine(peers, tall, *refs):
    sums, (old, z0, p0, zs) = refs[0], refs[1:5]
    *ps, fields, raw, ends_z0, ends_p0, ends_zs, ends_ps = refs[5:-6]
    ps = Joined(*ps)
    pressure, motion, strain, moved, ends_moved, turned = refs[-6:]
    line = jnp.sum(sums[...], axis=0, keepdims=True)
    lane = iota(line.shape, 1)

    def value(index):
        return jnp.sum(jnp.where(lane == index, line, 0.0), axis=1, keepdims=True)

    c1, c2 = step_sizes(*[value(i) for i in range(4)])
    weights = (jnp.ones_like(c1), c1, c2)

    def form(start):
        total = 0.0
        for i, (j, k) in enumerate(PAIRS):
            scale = 1.0 if j == k else 2.0
            total = total + scale * weights[j] * weights[k] * value(start + i)
        return total

    d1, d2 = step_sizes(form(4), form(10), form(16), form(22))
    on_z = [d1 * w for w in weights]
    on_p = [d2 * w for w in weights]

    def new_motion(start, z_part, p_part, c, i):
        total = start
        for j in range(3):
            total = total + on_z[j] * z_part[3 * j + c, i]
            total = total + on_p[j] * p_part[3 * j + c, i]
        return total

    nx, ny, nz = pressure.shape
    pack = LANES // tall
    ends = Ends(dict(row=tall))
    groups = raw.shape[1] - 1
    count = groups // len(blocks_of(peers))
    mine = own_groups(count, peers)
    every = pl.ds(0, groups)
    if peers[0] == 2 and pack > 3:
        every = pl.ds(lax.axis_index("gx") * (count - 1), count + 1)
    for c in range(3):
        for i in range(every.size):
            g = every.start + i
            ends_moved[c, g] = new_motion(raw[MOTION + c, g], ends_zs, ends_ps, c, g)
        ends_moved[c, every.start + every.size] = jnp.zeros((ENDS, LANES), jnp.float32)
    along_y, along_z = ends_moved[1, every], ends_moved[2, every]
    first = ends_moved.at[0]
    ends_moved[3, every] = 0.5 * (
        (ends.nxt(first, every) - ends.prv(first, every))
        + (ends.yp(along_y) - ends.ym(along_y))
        + (ends.zp(along_z) - ends.zm(along_z))
    )
    for c in range(3):
        around = 1 if c == 0 else 0
        for l in range(W - around, W + nx + around):
            moved[c, l] = new_motion(old[c, l], zs, ps, c, l)
    brick = Brick({})
    outs = [pressure] + [motion.at[c] for c in range(3)] + [strain]
    for g in range(count):
        at = mine + g
        edges = [raw[PRESS, at] + c1 * ends_z0[at] + c2 * ends_p0[at]]
        edges = edges + [ends_moved[c, at] for c in range(4)]
        flipped = []
        for o, edge in enumerate(edges):
            slot = g * len(outs) + o
            turned[slot, :W, :] = edge[W : 2 * W]
            turned[slot, LANES - W :, :] = edge[ENDS - 2 * W : ENDS - W]
            flipped.append(turned[slot].T)
        for i in range(pack):
            x = g * pack + i
            l = W + x
            top = i * tall + TILE
            column = iota((ny, LANES), 1)
            u = [moved[c, l] for c in range(3)]
            change = (
                (moved[0, l + 1] - moved[0, l - 1])
                + (brick.yp(u[1]) - brick.ym(u[1]))
                + (brick.zp(u[2]) - brick.zm(u[2]))
            )
            results = [fields[PRESS, x] + c1 * z0[l, :ny, :] + c2 * p0[l, :ny, :]]
            results = results + [v[:ny] for v in u] + [0.5 * change[:ny]]
            for out, result, edge in zip(outs, results, flipped):
                edge = edge[top : top + ny]
                if nz == LANES:
                    inner = (column >= W) & (column < LANES - W)
                    out[x] = jnp.where(inner, result, edge)
                else:
                    out[x] = result
                    out[x, :, :LANES] = jnp.where(column >= W, result[:, :LANES], edge)
                    out[x, :, nz - LANES :] = jnp.where(
                        column < LANES - W, result[:, nz - LANES :], edge
                    )


def f32(*shape):
    return jax.ShapeDtypeStruct(shape, jnp.float32)


def vmem(*shape):
    return pltpu.VMEM(shape, jnp.float32)


def call(kernel, outs, *args, unread=0, space=pltpu.VMEM, scratch=(), limit=8, cost=None):
    specs = [
        pl.BlockSpec(memory_space=space if i < len(args) - unread else pl.ANY)
        for i in range(len(args))
    ]
    return pl.pallas_call(
        kernel,
        out_shape=outs,
        in_specs=specs,
        scratch_shapes=scratch,
        cost_estimate=cost,
        compiler_params=pltpu.CompilerParams(vmem_limit_bytes=limit * MIB),
    )(*args)


def ring(value, axis, step):
    peers = lax.axis_size(axis)
    return lax.ppermute(value, axis, [(i, (i + step) % peers) for i in range(peers)])


def pairs(value, axis, start):
    peers = lax.axis_size(axis)
    swaps = [(i, i) for i in range(start)]
    for i in range(start, peers - 1, 2):
        swaps += [(i, i + 1), (i + 1, i)]
    swaps += [(i, i) for i in range(len(swaps), peers)]
    return lax.ppermute(value, axis, swaps)


def x_neighbours(value):
    peers = lax.axis_size("gx")
    above = ring(value, "gx", -1)
    below = above if peers == 2 else ring(value, "gx", 1)
    return below, above


def shards(
    source,
    pressure_old,
    strain_prev,
    motion_old,
    body_force,
    zone_ids,
    drained,
    perm_table,
    lame_table,
    shear_table,
):
    nx, ny, nz = source.shape
    peers = [lax.axis_size(a) for a in AXES]
    total = peers[0] * peers[1] * peers[2]
    pair = peers[0] == 2
    tall = ny + 2 * TILE
    groups = nx * tall // LANES

    def with_peers(kernel, *more):
        return lambda *refs: kernel(peers, *more, *refs)

    raw = (
        source,
        pressure_old,
        strain_prev,
        motion_old,
        body_force,
        zone_ids,
        drained,
    )
    raw = [pltpu.with_memory_space_constraint(a, pltpu.HBM) for a in raw]
    held = [pltpu.VMEM(a.shape, a.dtype) for a in raw]
    tables = [
        pltpu.with_memory_space_constraint(a, pltpu.HBM)
        for a in (perm_table, lame_table, shear_table)
    ]
    message = f32(up_to(nx * ROWS_EACH, TILE), nz)
    first, second, table = call(
        pack_rows,
        [message, message, f32(TILE, LANES)],
        *raw,
        *tables,
        space=pltpu.HBM,
        scratch=held
        + [pltpu.SMEM(a.shape, a.dtype) for a in tables]
        + [pltpu.SemaphoreType.DMA((len(raw) + len(tables),))],
    )
    (fields,) = call(
        pack_fields,
        [f32(NF, nx, ny, nz)],
        *raw,
        table,
        space=pltpu.HBM,
        unread=1,
        scratch=held + [pltpu.SemaphoreType.DMA((len(raw),))],
    )
    fields_below, fields_above = x_neighbours(fields)
    first = pairs(first, "gy", 0)
    second = pairs(second, "gy", 1)
    first_below, first_above = x_neighbours(first)
    second_below, second_above = x_neighbours(second)
    others = [
        (fields_below, first_below, second_below),
        (fields_above, first_above, second_above),
    ][: 1 if pair else 2]
    sides = 1 if pair else 2
    own_ends, *own_messages = call(
        with_peers(pack_own),
        [f32(NF, groups, ENDS, LANES)] + [f32(groups, MSG_ROWS, LANES)] * sides,
        fields,
        first,
        second,
        scratch=[vmem(NF * groups, LANES, nz)],
    )
    span = (1 + len(others)) * groups
    ends, *messages = call(
        with_peers(pack_others),
        [f32(NF, span, ENDS, LANES)] + [f32(span, MSG_ROWS, LANES)] * sides,
        own_ends,
        *own_messages,
        *[array for block in others for array in block],
        scratch=[vmem(NF * groups, LANES, nz)],
        limit=12,
    )
    if pair:
        n = peers[2]
        hops = [(i, (i + 1) % n) for i in range(n)]
        hops += [(n + i, n + (i - 1) % n) for i in range(n)]
        got = lax.ppermute(messages[0], ("gx", "gz"), hops)
    else:
        got, passed = ring(messages[0], "gz", 1), ring(messages[1], "gz", -1)
    depth = nx + 2 * W
    cells = depth * ny * nz

    def shaped(lead, *shape):
        return (lead,) * (lead > 0) + shape

    leads = dict(ARRAYS)
    sums_shape = (up_to(SUMS, TILE), TILE, LANES)

    def layers_of(name):
        return shaped(leads[name], depth, ny + TILE, nz)

    *halves, ps = call(
        with_peers(brick_first),
        [f32(*layers_of(name)) for name in FIRST_OUTS]
        + [f32(3 * len(FIRST_IMAGES), depth, ny + TILE, nz)],
        table,
        fields,
        fields_below,
        fields_above,
        first,
        second,
        first_below,
        second_below,
        first_above,
        second_above,
        scratch=[vmem(*layers_of(name)) for name in FIRST_SCRATCH]
        + [vmem(depth, tall, nz), vmem(depth, tall, nz), vmem(depth, ny + TILE, nz)],
        limit=16,
    )
    half = dict(zip(FIRST_OUTS, halves))
    if pair:
        passed = ring(got, "gx", -1)
    late = [f32(3 * len(SECOND_IMAGES), depth, ny + TILE, nz)] * bool(SECOND_IMAGES)
    *last, added = call(
        with_peers(brick_second, nx, ny),
        late + [f32(*sums_shape)],
        *[half[name] for name in SECOND_INS],
        ps,
    )
    kept = [half[name] for name in KEPT[:-1]] + [ps, *last]
    span = span + 1
    *ends_kept, partial = call(
        with_peers(ends_kernel, tall),
        [f32(NF, span, ENDS, LANES)]
        + [f32(*shaped(leads[name], span, ENDS, LANES)) for name in KEPT[1:]]
        + [f32(total, LANES)],
        table,
        ends,
        got,
        passed,
        added,
        scratch=[vmem(*sums_shape)]
        + [
            vmem(*shaped(lead, span, ENDS, LANES))
            for name, lead in ARRAYS[6:]
            if name not in KEPT
        ],
        limit=16,
    )
    sums = lax.all_to_all(partial, AXES, 0, 0, tiled=True)
    return tuple(
        call(
            with_peers(combine, tall),
            [f32(nx, ny, nz), f32(3, nx, ny, nz), f32(nx, ny, nz)],
            sums,
            *kept,
            fields,
            *ends_kept,
            scratch=[
                vmem(3, depth, ny + TILE, nz),
                vmem(4, span, ENDS, LANES),
                vmem(5 * groups, LANES, LANES),
            ],
            limit=16,
        )
    )


def solution(mesh):
    placed = (
        P("gx", "gy", "gz"),
        P("gx", "gy", "gz"),
        P("gx", "gy", "gz"),
        P(None, "gx", "gy", "gz"),
        P(None, "gx", "gy", "gz"),
        P("gx", "gy", "gz"),
        P("gx", "gy", "gz"),
        P(),
        P(),
        P(),
    )
    return jax.shard_map(
        shards,
        mesh=mesh,
        in_specs=placed,
        out_specs=(P("gx", "gy", "gz"), P(None, "gx", "gy", "gz"), P("gx", "gy", "gz")),
        check_vma=False,
    )
```

```python
import jax
import jax.numpy as jnp
from jax import lax
from jax.experimental import pallas as pl
from jax.experimental.pallas import tpu as pltpu
from jax.sharding import PartitionSpec as P


ZONES = 8

storage = 0.2
biot_coef = 0.8
leakage = 2.0
support = 1.0

AXES = ("gx", "gy", "gz")
LANES = 128
TILE = 8
MIB = 2**20

ZONE, PRESS, MOTION, SOURCE, DRAIN, BODY = 0, 1, 2, 5, 6, 7
WIDTHS = (5, 5, 5, 5, 5, 4, 4, 2, 2, 2)
NF = len(WIDTHS)
W = max(WIDTHS)
OFFSETS = tuple(sum(WIDTHS[:f]) for f in range(NF))
ROW_WIDTHS = (5, 4, 4, 3, 4, 4, 4, 2, 2, 2)
ROW_OFFSETS = tuple(sum(ROW_WIDTHS[:f]) for f in range(NF))
ROWS_EACH = sum(ROW_WIDTHS)
PAIRS = tuple((j, k) for j in range(3) for k in range(j, 3))
SUMS = 4 + 4 * len(PAIRS)
SEG = 16
ENDS_KEPT = (("press", 1), ("motion", 3), ("z0", 1), ("p0", 1), ("zs", 9), ("ps", 9))
ENDS_ARRAYS = sum(count for _, count in ENDS_KEPT)
ENDS_START = dict(press=0, motion=1, z0=4, p0=5, zs=6, ps=15)
UNROLL = dict(faces=8, start=8, next=8, shear=8, motion=8, image=3, finish=8)


def up_to(value, multiple):
    return -(-value // multiple) * multiple


MSG_ROWS = up_to(sum(WIDTHS), TILE)


def iota(shape, dim):
    return lax.broadcasted_iota(jnp.int32, shape, dim)


def field_of(raw, f, at):
    source, pressure, strain, motion, body, zones, drained = raw
    if f == ZONE:
        return zones[at].astype(jnp.float32) + 1.0
    if f == PRESS:
        return pressure[at]
    if f == SOURCE:
        return source[at] + biot_coef * strain[at]
    if f == DRAIN:
        return drained[at].astype(jnp.float32)
    return motion[f - MOTION, *at] if f < SOURCE else body[f - BODY, *at]


class Fetch:
    def __init__(self, sources, held, arrived):
        self.held = held
        self.copies = [
            pltpu.make_async_copy(source, copy, arrived.at[i])
            for i, (source, copy) in enumerate(zip(sources, held))
        ]
        self.waiting = set(range(len(held)))
        for i in sorted(self.waiting, key=lambda i: FETCH_ORDER.index(i)):
            self.copies[i].start()

    def need(self, *which):
        for i in which:
            if i in self.waiting:
                self.waiting.remove(i)
                self.copies[i].wait()


FETCH_ORDER = (5, 1, 3, 0, 2, 6, 4, 7, 8, 9)
NEEDS = ((5,), (1,), (3,), (3,), (3,), (0, 2), (6,), (4,), (4,), (4,))


def pack_rows(*refs):
    sources, (first, second, table), held, arrived = refs[:10], refs[10:13], refs[13:23], refs[23]
    fetch = Fetch(sources, held, arrived)
    raw, tables = held[:7], held[7:]
    nx, ny, nz = raw[0].shape
    even = lax.axis_index("gy") % 2 == 0
    fetch.need(7, 8, 9)
    shape = (TILE, LANES)
    tile = jnp.zeros(shape, jnp.float32)
    for t in range(len(tables)):
        for zone in range(ZONES):
            here = (iota(shape, 0) == t) & (iota(shape, 1) == zone + 1)
            tile = jnp.where(here, tables[t][zone], tile)
    table[...] = tile
    inner = iota((ny, nz), 0) < ny - 1
    for f in range(NF):
        width = ROW_WIDTHS[f]
        fetch.need(*NEEDS[f])
        for x in range(nx):
            at = (x, slice(None))
            value = field_of(raw, f, at)
            if f == SOURCE:
                zone, press, middle = [field_of(raw, g, at) for g in (ZONE, PRESS, MOTION + 1)]
                perm = lookup(zone, tile, 0)
                face = jnp.where(inner, harmonic(perm, rows_up(perm)), 0.0)
                value = value - y_part(face, press, middle, inner)
            upward, downward = value[ny - width :], value[:width]
            start = x * ROWS_EACH + ROW_OFFSETS[f]
            first[start : start + width, :] = jnp.where(even, upward, downward)
            second[start : start + width, :] = jnp.where(even, downward, upward)
    used = nx * ROWS_EACH
    for ref in (first, second):
        if ref.shape[0] > used:
            ref[used:, :] = jnp.zeros((ref.shape[0] - used, nz), jnp.float32)


def rows_up(v):
    return pltpu.roll(v, v.shape[0] - 1, 0)


def rows_down(v):
    return pltpu.roll(v, 1, 0)


def y_part(face, press, middle, marked, up=rows_up, down=rows_down):
    step = jnp.where(marked, face * (up(press) - press), 0.0)
    change = jnp.where(marked, up(middle), 0.0) - down(jnp.where(marked, middle, 0.0))
    return (down(step) - step) + (0.5 * biot_coef) * change


def pack_fields(*refs):
    sources, fields, held, arrived = refs[:7], refs[8], refs[9:16], refs[16]
    fetch = Fetch(sources, held, arrived)
    for f in range(NF):
        fetch.need(*NEEDS[f])
        for x in range(fields.shape[1]):
            fields[f, x] = field_of(held, f, (x, slice(None)))


def keeps(axis, peers):
    at = lax.axis_index(axis)
    return jnp.where(at > 0, 1.0, 0.0), jnp.where(at < peers - 1, 1.0, 0.0)


def blocks_of(peers):
    at = lax.axis_index("gx")
    if peers[0] == 2:
        return [(at, 1.0), (1 - at, 1.0)]
    keep_below, keep_above = keeps("gx", peers[0])
    return [(1, 1.0), (0, keep_below), (2, keep_above)]


class Rows:
    def __init__(self, first, second, peers):
        self.refs = first, second
        self.even = lax.axis_index("gy") % 2 == 0
        self.keep = keeps("gy", peers[1])

    def read(self, f, x):
        start = x * ROWS_EACH + ROW_OFFSETS[f]
        a, b = [ref[start : start + ROW_WIDTHS[f], :] for ref in self.refs]
        low, high = jnp.where(self.even, b, a), jnp.where(self.even, a, b)
        return low * self.keep[0], high * self.keep[1]


def keeps(axis, peers):
    at = lax.axis_index(axis)
    return jnp.where(at > 0, 1.0, 0.0), jnp.where(at < peers - 1, 1.0, 0.0)


def block_ends(peers, keep, fields, first, second, stage, put):
    _, nx, ny, nz = fields.shape
    tall = ny + 2 * TILE
    pack = LANES // tall
    count = nx // pack
    gap = jnp.zeros((TILE, nz), jnp.float32)
    rows = Rows(first, second, peers)
    for g in range(count):
        for f in range(NF):
            width = ROW_WIDTHS[f]
            slot = g * NF + f
            for p in range(pack):
                x = g * pack + p
                top = p * tall
                stage[slot, top : top + TILE, :] = gap
                stage[slot, top + TILE + ny : top + tall, :] = gap
                stage[slot, top + TILE : top + TILE + ny, :] = fields[f, x]
                low, high = rows.read(f, x)
                stage[slot, top + TILE - width : top + TILE, :] = low
                stage[slot, top + TILE + ny : top + TILE + ny + width, :] = high
            begin = stage[slot, :, :LANES].T
            finish = begin if nz == LANES else stage[slot, :, nz - LANES :].T
            if not isinstance(keep, float):
                begin, finish = begin * keep, finish * keep
            put(f, g, begin, finish)


def sides_of(peers):
    return 1 if peers[0] == 2 else 2


def put_ends(peers, ends, f, g, begin, finish):
    row = iota((SEG, LANES), 0)
    left = pltpu.roll(begin[:SEG], W, 0)
    right = pltpu.roll(finish[LANES - SEG :], SEG - W, 0)
    left = jnp.where(row >= W, left, 0.0)
    right = jnp.where(row < SEG - W, right, 0.0)
    if sides_of(peers) == 1:
        ends[f, g] = jnp.where(lax.axis_index("gx") == 0, left, right)
    else:
        ends[f, g, :SEG, :] = left
        ends[f, g, SEG:, :] = right


def put_message(peers, messages, f, g, begin, finish):
    rows = slice(OFFSETS[f], OFFSETS[f] + WIDTHS[f])
    rightward, leftward = finish[LANES - WIDTHS[f] :], begin[: WIDTHS[f]]
    if peers[0] == 2:
        first = lax.axis_index("gx") == 0
        messages[0][g, rows, :] = jnp.where(first, rightward, leftward)
    else:
        messages[0][g, rows, :] = rightward
        messages[1][g, rows, :] = leftward


def pack_own(peers, fields, first, second, ends, *refs):
    *messages, stage = refs

    def put(f, g, begin, finish):
        put_ends(peers, ends, f, g, begin, finish)
        put_message(peers, messages, f, g, begin, finish)

    for message in messages:
        message[:, MSG_ROWS - TILE :, :] = jnp.zeros(
            (message.shape[0], TILE, LANES), jnp.float32
        )
    block_ends(peers, 1.0, fields, first, second, stage, put)


def pack_others(peers, *refs):
    blocks = blocks_of(peers)
    sides = 1 if peers[0] == 2 else 2
    own_ends, own = refs[0], refs[1 : 1 + sides]
    others = refs[1 + sides : 1 + sides + 3 * (len(blocks) - 1)]
    ends, *messages, stage = refs[1 + sides + 3 * (len(blocks) - 1) :]
    count = own_ends.shape[1]
    mine = blocks[0][0] * count
    for g in range(count):
        for f in range(NF):
            ends[f, mine + g] = own_ends[f, g]
        for message, part in zip(messages, own):
            message[mine + g] = part[g]
    for b, (start, keep) in enumerate(blocks[1:]):

        def put(f, g, begin, finish, start=start):
            put_ends(peers, ends, f, start * count + g, begin, finish)
            put_message(peers, messages, f, start * count + g, begin, finish)

        for message in messages:
            for g in range(count):
                message[start * count + g, MSG_ROWS - TILE :, :] = jnp.zeros(
                    (TILE, LANES), jnp.float32
                )
        block_ends(peers, keep, *others[3 * b : 3 * b + 3], stage, put)


def times(value, factor):
    return value if factor == 1.0 else factor * value


def harmonic(a, b):
    return 2.0 * a * b / jnp.maximum(a + b, 1e-30)


def lookup(zone, table, row):
    entries = jnp.broadcast_to(table[row : row + 1, :], zone.shape[:-1] + (LANES,))
    index = zone.astype(jnp.int32)
    picked = [
        jnp.take_along_axis(
            entries, index[:, start : start + LANES], axis=1, mode="promise_in_bounds"
        )
        for start in range(0, zone.shape[1], LANES)
    ]
    return picked[0] if len(picked) == 1 else jnp.concatenate(picked, axis=1)


def fixed_term(zone, lame, shear):
    scale = jnp.maximum(lame + 2.0 * shear / 3.0, 1e-30)
    return jnp.where(zone > 0.0, biot_coef * biot_coef / scale, 0.0)


FIRST_IMAGES, SECOND_IMAGES = (0, 1, 2), ()
KEPT = ("motion", "z0", "p0", "zs", "ps")
PASSED = ("heft", "mx", "my", "mz", "react", "tx", "ty", "tz", "pdiag", "ediag", "einv")
ARRAYS = (
    ("zone", 0),
    ("press", 0),
    ("motion", 3),
    ("load", 0),
    ("drain", 0),
    ("body", 3),
    ("perm", 0),
    ("heft", 0),
    ("shear", 0),
    ("fixed", 0),
    ("tx", 0),
    ("ty", 0),
    ("tz", 0),
    ("mx", 0),
    ("my", 0),
    ("mz", 0),
    ("react", 0),
    ("pdiag", 0),
    ("pinv", 0),
    ("z0", 0),
    ("p0", 0),
    ("ediag", 3),
    ("einv", 3),
    ("zs", 9),
    ("ps", 9),
)


class Domain:
    def __init__(self, arrays):
        self.__dict__.update(arrays)

    def press_faces(self, l):
        own = self.perm[l]
        self.tx[l] = harmonic(own, self.nxt(self.perm, l))
        self.ty[l] = harmonic(own, self.yp(own))
        self.tz[l] = harmonic(own, self.zp(own))

    def motion_faces(self, l):
        own = self.shear[l]
        self.mx[l] = harmonic(own, self.nxt(self.shear, l))
        self.my[l] = harmonic(own, self.yp(own))
        self.mz[l] = harmonic(own, self.zp(own))

    def steps(self, ref, l):
        own = ref[l]
        return self.nxt(ref, l) - own, self.yp(own) - own, self.zp(own) - own

    def back_y(self, value):
        return self.ym(value) - value

    def back_z(self, value):
        return self.zm(value) - value

    def press_flux(self, ref, l, along_y=True):
        dx, dy, dz = self.steps(ref, l)
        (part,) = self.back_x(
            [self.tx[l] * dx],
            lambda: [self.tx[l - 1] * (ref[l] - ref[l - 1])],
        )
        total = part + self.back_z(self.tz[l] * dz)
        return total + self.back_y(self.ty[l] * dy) if along_y else total

    def y_terms(self, l):
        face = self.ty[l]
        marked = self.near_faces(face.shape)
        part = y_part(face, self.press[l], self.motion[1, l], marked, self.yp, self.ym)
        return self.y_sum(l), part

    def press_start(self, l):
        face_sum, y_part = self.y_terms(l)
        face = self.tz[l]
        leak = leakage * self.drain[l]
        reaction = storage + self.fixed[l] + leak
        diag = (
            reaction
            + self.tx[l]
            + self.prv(self.tx, l)
            + face_sum
            + (face + self.zm(face))
        )
        inverse = jnp.where(self.zone[l] > 0.0, 1.0 / diag, 0.0)
        along_x, along_z = self.motion.at[0], self.motion[2, l]
        change = (self.nxt(along_x, l) - self.prv(along_x, l)) + (
            self.zp(along_z) - self.zm(along_z)
        )
        residual = (
            self.load[l]
            - (0.5 * biot_coef) * change
            - leak * self.press[l]
            - self.press_flux(self.press, l, False)
            - y_part
        )
        self.react[l] = reaction
        self.pdiag[l] = diag
        self.pinv[l] = inverse
        self.z0[l] = residual * inverse

    def press_next(self, l):
        image = self.react[l] * self.z0[l] + self.press_flux(self.z0, l)
        self.p0[l] = image * self.pinv[l]

    @staticmethod
    def parts(ref, j):
        return [ref.at[3 * j + c] for c in range(3)]

    def elastic(self, refs, l):
        steps = [self.steps(ref, l) for ref in refs]
        pushed = self.heft[l] * (steps[0][0] + steps[1][1] + steps[2][2])
        face = self.mx[l]
        along_x = [face * steps[c][0] for c in range(3)]
        along_x[0] = along_x[0] + pushed
        parts_x = self.back_x(along_x, lambda: self.motion_fluxes(refs, l - 1))
        out = []
        for c in range(3):
            _, dy, dz = steps[c]
            step_y, step_z = self.my[l] * dy, self.mz[l] * dz
            if c == 1:
                step_y = step_y + pushed
            if c == 2:
                step_z = step_z + pushed
            out.append(
                times(refs[c][l], support)
                + parts_x[c]
                + self.back_y(step_y)
                + self.back_z(step_z)
            )
        return out

    def motion_fluxes(self, refs, l):
        a, b, c = [ref[l] for ref in refs]
        steps = [self.nxt(ref, l) - own for ref, own in zip(refs, (a, b, c))]
        face = self.mx[l]
        pushed = self.heft[l] * (steps[0] + (self.yp(b) - b) + (self.zp(c) - c))
        return [face * steps[0] + pushed, face * steps[1], face * steps[2]]

    def gradient(self, ref, l):
        own = ref[l]
        return (
            self.nxt(ref, l) - self.prv(ref, l),
            self.yp(own) - self.ym(own),
            self.zp(own) - self.zm(own),
        )

    def motion_start(self, l):
        weight = self.heft[l]
        along_y, along_z = self.my[l], self.mz[l]
        base = (
            support
            + self.mx[l]
            + self.prv(self.mx, l)
            + (along_y + self.ym(along_y))
            + (along_z + self.zm(along_z))
            + weight
        )
        inside = self.zone[l] > 0.0
        beside = (self.prv(self.heft, l), self.ym(weight), self.zm(weight))
        image = self.elastic(self.parts(self.motion, 0), l)
        grads = [self.gradient(ref, l) for ref in (self.press, self.z0, self.p0)]
        for c in range(3):
            diag = base + beside[c]
            inverse = jnp.where(inside, 1.0 / diag, 0.0)
            self.ediag[c, l] = diag
            self.einv[c, l] = inverse
            start = self.body[c, l] - (0.5 * biot_coef) * grads[0][c] - image[c]
            self.zs[c, l] = start * inverse
            scale = (-0.5 * biot_coef) * inverse
            self.zs[3 + c, l] = grads[1][c] * scale
            self.zs[6 + c, l] = grads[2][c] * scale

    def motion_next(self, l, j):
        image = self.elastic(self.parts(self.zs, j), l)
        for c in range(3):
            self.ps[3 * j + c, l] = image[c] * self.einv[c, l]

    def stages(self):
        self.first_half()
        self.second_half()

    def first_half(self):
        self.run(4, self.press_faces, "faces", 1)
        self.run(4, self.press_start, "start")
        self.run(3, self.press_next, "next")
        self.run(2, self.motion_faces, "shear", 1)
        self.run(2, self.motion_start, "motion")
        for j in FIRST_IMAGES:
            self.images(j)

    def second_half(self):
        for j in SECOND_IMAGES:
            self.images(j)

    def images(self, j):
        self.run(1, lambda l: self.motion_next(l, j), "image")

    def finish(self, l, acc, mask):
        own = self.own

        def add(index, value):
            acc[index] = acc[index] + self.fold(value, mask)

        def total(pairs):
            out = None
            for a, b in pairs:
                out = a * b if out is None else out + a * b
            return out

        a, b = own(self.z0[l]), own(self.p0[l])
        diag = own(self.pdiag[l])
        scaled = diag * b
        add(0, diag * a * a)
        add(1, scaled * a)
        add(2, scaled * b)
        energy = own(self.react[l]) * b * b
        for face, step in zip((self.tx, self.ty, self.tz), self.steps(self.p0, l)):
            step = own(step)
            energy = energy + own(face[l]) * step * step
        add(3, energy)
        diags = [own(self.ediag[c, l]) for c in range(3)]
        faces = [own(ref[l]) for ref in (self.mx, self.my, self.mz)]
        weight = own(self.heft[l])
        za, pa, dz, dp, steps, heavy = [], [], [], [], [], []
        for j in range(3):
            zj, pj = self.parts(self.zs, j), self.parts(self.ps, j)
            za.append([own(ref[l]) for ref in zj])
            pa.append([own(ref[l]) for ref in pj])
            dz.append([d * v for d, v in zip(diags, za[j])])
            dp.append([d * v for d, v in zip(diags, pa[j])])
            moved = [[own(v) for v in self.steps(ref, l)] for ref in pj]
            div = moved[0][0] + moved[1][1] + moved[2][2]
            flat = [(faces[d], moved[c][d]) for c in range(3) for d in range(3)]
            steps.append([v for _, v in flat] + [div] + pa[j])
            heavy.append([f * v for f, v in flat] + [weight * div])
            heavy[j] = heavy[j] + [times(v, support) for v in pa[j]]
        for i, (j, k) in enumerate(PAIRS):
            add(4 + i, total(zip(dz[j], za[k])))
            add(10 + i, total(zip(dp[k], za[j])))
            add(16 + i, total(zip(dp[j], pa[k])))
            add(22 + i, total(zip(heavy[j], steps[k])))

    def loop(self, start, count, body, stage):
        unroll = 1
        if isinstance(count, int):
            unroll = -(-count // -(-count // UNROLL[stage]))
        chunks = count // unroll

        def step(i, carry):
            self.carried = None
            for u in range(unroll):
                body(start + i * unroll + u)
            return carry

        if isinstance(chunks, int) and chunks == 1:
            step(0, 0)
        else:
            lax.fori_loop(0, chunks, step, 0)
            self.carried = None
        if isinstance(count, int):
            for u in range(chunks * unroll, count):
                body(start + u)


class Brick(Domain):
    def nxt(self, ref, l):
        return ref[l + 1]

    def prv(self, ref, l):
        return ref[l - 1]

    def yp(self, v):
        return pltpu.roll(v, v.shape[0] - 1, 0)

    def ym(self, v):
        return pltpu.roll(v, 1, 0)

    def zp(self, v):
        return pltpu.roll(v, v.shape[1] - 1, 1)

    def zm(self, v):
        return pltpu.roll(v, 1, 1)

    def back_x(self, values, again):
        before = again() if self.carried is None else self.carried
        self.carried = values
        return [a - b for a, b in zip(before, values)]

    def own(self, v):
        return v[: self.ny]

    def fold(self, value, mask):
        total = value[:TILE]
        for start in range(TILE, value.shape[0], TILE):
            total = total + value[start : start + TILE]
        nz = value.shape[1]
        if nz > LANES:
            column = iota(total.shape, 1)
            total = jnp.where((column >= W) & (column < nz - W), total, 0.0)
        folded = total[:, :LANES]
        for start in range(LANES, nz, LANES):
            folded = folded + total[:, start : start + LANES]
        return folded

    def first(self, halo):
        return W - halo * self.has_below

    def reach(self, halo):
        if self.pair:
            return halo
        return halo * (self.has_below + self.has_above)

    def run(self, halo, body, stage, before=0):
        count = self.nx + self.reach(halo) + before
        self.loop(self.first(halo) - before, count, body, stage)

    def narrow(self, v):
        ny = self.ny
        upper, lower = v[ny : ny + TILE], v[ny + TILE :]
        both = jnp.where(iota(upper.shape, 0) < TILE // 2, upper, lower)
        return jnp.concatenate([v[:ny], both], axis=0)

    def press_faces(self, l):
        own = self.perm[l]
        self.tx[l] = harmonic(own, self.nxt(self.perm, l))
        tall = self.perm_tall[l]
        face = harmonic(tall, self.yp(tall))
        self.ty[l] = self.narrow(face)
        self.face_sum[l] = self.narrow(face + self.ym(face))
        self.tz[l] = harmonic(own, self.zp(own))

    def y_sum(self, l):
        return self.face_sum[l]

    def near_faces(self, shape):
        row = iota(shape, 0)
        return (row < self.ny) | (row == shape[0] - 1)

    def assemble(self, l, x, fields, beside, table, keep=None):
        ny = self.ny
        gap = jnp.zeros((2 * TILE, fields.shape[3]), jnp.float32)
        refs = [self.zone_tall, self.press] + [self.motion.at[c] for c in range(3)]
        refs += [self.load, self.drain] + [self.body.at[c] for c in range(3)]
        for f, ref in enumerate(refs):
            width, rows = ROW_WIDTHS[f], ref.shape[1]
            below, above = beside(f)
            middle = fields[f, x]
            if keep is not None:
                below, above, middle = below * keep, above * keep, middle * keep
            ref[l, :ny, :] = middle
            ref[l, ny:, :] = gap[: rows - ny]
            ref[l, ny : ny + width, :] = above
            ref[l, rows - width :, :] = below
        tall_zone = self.zone_tall[l]
        perm = lookup(tall_zone, table, 0)
        self.perm_tall[l] = perm
        self.perm[l] = self.narrow(perm)
        zone = self.narrow(tall_zone)
        self.zone[l] = zone
        lame, shear = lookup(zone, table, 1), lookup(zone, table, 2)
        self.heft[l] = lame + shear
        self.shear[l] = shear
        self.fixed[l] = fixed_term(zone, lame, shear)


def new_brick(peers, nx, ny):
    domain = Brick(dict(nx=nx, ny=ny, pair=peers[0] == 2))
    at = lax.axis_index("gx")
    domain.has_below = (at > 0).astype(jnp.int32)
    domain.has_above = (at < peers[0] - 1).astype(jnp.int32)
    return domain


FIRST_OUTS = ("motion", "z0", "p0", "zs") + PASSED
FIRST_SCRATCH = tuple(n for n, _ in ARRAYS if n not in FIRST_OUTS + ("ps",))


class Joined:
    def __init__(self, *refs):
        self.refs = refs
        self.at = self

    def __getitem__(self, index):
        first, *rest = index if isinstance(index, tuple) else (index,)
        for ref in self.refs:
            if first < ref.shape[0]:
                return ref[first, *rest] if rest else ref.at[first]
            first -= ref.shape[0]

    def __setitem__(self, index, value):
        self[index[0]][index[1:]] = value


def brick_first(peers, *refs):
    table, fields, below, above = refs[:4]
    rows = [Rows(*refs[i : i + 2], peers) for i in (4, 6, 8)]
    outs = refs[10 : 10 + len(FIRST_OUTS)]
    ps, *scratch = refs[10 + len(FIRST_OUTS) :]
    _, nx, ny, nz = fields.shape
    domain = new_brick(peers, nx, ny)
    domain.__dict__.update(zip(FIRST_OUTS, outs))
    domain.__dict__.update(zip(FIRST_SCRATCH, scratch))
    domain.zone_tall, domain.perm_tall, domain.face_sum = scratch[len(FIRST_SCRATCH) :]
    domain.ps = Joined(ps)

    empty = jnp.zeros((ny + TILE, nz), jnp.float32)
    for l in (W - 1, W + nx):
        for name in ("perm", "heft", "shear", "press", "z0", "p0"):
            getattr(domain, name)[l] = empty
        for c in range(3):
            domain.motion[c, l] = empty
        for i in range(9):
            domain.zs[i, l] = empty
        for i in range(ps.shape[0]):
            ps[i, l] = empty
        domain.perm_tall[l] = jnp.zeros((ny + 2 * TILE, nz), jnp.float32)

    for x in range(nx):
        domain.assemble(W + x, x, fields, lambda f, x=x: rows[0].read(f, x), table)
    if domain.pair:
        upper = lax.axis_index("gx") > 0
        for u in range(W):

            def beside(f, u=u):
                ending, starting = rows[1].read(f, nx - W + u), rows[1].read(f, u)
                return [jnp.where(upper, a, b) for a, b in zip(ending, starting)]

            l = jnp.where(upper, u, W + nx + u)
            x = jnp.where(upper, nx - W + u, u)
            domain.assemble(l, x, below, beside, table)
    else:
        keep_below, keep_above = keeps("gx", peers[0])
        for u in range(W):
            x = nx - W + u
            domain.assemble(u, x, below, lambda f, x=x: rows[1].read(f, x), table, keep_below)
            l = W + nx + u
            domain.assemble(l, u, above, lambda f, u=u: rows[2].read(f, u), table, keep_above)
    domain.first_half()


SECOND_INS = ("z0", "p0", "zs") + PASSED


def brick_second(peers, nx, ny, *refs):
    domain = new_brick(peers, nx, ny)
    domain.__dict__.update(zip(SECOND_INS, refs))
    ready, *made, acc = refs[len(SECOND_INS) :]
    domain.ps = Joined(ready, *made)
    nz = ready.shape[3]
    empty = jnp.zeros((ny + TILE, nz), jnp.float32)
    for ps in made:
        for l in (W - 1, W + nx):
            for i in range(ps.shape[0]):
                ps[i, l] = empty
    domain.second_half()
    acc[...] = jnp.zeros(acc.shape, jnp.float32)
    domain.loop(W, nx, lambda l: domain.finish(l, acc, None), "finish")
    if nz == LANES:
        column = iota((TILE, LANES), 1)
        mask = (column >= W) & (column < nz - W)
        for i in range(SUMS):
            acc[i] = jnp.where(mask, acc[i], 0.0)


class Ends(Domain):
    def roll(self, v, shift):
        return pltpu.roll(v, shift % LANES, v.ndim - 1)

    def nxt(self, ref, l):
        moved = self.roll(ref[pl.ds(l.start, l.size + 1)], -self.row)
        lane = iota(moved[1:].shape, 2)
        return jnp.where(lane < LANES - self.row, moved[:-1], moved[1:])

    def before(self, v):
        moved = self.roll(v, self.row)
        back = jnp.concatenate([jnp.zeros_like(moved[:1]), moved[:-1]], axis=0)
        return jnp.where(iota(moved.shape, 2) >= self.row, moved, back)

    def prv(self, ref, l):
        return self.before(ref[l])

    def back_x(self, values, again):
        return [self.before(value) - value for value in values]

    def yp(self, v):
        return self.roll(v, -1)

    def ym(self, v):
        return self.roll(v, 1)

    def zp(self, v):
        return pltpu.roll(v, v.shape[1] - 1, 1)

    def zm(self, v):
        return pltpu.roll(v, 1, 1)

    def y_sum(self, l):
        face = self.ty[l]
        return face + self.ym(face)

    def near_faces(self, shape):
        row = iota(shape, len(shape) - 1) % self.row
        return (row >= TILE - 1) & (row < self.row - TILE)

    def own(self, v):
        return v

    def fold(self, value, mask):
        total = None
        for g in range(value.shape[0]):
            part = jnp.where(mask, value[g], 0.0)
            for start in range(0, value.shape[1], TILE):
                piece = part[start : start + TILE]
                total = piece if total is None else total + piece
        return total

    def run(self, halo, body, stage, before=0):
        body(pl.ds(0, self.groups))

    def assemble(self, peers, ends, messages, table):
        keep = keeps("gz", peers[2])
        for g in range(self.groups):
            for f in range(NF):
                self.raw[f, g] = ends[f, g]

        def halo(message, side, base, keep):
            for g in range(self.groups):
                for f in range(NF):
                    width, offset = WIDTHS[f], OFFSETS[f]
                    start = base + (SEG - W if side else W - width)
                    self.raw[f, g, start : start + width, :] = (
                        message[g, offset : offset + width, :] * keep
                    )

        if sides_of(peers) == 1:
            first = lax.axis_index("gx") == 0
            pl.when(first)(lambda: halo(messages[0], 0, 0, keep[0]))
            pl.when(jnp.logical_not(first))(lambda: halo(messages[0], 1, 0, keep[1]))
        else:
            halo(messages[0], 0, 0, keep[0])
            halo(messages[1], 1, SEG, keep[1])
        for g in range(self.groups):
            zone = self.raw[ZONE, g]
            lame, shear = lookup(zone, table, 1), lookup(zone, table, 2)
            self.perm[g] = lookup(zone, table, 0)
            self.heft[g] = lame + shear
            self.shear[g] = shear
            self.fixed[g] = fixed_term(zone, lame, shear)


class Either:
    def __init__(self, condition, yes, no):
        self.condition, self.refs = condition, (yes, no)

    def __getitem__(self, index):
        return jnp.where(self.condition, *[ref[index] for ref in self.refs])


def own_groups(count, peers):
    return count * blocks_of(peers)[0][0]


def ends_kernel(peers, tall, *refs):
    sides = sides_of(peers)
    table, ends, *messages = refs[: 2 + sides]
    added, out, partial, raw, acc, *scratch = refs[2 + sides :]
    names = [name for name, _ in ARRAYS[6:] if name not in KEPT]
    domain = Ends(dict(zip(names, scratch)))
    domain.raw = raw
    kept = {n: out.at[ENDS_START[n] : ENDS_START[n] + k] for n, k in ENDS_KEPT}
    domain.z0, domain.p0 = out.at[ENDS_START["z0"]], out.at[ENDS_START["p0"]]
    domain.zs, domain.ps = kept["zs"], kept["ps"]
    domain.zone, domain.press = raw.at[ZONE], raw.at[PRESS]
    domain.motion = raw.at[MOTION : MOTION + 3]
    domain.load, domain.drain = raw.at[SOURCE], raw.at[DRAIN]
    domain.body = raw.at[BODY : BODY + 3]
    domain.row = tall
    domain.groups = groups = raw.shape[1] - 1
    columns = raw.shape[2]
    empty = jnp.zeros((columns, LANES), jnp.float32)
    for ref in (raw, out):
        for i in range(ref.shape[0]):
            ref[i, groups] = empty
    for ref in (domain.perm, domain.shear):
        ref[groups] = empty
    domain.assemble(peers, ends, messages, table)
    domain.stages()
    for g in range(groups):
        for i in range(4):
            out[i, g] = raw[PRESS + i, g]
    acc[...] = added[...]
    shape = (columns, LANES)
    column, row = iota(shape, 0), iota(shape, 1) % tall
    if sides == 1:
        start = jnp.where(lax.axis_index("gx") == 0, W, SEG - 2 * W)
        at_end = (column >= start) & (column < start + W)
        mine = pl.ds(0, groups)
    else:
        inner = column % SEG
        start = jnp.where(column < SEG, W, SEG - 2 * W)
        at_end = (inner >= start) & (inner < start + W)
        count = groups // len(blocks_of(peers))
        mine = pl.ds(own_groups(count, peers), count)
    mask = at_end & (row >= TILE) & (row < tall - TILE)
    domain.finish(mine, acc, mask)

    sums = jnp.concatenate(
        [jnp.sum(acc[i], axis=0, keepdims=True) for i in range(acc.shape[0])], axis=0
    )
    totals = jnp.sum(sums, axis=1, keepdims=True)
    spread = jnp.where(iota(sums.shape, 0) == iota(sums.shape, 1), totals, 0.0)
    line = jnp.sum(spread, axis=0, keepdims=True)
    partial[...] = jnp.broadcast_to(line, partial.shape)


def step_sizes(gamma, delta, cross, energy):
    first = gamma / delta
    gamma_new = gamma - 2.0 * first * delta + first * first * cross
    curved = delta - 2.0 * first * cross + first * first * energy
    ratio = gamma_new / gamma
    second = gamma_new / (curved - ratio * gamma_new / first)
    return first + second * (1.0 + ratio), -first * second


def combine(peers, tall, *refs):
    pair = sides_of(peers) == 1
    sums, (old, z0, p0, zs) = refs[0], refs[1:5]
    *ps, fields, own_ends, other_ends = refs[5:-6] if pair else refs[5:-6] + refs[-7:-6]
    ps = Joined(*ps)
    pressure, motion, strain, moved, ends_moved, turned = refs[-6:]
    if pair:
        first = lax.axis_index("gx") == 0
        halves = (Either(first, own_ends, other_ends), Either(first, other_ends, own_ends))

    def end_of(side, i, g):
        if pair:
            return halves[side][i, g]
        return own_ends[i, g, side * SEG : (side + 1) * SEG, :]

    line = jnp.sum(sums[...], axis=0, keepdims=True)
    lane = iota(line.shape, 1)

    def value(index):
        return jnp.sum(jnp.where(lane == index, line, 0.0), axis=1, keepdims=True)

    c1, c2 = step_sizes(*[value(i) for i in range(4)])
    weights = (jnp.ones_like(c1), c1, c2)

    def form(start):
        total = 0.0
        for i, (j, k) in enumerate(PAIRS):
            scale = 1.0 if j == k else 2.0
            total = total + scale * weights[j] * weights[k] * value(start + i)
        return total

    d1, d2 = step_sizes(form(4), form(10), form(16), form(22))
    on_z = [d1 * w for w in weights]
    on_p = [d2 * w for w in weights]

    def new_motion(start, z_part, p_part, c):
        total = start
        for j in range(3):
            total = total + on_z[j] * z_part(3 * j + c)
            total = total + on_p[j] * p_part(3 * j + c)
        return total

    nx, ny, nz = pressure.shape
    pack = LANES // tall
    ends = Ends(dict(row=tall))
    groups = own_ends.shape[1] - 1
    count = groups // len(blocks_of(peers))
    mine = own_groups(count, peers)
    every = pl.ds(0, groups)
    if pair:
        every = pl.ds(lax.axis_index("gx") * (count - 1), count + 1)
    empty = jnp.zeros((SEG, LANES), jnp.float32)
    start = ENDS_START
    for side in range(2):
        for c in range(3):
            for i in range(every.size):
                g = every.start + i
                ends_moved[side, c, g] = new_motion(
                    end_of(side, start["motion"] + c, g),
                    lambda k, side=side, g=g: end_of(side, start["zs"] + k, g),
                    lambda k, side=side, g=g: end_of(side, start["ps"] + k, g),
                    c,
                )
            ends_moved[side, c, every.start + every.size] = empty
        along_y, along_z = ends_moved[side, 1, every], ends_moved[side, 2, every]
        along_x = ends_moved.at[side, 0]
        ends_moved[side, 3, every] = 0.5 * (
            (ends.nxt(along_x, every) - ends.prv(along_x, every))
            + (ends.yp(along_y) - ends.ym(along_y))
            + (ends.zp(along_z) - ends.zm(along_z))
        )
    for c in range(3):
        around = 1 if c == 0 else 0
        for l in range(W - around, W + nx + around):
            moved[c, l] = new_motion(
                old[c, l], lambda k, l=l: zs[k, l], lambda k, l=l: ps[k, l], c
            )
    brick = Brick({})
    outs = [pressure] + [motion.at[c] for c in range(3)] + [strain]
    for g in range(count):
        at = mine + g
        flipped = []
        for o in range(len(outs)):
            slot = g * len(outs) + o
            for side, (row, first_row) in enumerate(((0, W), (LANES - W, SEG - 2 * W))):
                if o == 0:
                    edge = end_of(side, start["press"], at)
                    edge = edge + c1 * end_of(side, start["z0"], at)
                    edge = edge + c2 * end_of(side, start["p0"], at)
                else:
                    edge = ends_moved[side, o - 1, at]
                turned[slot, row : row + W, :] = edge[first_row : first_row + W]
            flipped.append(turned[slot].T)
        for i in range(pack):
            x = g * pack + i
            l = W + x
            top = i * tall + TILE
            column = iota((ny, LANES), 1)
            u = [moved[c, l] for c in range(3)]
            change = (
                (moved[0, l + 1] - moved[0, l - 1])
                + (brick.yp(u[1]) - brick.ym(u[1]))
                + (brick.zp(u[2]) - brick.zm(u[2]))
            )
            results = [fields[PRESS, x] + c1 * z0[l, :ny, :] + c2 * p0[l, :ny, :]]
            results = results + [v[:ny] for v in u] + [0.5 * change[:ny]]
            for out, result, edge in zip(outs, results, flipped):
                edge = edge[top : top + ny]
                if nz == LANES:
                    inner = (column >= W) & (column < LANES - W)
                    out[x] = jnp.where(inner, result, edge)
                else:
                    out[x] = result
                    out[x, :, :LANES] = jnp.where(column >= W, result[:, :LANES], edge)
                    out[x, :, nz - LANES :] = jnp.where(
                        column < LANES - W, result[:, nz - LANES :], edge
                    )


def f32(*shape):
    return jax.ShapeDtypeStruct(shape, jnp.float32)


def vmem(*shape):
    return pltpu.VMEM(shape, jnp.float32)


def call(kernel, outs, *args, unread=0, space=pltpu.VMEM, scratch=(), limit=8, cost=None):
    specs = [
        pl.BlockSpec(memory_space=space if i < len(args) - unread else pl.ANY)
        for i in range(len(args))
    ]
    return pl.pallas_call(
        kernel,
        out_shape=outs,
        in_specs=specs,
        scratch_shapes=scratch,
        cost_estimate=cost,
        compiler_params=pltpu.CompilerParams(vmem_limit_bytes=limit * MIB),
    )(*args)


def ring(value, axis, step):
    peers = lax.axis_size(axis)
    return lax.ppermute(value, axis, [(i, (i + step) % peers) for i in range(peers)])


def pairs(value, axis, start):
    peers = lax.axis_size(axis)
    swaps = [(i, i) for i in range(start)]
    for i in range(start, peers - 1, 2):
        swaps += [(i, i + 1), (i + 1, i)]
    swaps += [(i, i) for i in range(len(swaps), peers)]
    return lax.ppermute(value, axis, swaps)


def x_neighbours(value):
    peers = lax.axis_size("gx")
    above = ring(value, "gx", -1)
    below = above if peers == 2 else ring(value, "gx", 1)
    return below, above


def shards(
    source,
    pressure_old,
    strain_prev,
    motion_old,
    body_force,
    zone_ids,
    drained,
    perm_table,
    lame_table,
    shear_table,
):
    nx, ny, nz = source.shape
    peers = [lax.axis_size(a) for a in AXES]
    total = peers[0] * peers[1] * peers[2]
    pair = peers[0] == 2
    tall = ny + 2 * TILE
    groups = nx * tall // LANES

    def with_peers(kernel, *more):
        return lambda *refs: kernel(peers, *more, *refs)

    raw = (
        source,
        pressure_old,
        strain_prev,
        motion_old,
        body_force,
        zone_ids,
        drained,
    )
    raw = [pltpu.with_memory_space_constraint(a, pltpu.HBM) for a in raw]
    held = [pltpu.VMEM(a.shape, a.dtype) for a in raw]
    tables = [
        pltpu.with_memory_space_constraint(a, pltpu.HBM)
        for a in (perm_table, lame_table, shear_table)
    ]
    message = f32(up_to(nx * ROWS_EACH, TILE), nz)
    first, second, table = call(
        pack_rows,
        [message, message, f32(TILE, LANES)],
        *raw,
        *tables,
        space=pltpu.HBM,
        scratch=held
        + [pltpu.SMEM(a.shape, a.dtype) for a in tables]
        + [pltpu.SemaphoreType.DMA((len(raw) + len(tables),))],
    )
    (fields,) = call(
        pack_fields,
        [f32(NF, nx, ny, nz)],
        *raw,
        table,
        space=pltpu.HBM,
        unread=1,
        scratch=held + [pltpu.SemaphoreType.DMA((len(raw),))],
    )
    fields_below, fields_above = x_neighbours(fields)
    first = pairs(first, "gy", 0)
    second = pairs(second, "gy", 1)
    first_below, first_above = x_neighbours(first)
    second_below, second_above = x_neighbours(second)
    others = [
        (fields_below, first_below, second_below),
        (fields_above, first_above, second_above),
    ][: 1 if pair else 2]
    sides = 1 if pair else 2
    own_ends, *own_messages = call(
        with_peers(pack_own),
        [f32(NF, groups, sides * SEG, LANES)] + [f32(groups, MSG_ROWS, LANES)] * sides,
        fields,
        first,
        second,
        scratch=[vmem(NF * groups, LANES, nz)],
    )
    span = (1 + len(others)) * groups
    ends, *messages = call(
        with_peers(pack_others),
        [f32(NF, span, sides * SEG, LANES)] + [f32(span, MSG_ROWS, LANES)] * sides,
        own_ends,
        *own_messages,
        *[array for block in others for array in block],
        scratch=[vmem(NF * groups, LANES, nz)],
        limit=12,
    )
    if pair:
        n = peers[2]
        hops = [(i, (i + 1) % n) for i in range(n)]
        hops += [(n + i, n + (i - 1) % n) for i in range(n)]
        got = [lax.ppermute(messages[0], ("gx", "gz"), hops)]
    else:
        got = [ring(messages[0], "gz", 1), ring(messages[1], "gz", -1)]
    depth = nx + 2 * W
    cells = depth * ny * nz

    def shaped(lead, *shape):
        return (lead,) * (lead > 0) + shape

    leads = dict(ARRAYS)
    sums_shape = (up_to(SUMS, TILE), TILE, LANES)

    def layers_of(name):
        return shaped(leads[name], depth, ny + TILE, nz)

    *halves, ps = call(
        with_peers(brick_first),
        [f32(*layers_of(name)) for name in FIRST_OUTS]
        + [f32(3 * len(FIRST_IMAGES), depth, ny + TILE, nz)],
        table,
        fields,
        fields_below,
        fields_above,
        first,
        second,
        first_below,
        second_below,
        first_above,
        second_above,
        scratch=[vmem(*layers_of(name)) for name in FIRST_SCRATCH]
        + [vmem(depth, tall, nz), vmem(depth, tall, nz), vmem(depth, ny + TILE, nz)],
        limit=16,
    )
    half = dict(zip(FIRST_OUTS, halves))
    late = [f32(3 * len(SECOND_IMAGES), depth, ny + TILE, nz)] * bool(SECOND_IMAGES)
    *last, added = call(
        with_peers(brick_second, nx, ny),
        late + [f32(*sums_shape)],
        *[half[name] for name in SECOND_INS],
        ps,
    )
    kept = [half[name] for name in KEPT[:-1]] + [ps, *last]
    span, columns = span + 1, sides * SEG
    ends_kept, partial = call(
        with_peers(ends_kernel, tall),
        [f32(ENDS_ARRAYS, span, columns, LANES), f32(total, LANES)],
        table,
        ends,
        *got,
        added,
        scratch=[vmem(NF, span, columns, LANES), vmem(*sums_shape)]
        + [
            vmem(*shaped(lead, span, columns, LANES))
            for name, lead in ARRAYS[6:]
            if name not in KEPT
        ],
        limit=16,
    )
    both = [ends_kept]
    if pair:
        both.append(ring(ends_kept, "gx", -1))
    sums = lax.all_to_all(partial, AXES, 0, 0, tiled=True)
    return tuple(
        call(
            with_peers(combine, tall),
            [f32(nx, ny, nz), f32(3, nx, ny, nz), f32(nx, ny, nz)],
            sums,
            *kept,
            fields,
            *both,
            scratch=[
                vmem(3, depth, ny + TILE, nz),
                vmem(2, 4, span, SEG, LANES),
                vmem(5 * groups, LANES, LANES),
            ],
            limit=16,
        )
    )


def solution(mesh):
    placed = (
        P("gx", "gy", "gz"),
        P("gx", "gy", "gz"),
        P("gx", "gy", "gz"),
        P(None, "gx", "gy", "gz"),
        P(None, "gx", "gy", "gz"),
        P("gx", "gy", "gz"),
        P("gx", "gy", "gz"),
        P(),
        P(),
        P(),
    )
    return jax.shard_map(
        shards,
        mesh=mesh,
        in_specs=placed,
        out_specs=(P("gx", "gy", "gz"), P(None, "gx", "gy", "gz"), P("gx", "gy", "gz")),
        check_vma=False,
    )
```

```python
import jax
import jax.numpy as jnp
from jax import lax
from jax.experimental import pallas as pl
from jax.experimental.pallas import tpu as pltpu
from jax.sharding import PartitionSpec as P


ZONES = 8

storage = 0.2
biot_coef = 0.8
leakage = 2.0
support = 1.0

AXES = ("gx", "gy", "gz")
LANES = 128
TILE = 8
MIB = 2**20

ZONE, PRESS, MOTION, SOURCE, DRAIN, BODY = 0, 1, 2, 5, 6, 7
WIDTHS = (5, 5, 5, 5, 5, 4, 4, 2, 2, 2)
NF = len(WIDTHS)
W = max(WIDTHS)
OFFSETS = tuple(sum(WIDTHS[:f]) for f in range(NF))
ROW_WIDTHS = (5, 4, 4, 3, 4, 4, 4, 2, 2, 2)
ROW_OFFSETS = tuple(sum(ROW_WIDTHS[:f]) for f in range(NF))
ROWS_EACH = sum(ROW_WIDTHS)
PAIRS = tuple((j, k) for j in range(3) for k in range(j, 3))
SUMS = 4 + 4 * len(PAIRS)
SEG = 16
ENDS_KEPT = (("press", 1), ("motion", 3), ("z0", 1), ("p0", 1), ("zs", 9), ("ps", 9))
ENDS_ARRAYS = sum(count for _, count in ENDS_KEPT)
ENDS_START = dict(press=0, motion=1, z0=4, p0=5, zs=6, ps=15)
UNROLL = dict(faces=8, start=8, next=8, shear=8, motion=8, image=3, finish=8)


def up_to(value, multiple):
    return -(-value // multiple) * multiple


MSG_ROWS = up_to(sum(WIDTHS), TILE)


def iota(shape, dim):
    return lax.broadcasted_iota(jnp.int32, shape, dim)


def field_of(raw, f, at):
    source, pressure, strain, motion, body, zones, drained = raw
    if f == ZONE:
        return zones[at].astype(jnp.float32) + 1.0
    if f == PRESS:
        return pressure[at]
    if f == SOURCE:
        return source[at] + biot_coef * strain[at]
    if f == DRAIN:
        return drained[at].astype(jnp.float32)
    return motion[f - MOTION, *at] if f < SOURCE else body[f - BODY, *at]


class Fetch:
    def __init__(self, sources, held, arrived):
        self.held = held
        self.copies = [
            pltpu.make_async_copy(source, copy, arrived.at[i])
            for i, (source, copy) in enumerate(zip(sources, held))
        ]
        self.waiting = set(range(len(held)))
        for i in sorted(self.waiting, key=lambda i: FETCH_ORDER.index(i)):
            self.copies[i].start()

    def need(self, *which):
        for i in which:
            if i in self.waiting:
                self.waiting.remove(i)
                self.copies[i].wait()


FETCH_ORDER = (5, 1, 3, 0, 2, 6, 4, 7, 8, 9)
NEEDS = ((5,), (1,), (3,), (3,), (3,), (0, 2), (6,), (4,), (4,), (4,))


def pack_rows(*refs):
    sources, (first, second, table), held, arrived = refs[:10], refs[10:13], refs[13:23], refs[23]
    fetch = Fetch(sources, held, arrived)
    raw, tables = held[:7], held[7:]
    nx, ny, nz = raw[0].shape
    even = lax.axis_index("gy") % 2 == 0
    fetch.need(7, 8, 9)
    shape = (TILE, LANES)
    tile = jnp.zeros(shape, jnp.float32)
    for t in range(len(tables)):
        for zone in range(ZONES):
            here = (iota(shape, 0) == t) & (iota(shape, 1) == zone + 1)
            tile = jnp.where(here, tables[t][zone], tile)
    table[...] = tile
    inner = iota((ny, nz), 0) < ny - 1
    for f in range(NF):
        width = ROW_WIDTHS[f]
        fetch.need(*NEEDS[f])
        for x in range(nx):
            at = (x, slice(None))
            value = field_of(raw, f, at)
            if f == SOURCE:
                zone, press, middle = [field_of(raw, g, at) for g in (ZONE, PRESS, MOTION + 1)]
                perm = lookup(zone, tile, 0)
                face = jnp.where(inner, harmonic(perm, rows_up(perm)), 0.0)
                value = value - y_part(face, press, middle, inner)
            upward, downward = value[ny - width :], value[:width]
            start = x * ROWS_EACH + ROW_OFFSETS[f]
            first[start : start + width, :] = jnp.where(even, upward, downward)
            second[start : start + width, :] = jnp.where(even, downward, upward)
    used = nx * ROWS_EACH
    for ref in (first, second):
        if ref.shape[0] > used:
            ref[used:, :] = jnp.zeros((ref.shape[0] - used, nz), jnp.float32)


def rows_up(v):
    return pltpu.roll(v, v.shape[0] - 1, 0)


def rows_down(v):
    return pltpu.roll(v, 1, 0)


def y_part(face, press, middle, marked, up=rows_up, down=rows_down):
    step = jnp.where(marked, face * (up(press) - press), 0.0)
    change = jnp.where(marked, up(middle), 0.0) - down(jnp.where(marked, middle, 0.0))
    return (down(step) - step) + (0.5 * biot_coef) * change


def pack_fields(*refs):
    sources, fields, held, arrived = refs[:7], refs[8], refs[9:16], refs[16]
    fetch = Fetch(sources, held, arrived)
    for f in range(NF):
        fetch.need(*NEEDS[f])
        for x in range(fields.shape[1]):
            fields[f, x] = field_of(held, f, (x, slice(None)))


def keeps(axis, peers):
    at = lax.axis_index(axis)
    return jnp.where(at > 0, 1.0, 0.0), jnp.where(at < peers - 1, 1.0, 0.0)


def blocks_of(peers):
    at = lax.axis_index("gx")
    if peers[0] == 2:
        return [(at, 1.0), (1 - at, 1.0)]
    keep_below, keep_above = keeps("gx", peers[0])
    return [(1, 1.0), (0, keep_below), (2, keep_above)]


class Rows:
    def __init__(self, first, second, peers):
        self.refs = first, second
        self.even = lax.axis_index("gy") % 2 == 0
        self.keep = keeps("gy", peers[1])

    def read(self, f, x):
        start = x * ROWS_EACH + ROW_OFFSETS[f]
        a, b = [ref[start : start + ROW_WIDTHS[f], :] for ref in self.refs]
        low, high = jnp.where(self.even, b, a), jnp.where(self.even, a, b)
        return low * self.keep[0], high * self.keep[1]


def keeps(axis, peers):
    at = lax.axis_index(axis)
    return jnp.where(at > 0, 1.0, 0.0), jnp.where(at < peers - 1, 1.0, 0.0)


def block_ends(peers, keep, fields, first, second, stage, put):
    _, nx, ny, nz = fields.shape
    tall = ny + 2 * TILE
    pack = LANES // tall
    count = nx // pack
    gap = jnp.zeros((TILE, nz), jnp.float32)
    rows = Rows(first, second, peers)
    for g in range(count):
        for f in range(NF):
            width = ROW_WIDTHS[f]
            slot = g * NF + f
            for p in range(pack):
                x = g * pack + p
                top = p * tall
                stage[slot, top : top + TILE, :] = gap
                stage[slot, top + TILE + ny : top + tall, :] = gap
                stage[slot, top + TILE : top + TILE + ny, :] = fields[f, x]
                low, high = rows.read(f, x)
                stage[slot, top + TILE - width : top + TILE, :] = low
                stage[slot, top + TILE + ny : top + TILE + ny + width, :] = high
            begin = stage[slot, :, :LANES].T
            finish = begin if nz == LANES else stage[slot, :, nz - LANES :].T
            if not isinstance(keep, float):
                begin, finish = begin * keep, finish * keep
            put(f, g, begin, finish)


def sides_of(peers):
    return 1 if peers[0] == 2 else 2


def put_ends(peers, ends, f, g, begin, finish):
    row = iota((SEG, LANES), 0)
    left = pltpu.roll(begin[:SEG], W, 0)
    right = pltpu.roll(finish[LANES - SEG :], SEG - W, 0)
    left = jnp.where(row >= W, left, 0.0)
    right = jnp.where(row < SEG - W, right, 0.0)
    if sides_of(peers) == 1:
        ends[f, g] = jnp.where(lax.axis_index("gx") == 0, left, right)
    else:
        ends[f, g, :SEG, :] = left
        ends[f, g, SEG:, :] = right


def put_message(peers, messages, f, g, begin, finish):
    rows = slice(OFFSETS[f], OFFSETS[f] + WIDTHS[f])
    rightward, leftward = finish[LANES - WIDTHS[f] :], begin[: WIDTHS[f]]
    if peers[0] == 2:
        first = lax.axis_index("gx") == 0
        messages[0][g, rows, :] = jnp.where(first, rightward, leftward)
    else:
        messages[0][g, rows, :] = rightward
        messages[1][g, rows, :] = leftward


def pack_own(peers, fields, first, second, ends, *refs):
    *messages, stage = refs

    def put(f, g, begin, finish):
        put_ends(peers, ends, f, g, begin, finish)
        put_message(peers, messages, f, g, begin, finish)

    for message in messages:
        message[:, MSG_ROWS - TILE :, :] = jnp.zeros(
            (message.shape[0], TILE, LANES), jnp.float32
        )
    block_ends(peers, 1.0, fields, first, second, stage, put)


def pack_others(peers, *refs):
    blocks = blocks_of(peers)
    sides = 1 if peers[0] == 2 else 2
    own_ends, own = refs[0], refs[1 : 1 + sides]
    others = refs[1 + sides : 1 + sides + 3 * (len(blocks) - 1)]
    ends, *messages, stage = refs[1 + sides + 3 * (len(blocks) - 1) :]
    count = own_ends.shape[1]
    mine = blocks[0][0] * count
    for g in range(count):
        for f in range(NF):
            ends[f, mine + g] = own_ends[f, g]
        for message, part in zip(messages, own):
            message[mine + g] = part[g]
    for b, (start, keep) in enumerate(blocks[1:]):

        def put(f, g, begin, finish, start=start):
            put_ends(peers, ends, f, start * count + g, begin, finish)
            put_message(peers, messages, f, start * count + g, begin, finish)

        for message in messages:
            for g in range(count):
                message[start * count + g, MSG_ROWS - TILE :, :] = jnp.zeros(
                    (TILE, LANES), jnp.float32
                )
        block_ends(peers, keep, *others[3 * b : 3 * b + 3], stage, put)


def times(value, factor):
    return value if factor == 1.0 else factor * value


def harmonic(a, b):
    return 2.0 * a * b / jnp.maximum(a + b, 1e-30)


def lookup(zone, table, row):
    entries = jnp.broadcast_to(table[row : row + 1, :], zone.shape[:-1] + (LANES,))
    index = zone.astype(jnp.int32)
    picked = [
        jnp.take_along_axis(
            entries, index[:, start : start + LANES], axis=1, mode="promise_in_bounds"
        )
        for start in range(0, zone.shape[1], LANES)
    ]
    return picked[0] if len(picked) == 1 else jnp.concatenate(picked, axis=1)


def fixed_term(zone, lame, shear):
    scale = jnp.maximum(lame + 2.0 * shear / 3.0, 1e-30)
    return jnp.where(zone > 0.0, biot_coef * biot_coef / scale, 0.0)


KEPT = ("motion", "z0", "p0", "zs", "ps")
ARRAYS = (
    ("zone", 0),
    ("press", 0),
    ("motion", 3),
    ("load", 0),
    ("drain", 0),
    ("body", 3),
    ("perm", 0),
    ("heft", 0),
    ("shear", 0),
    ("fixed", 0),
    ("tx", 0),
    ("ty", 0),
    ("tz", 0),
    ("mx", 0),
    ("my", 0),
    ("mz", 0),
    ("react", 0),
    ("pdiag", 0),
    ("pinv", 0),
    ("z0", 0),
    ("p0", 0),
    ("ediag", 3),
    ("einv", 3),
    ("zs", 9),
    ("ps", 9),
)


class Domain:
    def __init__(self, arrays):
        self.__dict__.update(arrays)

    def press_faces(self, l):
        own = self.perm[l]
        self.tx[l] = harmonic(own, self.nxt(self.perm, l))
        self.ty[l] = harmonic(own, self.yp(own))
        self.tz[l] = harmonic(own, self.zp(own))

    def motion_faces(self, l):
        own = self.shear[l]
        self.mx[l] = harmonic(own, self.nxt(self.shear, l))
        self.my[l] = harmonic(own, self.yp(own))
        self.mz[l] = harmonic(own, self.zp(own))

    def steps(self, ref, l):
        own = ref[l]
        return self.nxt(ref, l) - own, self.yp(own) - own, self.zp(own) - own

    def back_y(self, value):
        return self.ym(value) - value

    def back_z(self, value):
        return self.zm(value) - value

    def press_flux(self, ref, l, along_y=True):
        dx, dy, dz = self.steps(ref, l)
        (part,) = self.back_x(
            [self.tx[l] * dx],
            lambda: [self.tx[l - 1] * (ref[l] - ref[l - 1])],
        )
        total = part + self.back_z(self.tz[l] * dz)
        return total + self.back_y(self.ty[l] * dy) if along_y else total

    def y_terms(self, l):
        face = self.ty[l]
        marked = self.near_faces(face.shape)
        part = y_part(face, self.press[l], self.motion[1, l], marked, self.yp, self.ym)
        return self.y_sum(l), part

    def press_start(self, l):
        face_sum, y_part = self.y_terms(l)
        face = self.tz[l]
        leak = leakage * self.drain[l]
        reaction = storage + self.fixed[l] + leak
        diag = (
            reaction
            + self.tx[l]
            + self.prv(self.tx, l)
            + face_sum
            + (face + self.zm(face))
        )
        inverse = jnp.where(self.zone[l] > 0.0, 1.0 / diag, 0.0)
        along_x, along_z = self.motion.at[0], self.motion[2, l]
        change = (self.nxt(along_x, l) - self.prv(along_x, l)) + (
            self.zp(along_z) - self.zm(along_z)
        )
        residual = (
            self.load[l]
            - (0.5 * biot_coef) * change
            - leak * self.press[l]
            - self.press_flux(self.press, l, False)
            - y_part
        )
        self.react[l] = reaction
        self.pdiag[l] = diag
        self.pinv[l] = inverse
        self.z0[l] = residual * inverse

    def press_next(self, l):
        image = self.react[l] * self.z0[l] + self.press_flux(self.z0, l)
        self.p0[l] = image * self.pinv[l]

    @staticmethod
    def parts(ref, j):
        return [ref.at[3 * j + c] for c in range(3)]

    def elastic(self, refs, l):
        steps = [self.steps(ref, l) for ref in refs]
        pushed = self.heft[l] * (steps[0][0] + steps[1][1] + steps[2][2])
        face = self.mx[l]
        along_x = [face * steps[c][0] for c in range(3)]
        along_x[0] = along_x[0] + pushed
        parts_x = self.back_x(along_x, lambda: self.motion_fluxes(refs, l - 1))
        out = []
        for c in range(3):
            _, dy, dz = steps[c]
            step_y, step_z = self.my[l] * dy, self.mz[l] * dz
            if c == 1:
                step_y = step_y + pushed
            if c == 2:
                step_z = step_z + pushed
            out.append(
                times(refs[c][l], support)
                + parts_x[c]
                + self.back_y(step_y)
                + self.back_z(step_z)
            )
        return out

    def motion_fluxes(self, refs, l):
        a, b, c = [ref[l] for ref in refs]
        steps = [self.nxt(ref, l) - own for ref, own in zip(refs, (a, b, c))]
        face = self.mx[l]
        pushed = self.heft[l] * (steps[0] + (self.yp(b) - b) + (self.zp(c) - c))
        return [face * steps[0] + pushed, face * steps[1], face * steps[2]]

    def gradient(self, ref, l):
        own = ref[l]
        return (
            self.nxt(ref, l) - self.prv(ref, l),
            self.yp(own) - self.ym(own),
            self.zp(own) - self.zm(own),
        )

    def motion_start(self, l):
        weight = self.heft[l]
        along_y, along_z = self.my[l], self.mz[l]
        base = (
            support
            + self.mx[l]
            + self.prv(self.mx, l)
            + (along_y + self.ym(along_y))
            + (along_z + self.zm(along_z))
            + weight
        )
        inside = self.zone[l] > 0.0
        beside = (self.prv(self.heft, l), self.ym(weight), self.zm(weight))
        image = self.elastic(self.parts(self.motion, 0), l)
        grads = [self.gradient(ref, l) for ref in (self.press, self.z0, self.p0)]
        for c in range(3):
            diag = base + beside[c]
            inverse = jnp.where(inside, 1.0 / diag, 0.0)
            self.ediag[c, l] = diag
            self.einv[c, l] = inverse
            start = self.body[c, l] - (0.5 * biot_coef) * grads[0][c] - image[c]
            self.zs[c, l] = start * inverse
            scale = (-0.5 * biot_coef) * inverse
            self.zs[3 + c, l] = grads[1][c] * scale
            self.zs[6 + c, l] = grads[2][c] * scale

    def motion_next(self, l, j):
        image = self.elastic(self.parts(self.zs, j), l)
        for c in range(3):
            self.ps[3 * j + c, l] = image[c] * self.einv[c, l]

    def stages(self):
        self.run(4, self.press_faces, "faces", 1)
        self.run(4, self.press_start, "start")
        self.run(3, self.press_next, "next")
        self.run(2, self.motion_faces, "shear", 1)
        self.run(2, self.motion_start, "motion")
        for j in range(3):
            self.run(1, lambda l: self.motion_next(l, j), "image")

    def finish(self, l, acc, mask):
        own = self.own

        def add(index, value):
            acc[index] = acc[index] + self.fold(value, mask)

        def total(pairs):
            out = None
            for a, b in pairs:
                out = a * b if out is None else out + a * b
            return out

        a, b = own(self.z0[l]), own(self.p0[l])
        diag = own(self.pdiag[l])
        scaled = diag * b
        add(0, diag * a * a)
        add(1, scaled * a)
        add(2, scaled * b)
        energy = own(self.react[l]) * b * b
        for face, step in zip((self.tx, self.ty, self.tz), self.steps(self.p0, l)):
            step = own(step)
            energy = energy + own(face[l]) * step * step
        add(3, energy)
        diags = [own(self.ediag[c, l]) for c in range(3)]
        faces = [own(ref[l]) for ref in (self.mx, self.my, self.mz)]
        weight = own(self.heft[l])
        za, pa, dz, dp, steps, heavy = [], [], [], [], [], []
        for j in range(3):
            zj, pj = self.parts(self.zs, j), self.parts(self.ps, j)
            za.append([own(ref[l]) for ref in zj])
            pa.append([own(ref[l]) for ref in pj])
            dz.append([d * v for d, v in zip(diags, za[j])])
            dp.append([d * v for d, v in zip(diags, pa[j])])
            moved = [[own(v) for v in self.steps(ref, l)] for ref in pj]
            div = moved[0][0] + moved[1][1] + moved[2][2]
            flat = [(faces[d], moved[c][d]) for c in range(3) for d in range(3)]
            steps.append([v for _, v in flat] + [div] + pa[j])
            heavy.append([f * v for f, v in flat] + [weight * div])
            heavy[j] = heavy[j] + [times(v, support) for v in pa[j]]
        for i, (j, k) in enumerate(PAIRS):
            add(4 + i, total(zip(dz[j], za[k])))
            add(10 + i, total(zip(dp[k], za[j])))
            add(16 + i, total(zip(dp[j], pa[k])))
            add(22 + i, total(zip(heavy[j], steps[k])))

    def loop(self, start, count, body, stage):
        unroll = 1
        if isinstance(count, int):
            unroll = -(-count // -(-count // UNROLL[stage]))
        chunks = count // unroll

        def step(i, carry):
            self.carried = None
            for u in range(unroll):
                body(start + i * unroll + u)
            return carry

        if isinstance(chunks, int) and chunks == 1:
            step(0, 0)
        else:
            lax.fori_loop(0, chunks, step, 0)
            self.carried = None
        if isinstance(count, int):
            for u in range(chunks * unroll, count):
                body(start + u)


class Brick(Domain):
    def nxt(self, ref, l):
        return ref[l + 1]

    def prv(self, ref, l):
        return ref[l - 1]

    def yp(self, v):
        return pltpu.roll(v, v.shape[0] - 1, 0)

    def ym(self, v):
        return pltpu.roll(v, 1, 0)

    def zp(self, v):
        return pltpu.roll(v, v.shape[1] - 1, 1)

    def zm(self, v):
        return pltpu.roll(v, 1, 1)

    def back_x(self, values, again):
        before = again() if self.carried is None else self.carried
        self.carried = values
        return [a - b for a, b in zip(before, values)]

    def own(self, v):
        return v[: self.ny]

    def fold(self, value, mask):
        total = value[:TILE]
        for start in range(TILE, value.shape[0], TILE):
            total = total + value[start : start + TILE]
        nz = value.shape[1]
        if nz > LANES:
            column = iota(total.shape, 1)
            total = jnp.where((column >= W) & (column < nz - W), total, 0.0)
        folded = total[:, :LANES]
        for start in range(LANES, nz, LANES):
            folded = folded + total[:, start : start + LANES]
        return folded

    def first(self, halo):
        return W - halo * self.has_below

    def reach(self, halo):
        if self.pair:
            return halo
        return halo * (self.has_below + self.has_above)

    def run(self, halo, body, stage, before=0):
        count = self.nx + self.reach(halo) + before
        self.loop(self.first(halo) - before, count, body, stage)

    def narrow(self, v):
        ny = self.ny
        upper, lower = v[ny : ny + TILE], v[ny + TILE :]
        both = jnp.where(iota(upper.shape, 0) < TILE // 2, upper, lower)
        return jnp.concatenate([v[:ny], both], axis=0)

    def press_faces(self, l):
        own = self.perm[l]
        self.tx[l] = harmonic(own, self.nxt(self.perm, l))
        tall = self.perm_tall[l]
        face = harmonic(tall, self.yp(tall))
        self.ty[l] = self.narrow(face)
        self.face_sum[l] = self.narrow(face + self.ym(face))
        self.tz[l] = harmonic(own, self.zp(own))

    def y_sum(self, l):
        return self.face_sum[l]

    def near_faces(self, shape):
        row = iota(shape, 0)
        return (row < self.ny) | (row == shape[0] - 1)

    def assemble(self, l, x, fields, beside, table, keep=None):
        ny = self.ny
        gap = jnp.zeros((2 * TILE, fields.shape[3]), jnp.float32)
        refs = [self.zone_tall, self.press] + [self.motion.at[c] for c in range(3)]
        refs += [self.load, self.drain] + [self.body.at[c] for c in range(3)]
        for f, ref in enumerate(refs):
            width, rows = ROW_WIDTHS[f], ref.shape[1]
            below, above = beside(f)
            middle = fields[f, x]
            if keep is not None:
                below, above, middle = below * keep, above * keep, middle * keep
            ref[l, :ny, :] = middle
            ref[l, ny:, :] = gap[: rows - ny]
            ref[l, ny : ny + width, :] = above
            ref[l, rows - width :, :] = below
        tall_zone = self.zone_tall[l]
        perm = lookup(tall_zone, table, 0)
        self.perm_tall[l] = perm
        self.perm[l] = self.narrow(perm)
        zone = self.narrow(tall_zone)
        self.zone[l] = zone
        lame, shear = lookup(zone, table, 1), lookup(zone, table, 2)
        self.heft[l] = lame + shear
        self.shear[l] = shear
        self.fixed[l] = fixed_term(zone, lame, shear)


def new_brick(peers, nx, ny):
    domain = Brick(dict(nx=nx, ny=ny, pair=peers[0] == 2))
    at = lax.axis_index("gx")
    domain.has_below = (at > 0).astype(jnp.int32)
    domain.has_above = (at < peers[0] - 1).astype(jnp.int32)
    return domain


BRICK_SCRATCH = tuple(name for name, _ in ARRAYS if name not in KEPT)


def brick_kernel(peers, *refs):
    table, fields, below, above = refs[:4]
    rows = [Rows(*refs[i : i + 2], peers) for i in (4, 6, 8)]
    outs, acc, scratch = refs[10 : 10 + len(KEPT)], refs[10 + len(KEPT)], refs[11 + len(KEPT) :]
    _, nx, ny, nz = fields.shape
    domain = new_brick(peers, nx, ny)
    domain.__dict__.update(zip(KEPT, outs))
    domain.__dict__.update(zip(BRICK_SCRATCH, scratch))
    domain.zone_tall, domain.perm_tall, domain.face_sum = scratch[len(BRICK_SCRATCH) :]

    empty = jnp.zeros((ny + TILE, nz), jnp.float32)
    for l in (W - 1, W + nx):
        for name in ("perm", "heft", "shear", "press", "z0", "p0"):
            getattr(domain, name)[l] = empty
        for c in range(3):
            domain.motion[c, l] = empty
        for i in range(9):
            domain.zs[i, l] = empty
            domain.ps[i, l] = empty
        domain.perm_tall[l] = jnp.zeros((ny + 2 * TILE, nz), jnp.float32)

    for x in range(nx):
        domain.assemble(W + x, x, fields, lambda f, x=x: rows[0].read(f, x), table)
    if domain.pair:
        upper = lax.axis_index("gx") > 0
        for u in range(W):

            def beside(f, u=u):
                ending, starting = rows[1].read(f, nx - W + u), rows[1].read(f, u)
                return [jnp.where(upper, a, b) for a, b in zip(ending, starting)]

            l = jnp.where(upper, u, W + nx + u)
            x = jnp.where(upper, nx - W + u, u)
            domain.assemble(l, x, below, beside, table)
    else:
        keep_below, keep_above = keeps("gx", peers[0])
        for u in range(W):
            x = nx - W + u
            domain.assemble(u, x, below, lambda f, x=x: rows[1].read(f, x), table, keep_below)
            l = W + nx + u
            domain.assemble(l, u, above, lambda f, u=u: rows[2].read(f, u), table, keep_above)
    domain.stages()
    acc[...] = jnp.zeros(acc.shape, jnp.float32)
    domain.loop(W, nx, lambda l: domain.finish(l, acc, None), "finish")
    if nz == LANES:
        column = iota((TILE, LANES), 1)
        mask = (column >= W) & (column < nz - W)
        for i in range(SUMS):
            acc[i] = jnp.where(mask, acc[i], 0.0)


class Ends(Domain):
    def roll(self, v, shift):
        return pltpu.roll(v, shift % LANES, v.ndim - 1)

    def nxt(self, ref, l):
        moved = self.roll(ref[pl.ds(l.start, l.size + 1)], -self.row)
        lane = iota(moved[1:].shape, 2)
        return jnp.where(lane < LANES - self.row, moved[:-1], moved[1:])

    def before(self, v):
        moved = self.roll(v, self.row)
        back = jnp.concatenate([jnp.zeros_like(moved[:1]), moved[:-1]], axis=0)
        return jnp.where(iota(moved.shape, 2) >= self.row, moved, back)

    def prv(self, ref, l):
        return self.before(ref[l])

    def back_x(self, values, again):
        return [self.before(value) - value for value in values]

    def yp(self, v):
        return self.roll(v, -1)

    def ym(self, v):
        return self.roll(v, 1)

    def zp(self, v):
        return pltpu.roll(v, v.shape[1] - 1, 1)

    def zm(self, v):
        return pltpu.roll(v, 1, 1)

    def y_sum(self, l):
        face = self.ty[l]
        return face + self.ym(face)

    def near_faces(self, shape):
        row = iota(shape, len(shape) - 1) % self.row
        return (row >= TILE - 1) & (row < self.row - TILE)

    def own(self, v):
        return v

    def fold(self, value, mask):
        total = None
        for g in range(value.shape[0]):
            part = jnp.where(mask, value[g], 0.0)
            for start in range(0, value.shape[1], TILE):
                piece = part[start : start + TILE]
                total = piece if total is None else total + piece
        return total

    def run(self, halo, body, stage, before=0):
        body(pl.ds(0, self.groups))

    def assemble(self, peers, ends, messages, table):
        keep = keeps("gz", peers[2])
        for g in range(self.groups):
            for f in range(NF):
                self.raw[f, g] = ends[f, g]

        def halo(message, side, base, keep):
            for g in range(self.groups):
                for f in range(NF):
                    width, offset = WIDTHS[f], OFFSETS[f]
                    start = base + (SEG - W if side else W - width)
                    self.raw[f, g, start : start + width, :] = (
                        message[g, offset : offset + width, :] * keep
                    )

        if sides_of(peers) == 1:
            first = lax.axis_index("gx") == 0
            pl.when(first)(lambda: halo(messages[0], 0, 0, keep[0]))
            pl.when(jnp.logical_not(first))(lambda: halo(messages[0], 1, 0, keep[1]))
        else:
            halo(messages[0], 0, 0, keep[0])
            halo(messages[1], 1, SEG, keep[1])
        for g in range(self.groups):
            zone = self.raw[ZONE, g]
            lame, shear = lookup(zone, table, 1), lookup(zone, table, 2)
            self.perm[g] = lookup(zone, table, 0)
            self.heft[g] = lame + shear
            self.shear[g] = shear
            self.fixed[g] = fixed_term(zone, lame, shear)


class Either:
    def __init__(self, condition, yes, no):
        self.condition, self.refs = condition, (yes, no)

    def __getitem__(self, index):
        return jnp.where(self.condition, *[ref[index] for ref in self.refs])


def own_groups(count, peers):
    return count * blocks_of(peers)[0][0]


def ends_kernel(peers, tall, *refs):
    sides = sides_of(peers)
    table, ends, *messages = refs[: 2 + sides]
    added, out, partial, raw, acc, *scratch = refs[2 + sides :]
    names = [name for name, _ in ARRAYS[6:] if name not in KEPT]
    domain = Ends(dict(zip(names, scratch)))
    domain.raw = raw
    kept = {n: out.at[ENDS_START[n] : ENDS_START[n] + k] for n, k in ENDS_KEPT}
    domain.z0, domain.p0 = out.at[ENDS_START["z0"]], out.at[ENDS_START["p0"]]
    domain.zs, domain.ps = kept["zs"], kept["ps"]
    domain.zone, domain.press = raw.at[ZONE], raw.at[PRESS]
    domain.motion = raw.at[MOTION : MOTION + 3]
    domain.load, domain.drain = raw.at[SOURCE], raw.at[DRAIN]
    domain.body = raw.at[BODY : BODY + 3]
    domain.row = tall
    domain.groups = groups = raw.shape[1] - 1
    columns = raw.shape[2]
    empty = jnp.zeros((columns, LANES), jnp.float32)
    for ref in (raw, out):
        for i in range(ref.shape[0]):
            ref[i, groups] = empty
    for ref in (domain.perm, domain.shear):
        ref[groups] = empty
    domain.assemble(peers, ends, messages, table)
    domain.stages()
    for g in range(groups):
        for i in range(4):
            out[i, g] = raw[PRESS + i, g]
    acc[...] = added[...]
    shape = (columns, LANES)
    column, row = iota(shape, 0), iota(shape, 1) % tall
    if sides == 1:
        start = jnp.where(lax.axis_index("gx") == 0, W, SEG - 2 * W)
        at_end = (column >= start) & (column < start + W)
        mine = pl.ds(0, groups)
    else:
        inner = column % SEG
        start = jnp.where(column < SEG, W, SEG - 2 * W)
        at_end = (inner >= start) & (inner < start + W)
        count = groups // len(blocks_of(peers))
        mine = pl.ds(own_groups(count, peers), count)
    mask = at_end & (row >= TILE) & (row < tall - TILE)
    domain.finish(mine, acc, mask)

    sums = jnp.concatenate(
        [jnp.sum(acc[i], axis=0, keepdims=True) for i in range(acc.shape[0])], axis=0
    )
    totals = jnp.sum(sums, axis=1, keepdims=True)
    spread = jnp.where(iota(sums.shape, 0) == iota(sums.shape, 1), totals, 0.0)
    line = jnp.sum(spread, axis=0, keepdims=True)
    partial[...] = jnp.broadcast_to(line, partial.shape)


def step_sizes(gamma, delta, cross, energy):
    first = gamma / delta
    gamma_new = gamma - 2.0 * first * delta + first * first * cross
    curved = delta - 2.0 * first * cross + first * first * energy
    ratio = gamma_new / gamma
    second = gamma_new / (curved - ratio * gamma_new / first)
    return first + second * (1.0 + ratio), -first * second


def combine(peers, tall, *refs):
    pair = sides_of(peers) == 1
    sums, (old, z0, p0, zs) = refs[0], refs[1:5]
    ps, fields, own_ends, other_ends = refs[5:-6] if pair else refs[5:-6] + refs[-7:-6]
    pressure, motion, strain, moved, ends_moved, turned = refs[-6:]
    if pair:
        first = lax.axis_index("gx") == 0
        halves = (Either(first, own_ends, other_ends), Either(first, other_ends, own_ends))

    def end_of(side, i, g):
        if pair:
            return halves[side][i, g]
        return own_ends[i, g, side * SEG : (side + 1) * SEG, :]

    line = jnp.sum(sums[...], axis=0, keepdims=True)
    lane = iota(line.shape, 1)

    def value(index):
        return jnp.sum(jnp.where(lane == index, line, 0.0), axis=1, keepdims=True)

    c1, c2 = step_sizes(*[value(i) for i in range(4)])
    weights = (jnp.ones_like(c1), c1, c2)

    def form(start):
        total = 0.0
        for i, (j, k) in enumerate(PAIRS):
            scale = 1.0 if j == k else 2.0
            total = total + scale * weights[j] * weights[k] * value(start + i)
        return total

    d1, d2 = step_sizes(form(4), form(10), form(16), form(22))
    on_z = [d1 * w for w in weights]
    on_p = [d2 * w for w in weights]

    def new_motion(start, z_part, p_part, c):
        total = start
        for j in range(3):
            total = total + on_z[j] * z_part(3 * j + c)
            total = total + on_p[j] * p_part(3 * j + c)
        return total

    nx, ny, nz = pressure.shape
    pack = LANES // tall
    ends = Ends(dict(row=tall))
    groups = own_ends.shape[1] - 1
    count = groups // len(blocks_of(peers))
    mine = own_groups(count, peers)
    every = pl.ds(0, groups)
    if pair:
        every = pl.ds(lax.axis_index("gx") * (count - 1), count + 1)
    empty = jnp.zeros((SEG, LANES), jnp.float32)
    start = ENDS_START
    for side in range(2):
        for c in range(3):
            for i in range(every.size):
                g = every.start + i
                ends_moved[side, c, g] = new_motion(
                    end_of(side, start["motion"] + c, g),
                    lambda k, side=side, g=g: end_of(side, start["zs"] + k, g),
                    lambda k, side=side, g=g: end_of(side, start["ps"] + k, g),
                    c,
                )
            ends_moved[side, c, every.start + every.size] = empty
        along_y, along_z = ends_moved[side, 1, every], ends_moved[side, 2, every]
        along_x = ends_moved.at[side, 0]
        ends_moved[side, 3, every] = 0.5 * (
            (ends.nxt(along_x, every) - ends.prv(along_x, every))
            + (ends.yp(along_y) - ends.ym(along_y))
            + (ends.zp(along_z) - ends.zm(along_z))
        )
    for c in range(3):
        around = 1 if c == 0 else 0
        for l in range(W - around, W + nx + around):
            moved[c, l] = new_motion(
                old[c, l], lambda k, l=l: zs[k, l], lambda k, l=l: ps[k, l], c
            )
    brick = Brick({})
    outs = [pressure] + [motion.at[c] for c in range(3)] + [strain]
    for g in range(count):
        at = mine + g
        flipped = []
        for o in range(len(outs)):
            slot = g * len(outs) + o
            for side, (row, first_row) in enumerate(((0, W), (LANES - W, SEG - 2 * W))):
                if o == 0:
                    edge = end_of(side, start["press"], at)
                    edge = edge + c1 * end_of(side, start["z0"], at)
                    edge = edge + c2 * end_of(side, start["p0"], at)
                else:
                    edge = ends_moved[side, o - 1, at]
                turned[slot, row : row + W, :] = edge[first_row : first_row + W]
            flipped.append(turned[slot].T)
        for i in range(pack):
            x = g * pack + i
            l = W + x
            top = i * tall + TILE
            column = iota((ny, LANES), 1)
            u = [moved[c, l] for c in range(3)]
            change = (
                (moved[0, l + 1] - moved[0, l - 1])
                + (brick.yp(u[1]) - brick.ym(u[1]))
                + (brick.zp(u[2]) - brick.zm(u[2]))
            )
            results = [fields[PRESS, x] + c1 * z0[l, :ny, :] + c2 * p0[l, :ny, :]]
            results = results + [v[:ny] for v in u] + [0.5 * change[:ny]]
            for out, result, edge in zip(outs, results, flipped):
                edge = edge[top : top + ny]
                if nz == LANES:
                    inner = (column >= W) & (column < LANES - W)
                    out[x] = jnp.where(inner, result, edge)
                else:
                    out[x] = result
                    out[x, :, :LANES] = jnp.where(column >= W, result[:, :LANES], edge)
                    out[x, :, nz - LANES :] = jnp.where(
                        column < LANES - W, result[:, nz - LANES :], edge
                    )


def f32(*shape):
    return jax.ShapeDtypeStruct(shape, jnp.float32)


def vmem(*shape):
    return pltpu.VMEM(shape, jnp.float32)


def call(kernel, outs, *args, unread=0, space=pltpu.VMEM, scratch=(), limit=8, cost=None):
    specs = [
        pl.BlockSpec(memory_space=space if i < len(args) - unread else pl.ANY)
        for i in range(len(args))
    ]
    return pl.pallas_call(
        kernel,
        out_shape=outs,
        in_specs=specs,
        scratch_shapes=scratch,
        cost_estimate=cost,
        compiler_params=pltpu.CompilerParams(vmem_limit_bytes=limit * MIB),
    )(*args)


def ring(value, axis, step):
    peers = lax.axis_size(axis)
    return lax.ppermute(value, axis, [(i, (i + step) % peers) for i in range(peers)])


def pairs(value, axis, start):
    peers = lax.axis_size(axis)
    swaps = [(i, i) for i in range(start)]
    for i in range(start, peers - 1, 2):
        swaps += [(i, i + 1), (i + 1, i)]
    swaps += [(i, i) for i in range(len(swaps), peers)]
    return lax.ppermute(value, axis, swaps)


def x_neighbours(value):
    peers = lax.axis_size("gx")
    above = ring(value, "gx", -1)
    below = above if peers == 2 else ring(value, "gx", 1)
    return below, above


def shards(
    source,
    pressure_old,
    strain_prev,
    motion_old,
    body_force,
    zone_ids,
    drained,
    perm_table,
    lame_table,
    shear_table,
):
    nx, ny, nz = source.shape
    peers = [lax.axis_size(a) for a in AXES]
    total = peers[0] * peers[1] * peers[2]
    pair = peers[0] == 2
    tall = ny + 2 * TILE
    groups = nx * tall // LANES

    def with_peers(kernel, *more):
        return lambda *refs: kernel(peers, *more, *refs)

    raw = (
        source,
        pressure_old,
        strain_prev,
        motion_old,
        body_force,
        zone_ids,
        drained,
    )
    raw = [pltpu.with_memory_space_constraint(a, pltpu.HBM) for a in raw]
    held = [pltpu.VMEM(a.shape, a.dtype) for a in raw]
    tables = [
        pltpu.with_memory_space_constraint(a, pltpu.HBM)
        for a in (perm_table, lame_table, shear_table)
    ]
    message = f32(up_to(nx * ROWS_EACH, TILE), nz)
    first, second, table = call(
        pack_rows,
        [message, message, f32(TILE, LANES)],
        *raw,
        *tables,
        space=pltpu.HBM,
        scratch=held
        + [pltpu.SMEM(a.shape, a.dtype) for a in tables]
        + [pltpu.SemaphoreType.DMA((len(raw) + len(tables),))],
    )
    (fields,) = call(
        pack_fields,
        [f32(NF, nx, ny, nz)],
        *raw,
        table,
        space=pltpu.HBM,
        unread=1,
        scratch=held + [pltpu.SemaphoreType.DMA((len(raw),))],
    )
    fields_below, fields_above = x_neighbours(fields)
    first = pairs(first, "gy", 0)
    second = pairs(second, "gy", 1)
    first_below, first_above = x_neighbours(first)
    second_below, second_above = x_neighbours(second)
    others = [
        (fields_below, first_below, second_below),
        (fields_above, first_above, second_above),
    ][: 1 if pair else 2]
    sides = 1 if pair else 2
    own_ends, *own_messages = call(
        with_peers(pack_own),
        [f32(NF, groups, sides * SEG, LANES)] + [f32(groups, MSG_ROWS, LANES)] * sides,
        fields,
        first,
        second,
        scratch=[vmem(NF * groups, LANES, nz)],
    )
    span = (1 + len(others)) * groups
    ends, *messages = call(
        with_peers(pack_others),
        [f32(NF, span, sides * SEG, LANES)] + [f32(span, MSG_ROWS, LANES)] * sides,
        own_ends,
        *own_messages,
        *[array for block in others for array in block],
        scratch=[vmem(NF * groups, LANES, nz)],
        limit=12,
    )
    if pair:
        n = peers[2]
        hops = [(i, (i + 1) % n) for i in range(n)]
        hops += [(n + i, n + (i - 1) % n) for i in range(n)]
        got = [lax.ppermute(messages[0], ("gx", "gz"), hops)]
    else:
        got = [ring(messages[0], "gz", 1), ring(messages[1], "gz", -1)]
    depth = nx + 2 * W
    cells = depth * ny * nz

    def shaped(lead, *shape):
        return (lead,) * (lead > 0) + shape

    leads = dict(ARRAYS)
    sums_shape = (up_to(SUMS, TILE), TILE, LANES)

    def layers_of(name):
        return shaped(leads[name], depth, ny + TILE, nz)

    *kept, added = call(
        with_peers(brick_kernel),
        [f32(*layers_of(name)) for name in KEPT] + [f32(*sums_shape)],
        table,
        fields,
        fields_below,
        fields_above,
        first,
        second,
        first_below,
        second_below,
        first_above,
        second_above,
        scratch=[vmem(*layers_of(name)) for name in BRICK_SCRATCH]
        + [vmem(depth, tall, nz), vmem(depth, tall, nz), vmem(depth, ny + TILE, nz)],
        limit=20,
    )
    span, columns = span + 1, sides * SEG
    ends_kept, partial = call(
        with_peers(ends_kernel, tall),
        [f32(ENDS_ARRAYS, span, columns, LANES), f32(total, LANES)],
        table,
        ends,
        *got,
        added,
        scratch=[vmem(NF, span, columns, LANES), vmem(*sums_shape)]
        + [
            vmem(*shaped(lead, span, columns, LANES))
            for name, lead in ARRAYS[6:]
            if name not in KEPT
        ],
        limit=16,
    )
    both = [ends_kept]
    if pair:
        both.append(ring(ends_kept, "gx", -1))
    sums = lax.all_to_all(partial, AXES, 0, 0, tiled=True)
    return tuple(
        call(
            with_peers(combine, tall),
            [f32(nx, ny, nz), f32(3, nx, ny, nz), f32(nx, ny, nz)],
            sums,
            *kept,
            fields,
            *both,
            scratch=[
                vmem(3, depth, ny + TILE, nz),
                vmem(2, 4, span, SEG, LANES),
                vmem(5 * groups, LANES, LANES),
            ],
            limit=16,
        )
    )


def solution(mesh):
    placed = (
        P("gx", "gy", "gz"),
        P("gx", "gy", "gz"),
        P("gx", "gy", "gz"),
        P(None, "gx", "gy", "gz"),
        P(None, "gx", "gy", "gz"),
        P("gx", "gy", "gz"),
        P("gx", "gy", "gz"),
        P(),
        P(),
        P(),
    )
    return jax.shard_map(
        shards,
        mesh=mesh,
        in_specs=placed,
        out_specs=(P("gx", "gy", "gz"), P(None, "gx", "gy", "gz"), P("gx", "gy", "gz")),
        check_vma=False,
    )
```
